32 devices in a mesh: dp: 8 (over z, x), tensor: 4 (over y, core).
Axes of the slice: x: 2, y: 2, z: 4, core: 2. Of those that a mesh axis runs over, the one named last changes fastest.
Arguments:
- history: bfloat16 [9, 4096, 2048], P(None, 'dp'), may hold values from -6 to 6
- mix_weights: float32 [36, 4096], P(None, 'dp'), may hold values from -2.4 to 2.4
- segments: int32 [4096], P('dp'), may hold values from 0 to 1, as said below
- norm_gains: float32 [5, 2048], replicated, may hold values from 0.5 to 1.5
- w_query: bfloat16 [2048, 2048], P('dp', 'tensor'), may hold values from -0.125 to 0.125
- w_key: bfloat16 [2048, 2048], P('dp', 'tensor'), may hold values from -0.125 to 0.125
- w_value: bfloat16 [2048, 2048], P('dp', 'tensor'), may hold values from -0.125 to 0.125
- w_out: bfloat16 [2048, 2048], P('tensor', 'dp'), may hold values from -0.5 to 0.5
- w_up: bfloat16 [2048, 8192], P('dp', 'tensor'), may hold values from -0.125 to 0.125
- w_down: bfloat16 [8192, 2048], P('tensor', 'dp'), may hold values from -0.0625 to 0.0625
- gen_in: bfloat16 [2048, 40], replicated, may hold values from -0.125 to 0.125
- gen_out: bfloat16 [40, 40], replicated, may hold values from -1 to 1
- out_grad: bfloat16 [4096, 2048], P('dp'), may hold values from -6 to 6
- next_grad: float32 [40, 4096], P(None, 'dp'), may hold values from -6 to 6
Outputs:
- layer_out: bfloat16 [4096, 2048], P('dp')
- next_mix: float32 [40, 4096], P(None, 'dp')
- history_grad: bfloat16 [9, 4096, 2048], P(None, 'dp')
- mix_grad: float32 [36, 4096], P(None, 'dp')
- grad_gains: float32 [5, 2048], replicated
- grad_query: float32 [2048, 2048], P('dp', 'tensor')
- grad_key: float32 [2048, 2048], P('dp', 'tensor')
- grad_value: float32 [2048, 2048], P('dp', 'tensor')
- grad_out: float32 [2048, 2048], P('tensor', 'dp')
- grad_up: float32 [2048, 8192], P('dp', 'tensor')
- grad_down: float32 [8192, 2048], P('tensor', 'dp')
- grad_gen_in: float32 [2048, 40], replicated
- grad_gen_out: float32 [40, 40], replicated
The draws below stay inside these ranges and needn't reach their ends.
Inputs may be any that keep to these rules, and one draw needn't show every extreme that they name: `segments`: each block of 512 tokens of one dp index holds either one sequence (all 0) or two of 256 tokens (0 then 1); both kinds occur in every draw.
All inputs are finite; a program needn't handle non-finite values.
Results may differ from the reference program's by a relative error of at most 0.018.
Values may be sent and summed in bfloat16 or wider, within the bound.
A program may use at most 320 MiB of HBM per device.

```python
import jax
import jax.numpy as jnp
from jax import lax

D = 2048
HEADS = 16
HEAD_DIM = 128
FF = 8192
ROT = 32
GEN = 40
HIST = 9
MIXES = 36
NEXT = 40
TOK_DEV = 512
TOKENS = 4096


def draw_segments(key, part):
    blocks = TOKENS // TOK_DEV
    kinds = jax.random.randint(key, (blocks,), 0, 2, dtype=jnp.int32)
    kinds = kinds.at[0].set(1).at[1].set(0)
    positions = jnp.arange(TOKENS, dtype=jnp.int32)
    owner = positions // TOK_DEV
    inside = positions % TOK_DEV
    return (kinds[owner] * (inside >= TOK_DEV // 2).astype(jnp.int32)).astype(jnp.int32)


def with_spikes(entries, own_key, source, target, shards_of, factor):
    def block_of(axis_at):
        return (jnp.arange(entries.shape[axis_at]) // (entries.shape[axis_at] // shards_of)).reshape((-1,) + (1,) * (entries.ndim - 1 - axis_at))

    one_side = jax.random.permutation(own_key, shards_of)[block_of(target)]
    other_side = (block_of(target) + shards_of // 2) % shards_of
    return jnp.where((block_of(source) == one_side) | (block_of(source) == other_side), factor * entries, entries)


def level_of(own_key, dims, split, smallest, high):
    loudness = 1.0
    for position, parts in split:
        steps = jax.random.uniform(jax.random.fold_in(jax.random.fold_in(own_key, 6), position), (parts,), jnp.float32, smallest / len(split), high / len(split))
        loudness = loudness * jnp.repeat(jnp.exp(steps), dims[position] // parts).reshape((-1,) + (1,) * (len(dims) - 1 - position))
    return loudness


def noise(stream_key, extent, scale, limit, pieces=(), held_as=jnp.bfloat16):
    drawn = scale * jax.random.normal(stream_key, extent, jnp.float32)
    if pieces:
        drawn = drawn * level_of(stream_key, extent, pieces, -0.22, 0.18)
    return jnp.clip(drawn, -limit, limit).astype(held_as)


def gaussian_with(stream_key, shape, scale, most, split, heavy, kind=jnp.bfloat16):
    result = scale * jax.random.normal(stream_key, shape, jnp.float32)
    if split:
        result = result * level_of(stream_key, shape, split, -0.22, 0.18)
    return jnp.clip(with_spikes(result, jax.random.fold_in(stream_key, 3), *heavy), -most, most).astype(kind)


def setup_inputs(seed: int = 0) -> dict:
    key_list = jax.random.split(jax.random.key(seed), 15)
    history = noise(key_list[0], (HIST, TOKENS, D), 1.0, 6.0, ((1, 8),))
    mix_weights = noise(key_list[1], (MIXES, TOKENS), 0.4, 2.4, ((1, 8),), jnp.float32)
    segments = draw_segments(jax.random.fold_in(key_list[14], 71), 0)
    norm_gains = jnp.clip(1.0 + 0.1 * jax.random.normal(key_list[3], (5, D), jnp.float32), 0.5, 1.5)
    w_query = noise(key_list[4], (D, D), D ** -0.5, 0.125, ((0, 8), (1, 4)))
    w_key = noise(key_list[5], (D, D), D ** -0.5, 0.125, ((0, 8), (1, 4)))
    w_value = noise(key_list[6], (D, D), D ** -0.5, 0.125, ((0, 8), (1, 4)))
    w_out = noise(key_list[7], (D, D), (D // 16) ** -0.5, 0.5, ((0, 4), (1, 8)))
    w_up = noise(key_list[8], (D, FF), D ** -0.5, 0.125, ((0, 8), (1, 4)))
    w_down = noise(key_list[9], (FF, D), FF ** -0.5, 0.0625, ((0, 4), (1, 8)))
    gen_in = noise(key_list[10], (D, GEN), D ** -0.5, 0.125)
    gen_out = noise(key_list[11], (GEN, NEXT), GEN ** -0.5, 1.0)
    out_grad = gaussian_with(key_list[12], (TOKENS, D), 1.0, 6.0, ((0, 8),), (0, 1, 8, 2.0))
    next_grad = noise(key_list[13], (NEXT, TOKENS), 1.0, 6.0, ((1, 8),), jnp.float32)
    return dict(history=history, mix_weights=mix_weights, segments=segments, norm_gains=norm_gains, w_query=w_query, w_key=w_key, w_value=w_value, w_out=w_out, w_up=w_up, w_down=w_down, gen_in=gen_in, gen_out=gen_out, out_grad=out_grad, next_grad=next_grad)


EPSILON = 1e-05
ROPE_BASE = 10000.0
PRECISE = lax.Precision.HIGHEST

@jax.custom_vjp
def low(v):
    return lax.optimization_barrier(v.astype(jnp.bfloat16)).astype(jnp.float32)

@jax.custom_vjp
def low_back(v):
    return v

def low_keep(v):
    return (low(v), None)

def low_pass(kept, grad):
    return (grad,)

def back_keep(v):
    return (v, None)

def back_low(kept, grad):
    return (low(grad),)
low.defvjp(low_keep, low_pass)
low_back.defvjp(back_keep, back_low)

def layer_norm(values, gain_row):
    center = values - lax.optimization_barrier(jnp.mean(values, axis=-1, keepdims=True))
    spread = lax.optimization_barrier(jnp.mean(center * center, axis=-1, keepdims=True))
    return center * lax.rsqrt(spread + EPSILON) * gain_row

def rotary_tables(segments):
    tok_count = segments.shape[0]
    order_idx = jnp.arange(tok_count, dtype=jnp.int32)
    same_doc = segments[:, None] == segments[None, :]
    earlier = order_idx[None, :] < order_idx[:, None]
    places = lax.optimization_barrier(jnp.sum((same_doc & earlier).astype(jnp.int32), axis=1))
    halves = jnp.arange(ROT // 2, dtype=jnp.float32)
    frequency = ROPE_BASE ** (-2.0 * halves / ROT)
    angles = places.astype(jnp.float32)[:, None] * frequency[None, :]
    allowed = same_doc & (order_idx[None, :] <= order_idx[:, None])
    return (jnp.cos(angles)[:, None, :], jnp.sin(angles)[:, None, :], allowed)

def rotate(values, cosine, sine_tab):
    first_half = values[..., :ROT // 2]
    second = values[..., ROT // 2:ROT]
    return jnp.concatenate([first_half * cosine - second * sine_tab, second * cosine + first_half * sine_tab, values[..., ROT:]], axis=-1)

def forward(history, mix_weights, norm_gains, w_query, w_key, w_value, w_out, w_up, w_down, gen_in, gen_out, cosine, sine_tab, allowed):
    tok_count = history.shape[1]
    mix_view = mix_weights.reshape(4, HIST, tok_count)
    streams = jnp.einsum('sjt,jtd->std', mix_view, history, precision=PRECISE)
    normed = [low(layer_norm(streams[stream], norm_gains[stream])) for stream in range(4)]

    def heads_of(values):
        return values.reshape(tok_count, HEADS, HEAD_DIM)
    query_heads = low(rotate(heads_of(low_back(jnp.dot(normed[0], w_query, precision=PRECISE))), cosine, sine_tab))
    key_heads = low(rotate(heads_of(low_back(jnp.dot(normed[1], w_key, precision=PRECISE))), cosine, sine_tab))
    value_heads = low(low_back(heads_of(jnp.dot(normed[2], w_value, precision=PRECISE))))
    score_scale = HEAD_DIM ** (-0.5)
    raw_scores = low_back(jnp.einsum('thd,uhd->htu', query_heads, key_heads, precision=PRECISE) * score_scale)
    masked = jnp.where(allowed[None], raw_scores, -1e+30)
    row_max = lax.optimization_barrier(jnp.max(masked, axis=-1, keepdims=True))
    exp_scores = jnp.exp(masked - row_max)
    probs_low = low(exp_scores / lax.optimization_barrier(jnp.sum(exp_scores, axis=-1, keepdims=True)))
    attended = low(low_back(jnp.einsum('htu,uhd->thd', probs_low, value_heads, precision=PRECISE)))
    attention = jnp.dot(attended.reshape(tok_count, HEADS * HEAD_DIM), w_out, precision=PRECISE)
    hidden = low_back(jnp.dot(normed[3], w_up, precision=PRECISE))
    active = low(jax.nn.gelu(hidden, approximate=False))
    branch = low_back(attention + jnp.dot(active, w_down, precision=PRECISE))
    out_full = streams[3] + branch
    gen_normed = low(layer_norm(out_full, norm_gains[4]))
    gen_hidden = low_back(jnp.dot(gen_normed, gen_in, precision=PRECISE))
    gen_active = low(jax.nn.gelu(gen_hidden, approximate=False))
    next_mix = low_back(jnp.dot(gen_active, gen_out, precision=PRECISE))
    return (out_full, next_mix.T)

def reference(history, mix_weights, segments, norm_gains, w_query, w_key, w_value, w_out, w_up, w_down, gen_in, gen_out, out_grad, next_grad):
    blocks = TOKENS // TOK_DEV
    params = (norm_gains,) + tuple((matrix.astype(jnp.float32) for matrix in (w_query, w_key, w_value, w_out, w_up, w_down, gen_in, gen_out)))

    def block_step(totals, block_idx):
        row_start = block_idx * TOK_DEV
        hist_block = lax.dynamic_slice_in_dim(history, row_start, TOK_DEV, 1).astype(jnp.float32)
        mix_block = lax.dynamic_slice_in_dim(mix_weights, row_start, TOK_DEV, 1)
        seg_block = lax.dynamic_slice_in_dim(segments, row_start, TOK_DEV, 0)
        cosine, sine_tab, allowed = rotary_tables(seg_block)

        def local_fn(hist_in, mix_in, *param_list):
            return forward(hist_in, mix_in, *param_list, cosine, sine_tab, allowed)
        primal, pullback = jax.vjp(local_fn, hist_block, mix_block, *params)
        cot_out = lax.dynamic_slice_in_dim(out_grad, row_start, TOK_DEV, 0).astype(jnp.float32)
        cot_next = lax.dynamic_slice_in_dim(next_grad, row_start, TOK_DEV, 1)
        grad_list = pullback((cot_out, cot_next))
        totals = tuple((running + extra for running, extra in zip(totals, grad_list[2:])))
        return (totals, (primal[0].astype(jnp.bfloat16), primal[1], grad_list[0].astype(jnp.bfloat16), grad_list[1]))
    zeros_init = tuple((jnp.zeros_like(param) for param in params))
    totals, stacked = lax.scan(block_step, zeros_init, jnp.arange(blocks, dtype=jnp.int32))
    out_blocks, next_blocks, hist_blocks, mix_blocks = stacked
    layer_out = out_blocks.reshape(TOKENS, D)
    next_mix = next_blocks.transpose(1, 0, 2).reshape(NEXT, TOKENS)
    history_grad = hist_blocks.transpose(1, 0, 2, 3).reshape(HIST, TOKENS, D)
    mix_grad = mix_blocks.transpose(1, 0, 2).reshape(MIXES, TOKENS)
    return (layer_out, next_mix, history_grad, mix_grad, totals[0], totals[1], totals[2], totals[3], totals[4], totals[5], totals[6], totals[7], totals[8])
```

```python
import jax
import jax.numpy as jnp
from jax import lax
from jax.experimental import pallas as pl
from jax.experimental.pallas import tpu as pltpu
from jax.sharding import PartitionSpec as P

HEAD_DIM = 128
ROT = 32


EPSILON = 1e-05
ROPE_BASE = 10000.0

F32 = jnp.float32
BF16 = jnp.bfloat16


def layer_norm(values, gain_row):
    center = values - jnp.mean(values, axis=-1, keepdims=True)
    spread = jnp.mean(center * center, axis=-1, keepdims=True)
    return center * lax.rsqrt(spread + EPSILON) * gain_row


def rotary_tables(segments):
    tok_count = segments.shape[0]
    order_idx = jnp.arange(tok_count, dtype=jnp.int32)
    same_doc = segments[:, None] == segments[None, :]
    earlier = order_idx[None, :] < order_idx[:, None]
    places = jnp.sum((same_doc & earlier).astype(jnp.int32), axis=1)
    halves = jnp.arange(ROT // 2, dtype=jnp.float32)
    frequency = ROPE_BASE ** (-2.0 * halves / ROT)
    angles = places.astype(jnp.float32)[:, None] * frequency[None, :]
    allowed = same_doc & (order_idx[None, :] <= order_idx[:, None])
    return (jnp.cos(angles)[:, None, :], jnp.sin(angles)[:, None, :], allowed)


def rotate(values, cosine, sine_tab):
    first_half = values[..., : ROT // 2]
    second = values[..., ROT // 2 : ROT]
    return jnp.concatenate(
        [
            first_half * cosine - second * sine_tab,
            second * cosine + first_half * sine_tab,
            values[..., ROT:],
        ],
        axis=-1,
    )


def gelu_exact(values):
    return jax.nn.gelu(values, approximate=False)


def matmul(left_op, right_op):
    return jnp.dot(left_op, right_op, preferred_element_type=jnp.float32)


MIB = 1 << 20
GROUP = 16
CHUNK = 512


def mix_norm_kernel(history, mix, gains, streams, normed, stats):
    states, tokens, width = history.shape
    inverse = 1.0 / width

    @pl.loop(0, tokens // GROUP)
    def _(step):
        rows = pl.ds(pl.multiple_of(step * GROUP, GROUP), GROUP)
        weights = mix[rows, :]
        sums = [jnp.zeros((GROUP, 128), F32) for _ in range(4)]
        for at in range(0, width, CHUNK):
            cols = pl.ds(at, CHUNK)
            total = [None] * 4
            for source in range(states):
                state = history[source, rows, cols].astype(F32)
                for stream in range(4):
                    k = stream * states + source
                    term = weights[:, k : k + 1] * state
                    total[stream] = term if source == 0 else total[stream] + term
            for stream in range(4):
                streams[stream, rows, cols] = total[stream]
                for lane in range(0, CHUNK, 128):
                    sums[stream] = sums[stream] + total[stream][:, lane : lane + 128]
        for stream in range(4):
            mean = jnp.sum(sums[stream], axis=1, keepdims=True) * inverse
            square = jnp.zeros((GROUP, 128), F32)
            for at in range(0, width, CHUNK):
                center = streams[stream, rows, pl.ds(at, CHUNK)] - mean
                center = center * center
                for lane in range(0, CHUNK, 128):
                    square = square + center[:, lane : lane + 128]
            scale = lax.rsqrt(jnp.sum(square, axis=1, keepdims=True) * inverse + EPSILON)
            stats[rows, stream : stream + 1] = mean
            stats[rows, 4 + stream : 5 + stream] = scale
            for at in range(0, width, CHUNK):
                cols = pl.ds(at, CHUNK)
                center = streams[stream, rows, cols] - mean
                gain = gains[stream : stream + 1, cols]
                normed[stream, rows, cols] = (center * scale * gain).astype(BF16)


def mix_norm(history, mix, gains, block=64):
    states, tokens, width = history.shape
    return pl.pallas_call(
        mix_norm_kernel,
        grid=(tokens // block,),
        in_specs=[
            pl.BlockSpec((states, block, width), lambda i: (0, i, 0)),
            pl.BlockSpec((block, mix.shape[1]), lambda i: (i, 0)),
            pl.BlockSpec(gains.shape, lambda i: (0, 0)),
        ],
        out_specs=[
            pl.BlockSpec((4, block, width), lambda i: (0, i, 0)),
            pl.BlockSpec((4, block, width), lambda i: (0, i, 0)),
            pl.BlockSpec((block, 8), lambda i: (i, 0)),
        ],
        out_shape=[
            jax.ShapeDtypeStruct((4, tokens, width), F32),
            jax.ShapeDtypeStruct((4, tokens, width), BF16),
            jax.ShapeDtypeStruct((tokens, 8), F32),
        ],
        cost_estimate=pl.CostEstimate(
            flops=tokens * width * 100, bytes_accessed=tokens * width * 42, transcendentals=0
        ),
        compiler_params=pltpu.CompilerParams(vmem_limit_bytes=40 * MIB),
        name="mix_norm",
    )(history, mix, gains)


def mix_back_kernel(history, mix, gains, streams, stats, grads, out_total, history_grad, mix_grad, gain_grad, held):
    states, tokens, width = history.shape
    inverse = 1.0 / width

    @pl.when(pl.program_id(0) == 0)
    def _():
        gain_grad[...] = jnp.zeros_like(gain_grad)

    @pl.loop(0, tokens // GROUP)
    def _(step):
        rows = pl.ds(pl.multiple_of(step * GROUP, GROUP), GROUP)
        weights = mix[rows, :]
        for stream in range(4):
            mean = stats[rows, stream : stream + 1]
            scale = stats[rows, 4 + stream : 5 + stream]
            sum_e = jnp.zeros((GROUP, 128), F32)
            sum_ex = jnp.zeros((GROUP, 128), F32)
            for at in range(0, width, CHUNK):
                cols = pl.ds(at, CHUNK)
                unit = (streams[stream, rows, cols] - mean) * scale
                upstream = grads[stream, rows, cols].astype(F32)
                e = upstream * gains[stream : stream + 1, cols]
                gain = upstream * unit
                gain_grad[stream, :, cols] += gain[:8] + gain[8:]
                ex = e * unit
                for lane in range(0, CHUNK, 128):
                    sum_e = sum_e + e[:, lane : lane + 128]
                    sum_ex = sum_ex + ex[:, lane : lane + 128]
            mean_e = jnp.sum(sum_e, axis=1, keepdims=True) * inverse
            mean_ex = jnp.sum(sum_ex, axis=1, keepdims=True) * inverse
            for at in range(0, width, CHUNK):
                cols = pl.ds(at, CHUNK)
                unit = (streams[stream, rows, cols] - mean) * scale
                e = grads[stream, rows, cols].astype(F32) * gains[stream : stream + 1, cols]
                grad = scale * (e - mean_e - unit * mean_ex)
                if stream == 3:
                    grad = grad + out_total[rows, cols]
                held[stream, :, cols] = grad
        for source in range(states):
            sums = [jnp.zeros((GROUP, 128), F32) for _ in range(4)]
            for at in range(0, width, CHUNK):
                cols = pl.ds(at, CHUNK)
                state = history[source, rows, cols].astype(F32)
                total = None
                for stream in range(4):
                    k = stream * states + source
                    grad = held[stream, :, cols]
                    term = weights[:, k : k + 1] * grad
                    total = term if total is None else total + term
                    product = state * grad
                    for lane in range(0, CHUNK, 128):
                        sums[stream] = sums[stream] + product[:, lane : lane + 128]
                history_grad[source, rows, cols] = total.astype(BF16)
            for stream in range(4):
                k = stream * states + source
                mix_grad[rows, k : k + 1] = jnp.sum(sums[stream], axis=1, keepdims=True)


def mix_back(history, mix, gains, streams, stats, grads, out_total, block=64):
    states, tokens, width = history.shape
    return pl.pallas_call(
        mix_back_kernel,
        grid=(tokens // block,),
        in_specs=[
            pl.BlockSpec((states, block, width), lambda i: (0, i, 0)),
            pl.BlockSpec((block, mix.shape[1]), lambda i: (i, 0)),
            pl.BlockSpec(gains.shape, lambda i: (0, 0)),
            pl.BlockSpec((4, block, width), lambda i: (0, i, 0)),
            pl.BlockSpec((block, 8), lambda i: (i, 0)),
            pl.BlockSpec((4, block, width), lambda i: (0, i, 0)),
            pl.BlockSpec((block, width), lambda i: (i, 0)),
        ],
        out_specs=[
            pl.BlockSpec((states, block, width), lambda i: (0, i, 0)),
            pl.BlockSpec((block, mix.shape[1]), lambda i: (i, 0)),
            pl.BlockSpec((4, 8, width), lambda i: (0, 0, 0)),
        ],
        out_shape=[
            jax.ShapeDtypeStruct((states, tokens, width), BF16),
            jax.ShapeDtypeStruct((tokens, mix.shape[1]), F32),
            jax.ShapeDtypeStruct((4, 8, width), F32),
        ],
        scratch_shapes=[pltpu.VMEM((4, GROUP, width), F32)],
        cost_estimate=pl.CostEstimate(
            flops=tokens * width * 200, bytes_accessed=tokens * width * 64, transcendentals=0
        ),
        compiler_params=pltpu.CompilerParams(vmem_limit_bytes=48 * MIB),
        name="mix_back",
    )(history, mix, gains, streams, stats, grads, out_total)


def gelu(x):
    return 0.5 * x * (1.0 + lax.erf(x * (0.5**0.5)))


def gelu_slope(x):
    return 0.5 * (1.0 + lax.erf(x * (0.5**0.5))) + x * jnp.exp(-0.5 * x * x) * 0.3989422804014327


def dot(a, b, dims):
    return lax.dot_general(a, b, (dims, ((), ())), preferred_element_type=F32)


def gen_kernel(stream, branch, gain, gen_in, gen_out, out_grad, next_grad, layer_out, next_mix, out_total, branch_grad, gain_grad, in_grad, mid_grad):
    first = pl.program_id(0) == 0
    x = stream[0] + branch[...].astype(F32)
    layer_out[...] = x.astype(BF16)
    center = x - jnp.mean(x, axis=1, keepdims=True)
    scale = lax.rsqrt(jnp.mean(center * center, axis=1, keepdims=True) + EPSILON)
    unit = center * scale
    gains = gain[4:5, :]
    low = (unit * gains).astype(BF16)
    hidden = dot(low, gen_in[...], ((1,), (0,)))
    active = gelu(hidden).astype(BF16)
    next_mix[...] = dot(active, gen_out[...], ((1,), (0,)))
    upstream = next_grad[...].astype(BF16)
    active_grad = dot(upstream, gen_out[...], ((1,), (1,)))
    hidden_grad = (active_grad * gelu_slope(hidden)).astype(BF16)
    y = dot(hidden_grad, gen_in[...], ((1,), (1,)))
    e = y * gains
    grad = scale * (
        e - jnp.mean(e, axis=1, keepdims=True) - unit * jnp.mean(e * unit, axis=1, keepdims=True)
    )
    total = out_grad[...].astype(F32) + grad
    out_total[...] = total
    branch_grad[...] = total.astype(BF16)
    gain_part = jnp.sum(y * unit, axis=0, keepdims=True)
    in_part = dot(hidden_grad, low, ((0,), (0,)))
    mid_part = dot(active, upstream, ((0,), (0,)))

    @pl.when(first)
    def _():
        gain_grad[...] = gain_part
        in_grad[...] = in_part
        mid_grad[...] = mid_part

    @pl.when(jnp.logical_not(first))
    def _():
        gain_grad[...] += gain_part
        in_grad[...] += in_part
        mid_grad[...] += mid_part


def gen_stage(streams, branch, gains, gen_in, gen_out, out_grad, next_grad, block=128):
    _, tokens, width = streams.shape
    units = gen_in.shape[1]
    nxt = gen_out.shape[1]
    row = lambda i: (i, 0)
    fixed = lambda i: (0, 0)
    return pl.pallas_call(
        gen_kernel,
        grid=(tokens // block,),
        in_specs=[
            pl.BlockSpec((1, block, width), lambda i: (3, i, 0)),
            pl.BlockSpec((block, width), row),
            pl.BlockSpec(gains.shape, fixed),
            pl.BlockSpec(gen_in.shape, fixed),
            pl.BlockSpec(gen_out.shape, fixed),
            pl.BlockSpec((block, width), row),
            pl.BlockSpec((block, nxt), row),
        ],
        out_specs=[
            pl.BlockSpec((block, width), row),
            pl.BlockSpec((block, nxt), row),
            pl.BlockSpec((block, width), row),
            pl.BlockSpec((block, width), row),
            pl.BlockSpec((1, width), fixed),
            pl.BlockSpec((units, width), fixed),
            pl.BlockSpec((units, nxt), fixed),
        ],
        out_shape=[
            jax.ShapeDtypeStruct((tokens, width), BF16),
            jax.ShapeDtypeStruct((tokens, nxt), F32),
            jax.ShapeDtypeStruct((tokens, width), F32),
            jax.ShapeDtypeStruct((tokens, width), BF16),
            jax.ShapeDtypeStruct((1, width), F32),
            jax.ShapeDtypeStruct((units, width), F32),
            jax.ShapeDtypeStruct((units, nxt), F32),
        ],
        cost_estimate=pl.CostEstimate(
            flops=tokens * width * 300, bytes_accessed=tokens * width * 16, transcendentals=0
        ),
        compiler_params=pltpu.CompilerParams(vmem_limit_bytes=48 * MIB),
        name="gen_stage",
    )(streams, branch, gains, gen_in, gen_out, out_grad, next_grad)


def after(value, *others):
    return lax.optimization_barrier((value,) + others)[0]


class Ring:
    def __init__(self, size):
        self.size = size
        self.half = size // 2
        order = [2 * p if p < self.half else 2 * (size - 1 - p) + 1 for p in range(size)]
        self.right = [(order[p], order[(p + 1) % size]) for p in range(size)]
        self.left = [(b, a) for a, b in self.right]
        me = lax.axis_index("dp")
        self.place = jnp.where(lax.rem(me, 2) == 0, me // 2, size - 1 - me // 2)
        self.me = me

    def owner(self, shift):
        at = lax.rem(self.place + shift + self.size, self.size)
        return jnp.where(at < self.half, 2 * at, 2 * (self.size - 1 - at) + 1)

    def to_right(self, value):
        return lax.ppermute(value, "dp", self.right)

    def to_left(self, value):
        return lax.ppermute(value, "dp", self.left)

    def gather(self, shard):
        found = [(self.me, shard)]
        from_left, from_right = shard, shard
        for step in range(1, self.half):
            from_left, from_right = self.to_right(from_left), self.to_left(from_right)
            found.append((self.owner(-step), from_left))
            found.append((self.owner(step), from_right))
        cut = shard.shape[0] // 2
        top = self.to_right(from_left[:cut])
        low = self.to_left(from_right[cut:])
        found.append((self.owner(self.half), jnp.concatenate([top, low], axis=0)))
        return found

    def scatter(self, term, start=None):
        far = term(self.owner(self.half))
        cut = far.shape[0] // 2
        far = far.astype(BF16)
        if start is not None:
            far = after(far, start)
        top = self.to_right(far[:cut])
        low = self.to_left(far[cut:])
        near_right = term(self.owner(self.half - 1))
        near_left = term(self.owner(-(self.half - 1)))
        going_right = jnp.concatenate([near_right[:cut] + top.astype(F32), near_right[cut:]], axis=0)
        going_left = jnp.concatenate([near_left[:cut], near_left[cut:] + low.astype(F32)], axis=0)
        for distance in range(self.half - 1, 1, -1):
            got_left = self.to_right(going_right.astype(BF16))
            got_right = self.to_left(going_left.astype(BF16))
            going_right = term(self.owner(distance - 1)) + got_left.astype(F32)
            going_left = term(self.owner(1 - distance)) + got_right.astype(F32)
        got_left = self.to_right(going_right.astype(BF16))
        got_right = self.to_left(going_left.astype(BF16))
        return term(self.me) + got_left.astype(F32) + got_right.astype(F32)


def total_over(value, axis, size):
    bit = 1
    while bit < size:
        other = lax.ppermute(value, axis, [(i, i ^ bit) for i in range(size)])
        value = value + other
        bit *= 2
    return value


def tensor_sum(value, size):
    rows = value.shape[0] // 2
    core = lax.rem(lax.axis_index("tensor"), 2)
    swap = [(i, i ^ 1) for i in range(size)]
    low = value.astype(BF16)
    mine = lax.dynamic_slice_in_dim(low, core * rows, rows, 0)
    other = lax.dynamic_slice_in_dim(low, (1 - core) * rows, rows, 0)
    part = (mine.astype(F32) + lax.ppermute(other, "tensor", swap).astype(F32)).astype(BF16)
    bit = 2
    while bit < size:
        got = lax.ppermute(part, "tensor", [(i, i ^ bit) for i in range(size)])
        part = (part.astype(F32) + got.astype(F32)).astype(BF16)
        bit *= 2
    twin = lax.ppermute(part, "tensor", swap)
    first = jnp.where(core == 0, part, twin)
    second = jnp.where(core == 0, twin, part)
    return jnp.concatenate([first, second], axis=0)


def body(
    sizes,
    history,
    mix_weights,
    segments,
    norm_gains,
    w_query,
    w_key,
    w_value,
    w_out,
    w_up,
    w_down,
    gen_in,
    gen_out,
    out_grad,
    next_grad,
):
    dp_size, tensor_size = sizes
    states = history.shape[0]
    tok_count = history.shape[1]
    width = history.shape[2]
    local_cols = w_query.shape[1]
    local_hidden = w_up.shape[1]
    local_heads = local_cols // HEAD_DIM
    shard = w_query.shape[0]
    ring = Ring(dp_size)

    qkv_blocks = ring.gather(jnp.concatenate([w_query, w_key, w_value], axis=1))
    up_blocks = ring.gather(w_up)
    out_blocks = ring.gather(
        after(jnp.concatenate([w_out, w_down], axis=0), qkv_blocks[-2][1])
    )

    def by_rows(blocks):
        full = jnp.zeros((width, blocks[0][1].shape[1]), BF16)
        for owner, block in blocks:
            full = lax.dynamic_update_slice_in_dim(full, block, owner * shard, 0)
        return full

    def by_columns(blocks):
        full = jnp.zeros((blocks[0][1].shape[0], width), BF16)
        for owner, block in blocks:
            full = lax.dynamic_update_slice_in_dim(full, block, owner * shard, 1)
        return full

    mix_rows = mix_weights.T
    streams, normed, stats = mix_norm(history, mix_rows, norm_gains)
    cosine, sine_tab, allowed = rotary_tables(segments)

    full_qkv = by_rows(qkv_blocks)
    full_query = full_qkv[:, :local_cols]
    full_key = full_qkv[:, local_cols : 2 * local_cols]
    full_value = full_qkv[:, 2 * local_cols :]
    full_up = by_rows(up_blocks)

    def split_heads(values):
        return values.reshape(tok_count, local_heads, HEAD_DIM)

    query_heads = rotate(split_heads(matmul(normed[0], full_query)), cosine, sine_tab).astype(
        jnp.bfloat16
    )
    key_heads = rotate(split_heads(matmul(normed[1], full_key)), cosine, sine_tab).astype(
        jnp.bfloat16
    )
    value_heads = split_heads(matmul(normed[2], full_value)).astype(jnp.bfloat16)
    score_scale = HEAD_DIM ** (-0.5)
    raw_scores = (
        jnp.einsum("thd,uhd->htu", query_heads, key_heads, preferred_element_type=jnp.float32)
        * score_scale
    )
    masked = jnp.where(allowed[None], raw_scores, -1e30)
    row_max = jnp.max(masked, axis=-1, keepdims=True)
    exp_scores = jnp.exp(masked - row_max)
    attn_probs = exp_scores / jnp.sum(exp_scores, axis=-1, keepdims=True)
    probs_low = attn_probs.astype(jnp.bfloat16)
    attended = (
        jnp.einsum("htu,uhd->thd", probs_low, value_heads, preferred_element_type=jnp.float32)
        .astype(jnp.bfloat16)
        .reshape(tok_count, local_cols)
    )
    hidden = matmul(normed[3], full_up)
    active = gelu_exact(hidden).astype(jnp.bfloat16)
    both_low = jnp.concatenate([attended, active], axis=1)
    branch = jnp.zeros((tok_count, width), BF16)
    groups = [out_blocks[:1]] + [out_blocks[at : at + 2] for at in range(1, len(out_blocks), 2)]
    for group in groups:
        part = jnp.concatenate([matmul(both_low, block) for _, block in group], axis=1)
        summed = tensor_sum(part, tensor_size)
        for at, (owner, _) in enumerate(group):
            branch = lax.dynamic_update_slice_in_dim(
                branch, summed[:, at * shard : (at + 1) * shard], owner * shard, 1
            )
    layer_out, next_mix, out_total, branch_grad, gain_gen_grad, grad_gen_in, grad_gen_out = gen_stage(
        streams, branch, norm_gains, gen_in, gen_out, out_grad, next_grad.T
    )

    full_out_down = by_columns(out_blocks)

    def columns_of(array, owner):
        return lax.dynamic_slice_in_dim(array, owner * shard, shard, 1)

    grad_out_down = ring.scatter(lambda owner: matmul(both_low.T, columns_of(branch_grad, owner)))

    both_grad = matmul(branch_grad, full_out_down.T)
    active_grad = both_grad[:, local_cols:]
    gelu_mlp = jax.vjp(gelu_exact, hidden)[1]
    hidden_grad = gelu_mlp(active_grad)[0].astype(jnp.bfloat16)
    grad_up = ring.scatter(lambda owner: matmul(columns_of(normed[3], owner).T, hidden_grad))
    mlp_normed_grad = matmul(hidden_grad, full_up.T)
    attended_grad = (
        both_grad[:, :local_cols].astype(jnp.bfloat16).reshape(tok_count, local_heads, HEAD_DIM)
    )
    probs_grad = jnp.einsum(
        "thd,uhd->htu", attended_grad, value_heads, preferred_element_type=jnp.float32
    )
    values_grad = jnp.einsum(
        "htu,thd->uhd", probs_low, attended_grad, preferred_element_type=jnp.float32
    ).astype(jnp.bfloat16)
    row_dot = jnp.sum(attn_probs * probs_grad, axis=-1, keepdims=True)
    scores_grad = (attn_probs * (probs_grad - row_dot)).astype(jnp.bfloat16)
    query_grad = (
        jnp.einsum("htu,uhd->thd", scores_grad, key_heads, preferred_element_type=jnp.float32)
        * score_scale
    )
    key_grad = (
        jnp.einsum("htu,thd->uhd", scores_grad, query_heads, preferred_element_type=jnp.float32)
        * score_scale
    )
    query_low = (
        rotate(query_grad, cosine, -sine_tab).reshape(tok_count, local_cols).astype(jnp.bfloat16)
    )
    key_low = (
        rotate(key_grad, cosine, -sine_tab).reshape(tok_count, local_cols).astype(jnp.bfloat16)
    )
    value_low = values_grad.reshape(tok_count, local_cols)

    def qkv_term(owner):
        return jnp.concatenate(
            [
                matmul(columns_of(normed[0], owner).T, query_low),
                matmul(columns_of(normed[1], owner).T, key_low),
                matmul(columns_of(normed[2], owner).T, value_low),
            ],
            axis=1,
        )

    grad_qkv = ring.scatter(qkv_term, grad_out_down)
    summed_grads = (
        tensor_sum(matmul(query_low, full_query.T), tensor_size),
        tensor_sum(matmul(key_low, full_key.T), tensor_size),
        tensor_sum(matmul(value_low, full_value.T), tensor_size),
        tensor_sum(mlp_normed_grad, tensor_size),
    )
    history_grad, mix_grad, gain_grads = mix_back(
        history, mix_rows, norm_gains, streams, stats, jnp.stack(summed_grads), out_total
    )
    gain_rows = jnp.concatenate([jnp.sum(gain_grads, axis=1), gain_gen_grad], axis=0)
    out_rows = jnp.pad(grad_gen_out, ((0, 0), (0, width - gen_out.shape[1])))
    small = total_over(jnp.concatenate([gain_rows, grad_gen_in, out_rows], axis=0), "dp", dp_size)
    gains = gain_rows.shape[0]
    hidden_units = gen_in.shape[1]
    return (
        layer_out,
        next_mix.T,
        history_grad,
        mix_grad.T,
        small[:gains],
        grad_qkv[:, :local_cols],
        grad_qkv[:, local_cols : 2 * local_cols],
        grad_qkv[:, 2 * local_cols :],
        grad_out_down[:local_cols],
        grad_up,
        grad_out_down[local_cols:],
        small[gains : gains + hidden_units].T,
        small[gains + hidden_units :, : gen_out.shape[1]],
    )


def solution(mesh):
    sizes = (mesh.shape["dp"], mesh.shape["tensor"])
    in_specs = (
        P(None, "dp", None),
        P(None, "dp"),
        P("dp"),
        P(),
        P("dp", "tensor"),
        P("dp", "tensor"),
        P("dp", "tensor"),
        P("tensor", "dp"),
        P("dp", "tensor"),
        P("tensor", "dp"),
        P(),
        P(),
        P("dp", None),
        P(None, "dp"),
    )
    out_specs = (
        P("dp", None),
        P(None, "dp"),
        P(None, "dp", None),
        P(None, "dp"),
        P(),
        P("dp", "tensor"),
        P("dp", "tensor"),
        P("dp", "tensor"),
        P("tensor", "dp"),
        P("dp", "tensor"),
        P("tensor", "dp"),
        P(),
        P(),
    )

    def step(*arrays):
        return body(sizes, *arrays)

    return jax.shard_map(step, mesh=mesh, in_specs=in_specs, out_specs=out_specs, check_vma=False)
```

```python
import jax
import jax.numpy as jnp
from jax import lax
from jax.experimental import pallas as pl
from jax.experimental.pallas import tpu as pltpu
from jax.sharding import PartitionSpec as P

HEAD_DIM = 128
ROT = 32


EPSILON = 1e-05
ROPE_BASE = 10000.0

F32 = jnp.float32
BF16 = jnp.bfloat16


def rotary_tables(segments):
    tok_count = segments.shape[0]
    order_idx = jnp.arange(tok_count, dtype=jnp.int32)
    same_doc = segments[:, None] == segments[None, :]
    earlier = order_idx[None, :] < order_idx[:, None]
    places = jnp.sum((same_doc & earlier).astype(jnp.int32), axis=1)
    halves = jnp.arange(ROT // 2, dtype=jnp.float32)
    frequency = ROPE_BASE ** (-2.0 * halves / ROT)
    angles = places.astype(jnp.float32)[:, None] * frequency[None, :]
    return jnp.cos(angles), jnp.sin(angles)


MIB = 1 << 20
GROUP = 16
CHUNK = 512


def gelu(x):
    return 0.5 * x * (1.0 + lax.erf(x * (0.5**0.5)))


def gelu_slope(x):
    return 0.5 * (1.0 + lax.erf(x * (0.5**0.5))) + x * jnp.exp(-0.5 * x * x) * 0.3989422804014327


def dot(a, b, dims):
    return lax.dot_general(a, b, (dims, ((), ())), preferred_element_type=F32)


def gen_kernel(stream, branch, gain, gen_in, gen_out, out_grad, next_grad, layer_out, next_mix, out_total, branch_grad, gain_grad, in_grad, mid_grad):
    first = pl.program_id(0) == 0
    x = stream[0] + jnp.concatenate([branch[owner] for owner in range(branch.shape[0])], axis=1).astype(F32)
    layer_out[...] = x.astype(BF16)
    center = x - jnp.mean(x, axis=1, keepdims=True)
    scale = lax.rsqrt(jnp.mean(center * center, axis=1, keepdims=True) + EPSILON)
    unit = center * scale
    gains = gain[4:5, :]
    low = (unit * gains).astype(BF16)
    hidden = dot(low, gen_in[...], ((1,), (0,)))
    active = gelu(hidden).astype(BF16)
    next_mix[...] = dot(active, gen_out[...], ((1,), (0,)))
    upstream = next_grad[...].astype(BF16)
    active_grad = dot(upstream, gen_out[...], ((1,), (1,)))
    hidden_grad = (active_grad * gelu_slope(hidden)).astype(BF16)
    y = dot(hidden_grad, gen_in[...], ((1,), (1,)))
    e = y * gains
    grad = scale * (
        e - jnp.mean(e, axis=1, keepdims=True) - unit * jnp.mean(e * unit, axis=1, keepdims=True)
    )
    total = out_grad[...].astype(F32) + grad
    out_total[...] = total
    low_total = total.astype(BF16)
    shard = branch_grad.shape[2]
    for owner in range(branch_grad.shape[0]):
        branch_grad[owner] = low_total[:, owner * shard : (owner + 1) * shard]
    gain_part = jnp.sum(y * unit, axis=0, keepdims=True)
    in_part = dot(hidden_grad, low, ((0,), (0,)))
    mid_part = dot(active, upstream, ((0,), (0,)))

    @pl.when(first)
    def _():
        gain_grad[...] = gain_part
        in_grad[...] = in_part
        mid_grad[...] = mid_part

    @pl.when(jnp.logical_not(first))
    def _():
        gain_grad[...] += gain_part
        in_grad[...] += in_part
        mid_grad[...] += mid_part


def gen_stage(size, streams, branch, gains, gen_in, gen_out, out_grad, next_grad, block=128):
    _, tokens, width = streams.shape
    units = gen_in.shape[1]
    nxt = gen_out.shape[1]
    row = lambda i: (i, 0)
    fixed = lambda i: (0, 0)
    return pl.pallas_call(
        gen_kernel,
        grid=(tokens // block,),
        in_specs=[
            pl.BlockSpec((1, block, width), lambda i: (3, i, 0)),
            pl.BlockSpec((size, block, width // size), lambda i: (0, i, 0)),
            pl.BlockSpec(gains.shape, fixed),
            pl.BlockSpec(gen_in.shape, fixed),
            pl.BlockSpec(gen_out.shape, fixed),
            pl.BlockSpec((block, width), row),
            pl.BlockSpec((block, nxt), row),
        ],
        out_specs=[
            pl.BlockSpec((block, width), row),
            pl.BlockSpec((block, nxt), row),
            pl.BlockSpec((block, width), row),
            pl.BlockSpec((size, block, width // size), lambda i: (0, i, 0)),
            pl.BlockSpec((1, width), fixed),
            pl.BlockSpec((units, width), fixed),
            pl.BlockSpec((units, nxt), fixed),
        ],
        out_shape=[
            jax.ShapeDtypeStruct((tokens, width), BF16),
            jax.ShapeDtypeStruct((tokens, nxt), F32),
            jax.ShapeDtypeStruct((tokens, width), F32),
            jax.ShapeDtypeStruct((size, tokens, width // size), BF16),
            jax.ShapeDtypeStruct((1, width), F32),
            jax.ShapeDtypeStruct((units, width), F32),
            jax.ShapeDtypeStruct((units, nxt), F32),
        ],
        cost_estimate=pl.CostEstimate(
            flops=tokens * width * 300, bytes_accessed=tokens * width * 16, transcendentals=0
        ),
        compiler_params=pltpu.CompilerParams(vmem_limit_bytes=48 * MIB),
        name="gen_stage",
    )(streams, branch, gains, gen_in, gen_out, out_grad, next_grad)


MESH = pl.DeviceIdType.MESH


def place_of(me, size):
    odd = lax.rem(me, 2)
    at = lax.div(me, 2)
    return (1 - odd) * at + odd * (size - 1 - at)


def index_at(place, size):
    at = lax.rem(place + 2 * size, size)
    back = lax.div(at, size // 2)
    return (1 - back) * 2 * at + back * (2 * (size - 1 - at) + 1)


UNIT = 32


def back_kernel(
    size,
    normed,
    hidden_grad,
    qkv_low,
    stats,
    mix,
    gains,
    parts_in,
    history,
    streams,
    out_total,
    grad_up,
    grad_query,
    grad_key,
    grad_value,
    history_grad,
    mix_grad,
    gain_sum,
    gain_grad,
    gain_sent,
    gain_got,
    parts,
    from_core,
    from_link,
    far,
    ring,
    state_in,
    stream_in,
    total_in,
    state_out,
    held,
    ring_send,
    ring_recv,
    core_send,
    core_recv,
    link_send,
    link_recv,
    twin_send,
    twin_recv,
    load_sem,
    unit_sem,
    store_sem,
    gain_send,
    gain_recv,
    freed,
):
    half = size // 2
    shard = normed.shape[3]
    cut = shard // 2
    tokens, hidden_cols = hidden_grad.shape
    width = history.shape[2]
    inverse = 1.0 / width
    states = history.shape[0]
    me = lax.axis_index("dp")
    lane = lax.axis_index("tensor")
    place = place_of(me, size)
    right = index_at(place + 1, size)
    left = index_at(place - 1, size)
    core = lax.rem(lane, 2)
    chip = lax.div(lane, 2)
    twin = chip * 2 + 1 - core
    across = (1 - chip) * 2 + core

    barrier = pltpu.get_barrier_semaphore()
    steps = size.bit_length() - 1
    partners = [me + (1 << step) * (1 - 2 * lax.rem(lax.div(me, 1 << step), 2)) for step in range(steps)]
    for there in [(right, lane), (left, lane), (me, twin), (me, across)] + [(it, lane) for it in partners]:
        pl.semaphore_signal(barrier, inc=1, device_id=there, device_id_type=MESH)
    pl.semaphore_wait(barrier, 4 + steps)

    block = 64
    rows_half = tokens // 2
    blocks = rows_half // block
    load = pltpu.make_async_copy(parts_in, parts, load_sem)
    load.start()

    wide = 512 if half <= 4 else hidden_cols
    pieces = [(0, at, wide) for at in range(0, hidden_cols, wide)]
    local = qkv_low.shape[1] // 3
    pieces += [(1 + which, which * local, local) for which in range(3)]
    starts = []
    offset = 0
    for _, _, cols in pieces:
        starts.append(offset)
        offset += cols

    def term(distance, piece):
        owner = index_at(place + distance, size)
        which, at, cols = pieces[piece]
        if which == 0:
            return dot(normed[3, owner], hidden_grad[:, at : at + cols], ((0,), (0,)))
        return dot(normed[which - 1, owner], qkv_low[:, at : at + cols], ((0,), (0,)))

    def send(hop, way, piece):
        cols = pl.ds(starts[piece], pieces[piece][2])
        if hop == 0:
            rows = pl.ds(way * cut, cut)
            source = far.at[rows, cols]
            target = ring.at[0, way, rows, cols]
        else:
            source = ring.at[hop - 1, way, :, cols]
            target = ring.at[hop, way, :, cols]
        return pltpu.make_async_remote_copy(
            src_ref=source,
            dst_ref=target,
            send_sem=ring_send.at[hop, way, piece],
            recv_sem=ring_recv.at[hop, way, piece],
            device_id=((right, left)[way], lane),
            device_id_type=MESH,
        )

    for piece in range(len(pieces)):
        cols = pl.ds(starts[piece], pieces[piece][2])
        far[:, cols] = term(half, piece).astype(BF16)
        for way in range(2):
            send(0, way, piece).start()
        if piece == 0:
            load.wait()
            for at in range(blocks):
                rows = pl.ds(pl.multiple_of((1 - core) * rows_half + at * block, block), block)
                pltpu.make_async_remote_copy(
                    src_ref=parts.at[:, rows, :],
                    dst_ref=from_core.at[at],
                    send_sem=core_send.at[at],
                    recv_sem=core_recv.at[at],
                    device_id=(me, twin),
                    device_id_type=MESH,
                ).start()

    def mine(at):
        return pl.ds(pl.multiple_of(core * rows_half + at * block, block), block)

    def core_copy(at):
        rows = pl.ds(pl.multiple_of((1 - core) * rows_half + at * block, block), block)
        return pltpu.make_async_remote_copy(
            src_ref=parts.at[:, rows, :],
            dst_ref=from_core.at[at],
            send_sem=core_send.at[at],
            recv_sem=core_recv.at[at],
            device_id=(me, twin),
            device_id_type=MESH,
        )

    def link_copy(at):
        return pltpu.make_async_remote_copy(
            src_ref=parts.at[:, mine(at), :],
            dst_ref=from_link.at[at],
            send_sem=link_send.at[at],
            recv_sem=link_recv.at[at],
            device_id=(me, across),
            device_id_type=MESH,
        )

    def twin_copy(at):
        return pltpu.make_async_remote_copy(
            src_ref=parts.at[:, mine(at), :],
            dst_ref=parts.at[:, mine(at), :],
            send_sem=twin_send.at[at],
            recv_sem=twin_recv.at[at],
            device_id=(me, twin),
            device_id_type=MESH,
        )

    def add_into(at, other):
        base = core * rows_half + at * block

        @pl.loop(0, block // 16)
        def _(step):
            rows = pl.ds(pl.multiple_of(base + step * 16, 16), 16)
            theirs = pl.ds(pl.multiple_of(step * 16, 16), 16)
            for stream in range(4):
                total = parts[stream, rows, :].astype(F32) + other[at, stream, theirs, :].astype(F32)
                parts[stream, rows, :] = total.astype(BF16)

    def to_link(at):
        copy = core_copy(at)
        copy.wait_send()
        pl.semaphore_signal(freed.at[at], inc=1, device_id=(me, twin), device_id_type=MESH)
        copy.wait_recv()
        add_into(at, from_core)
        link_copy(at).start()

    def to_twin(at):
        copy = link_copy(at)
        copy.wait_send()
        copy.wait_recv()
        add_into(at, from_link)
        pl.semaphore_wait(freed.at[at], 1)
        twin_copy(at).start()

    def ready(at):
        copy = twin_copy(at)
        copy.wait_send()
        copy.wait_recv()

    per_block = 2 * block // UNIT
    units = tokens // UNIT

    def unit_base(unit):
        at, inner = divmod(unit, per_block)
        side, part = divmod(inner, per_block // 2)
        return side * rows_half + at * block + part * UNIT

    def unit_loads(unit):
        rows = pl.ds(unit_base(unit), UNIT)
        slot = unit % 2
        return (
            pltpu.make_async_copy(history.at[:, rows, :], state_in.at[slot], unit_sem.at[slot, 0]),
            pltpu.make_async_copy(streams.at[:, rows, :], stream_in.at[slot], unit_sem.at[slot, 1]),
            pltpu.make_async_copy(out_total.at[rows, :], total_in.at[slot], unit_sem.at[slot, 2]),
        )

    def unit_store(unit):
        rows = pl.ds(unit_base(unit), UNIT)
        slot = unit % 2
        return pltpu.make_async_copy(state_out.at[slot], history_grad.at[:, rows, :], store_sem.at[slot])

    gain_grad[...] = jnp.zeros_like(gain_grad)
    for copy in unit_loads(0):
        copy.start()

    def run_unit(unit):
        slot = unit % 2
        base = unit_base(unit)
        if unit + 1 < units:
            for copy in unit_loads(unit + 1):
                copy.start()
        for copy in unit_loads(unit):
            copy.wait()
        if unit >= 2:
            unit_store(unit - 2).wait()

        @pl.loop(0, UNIT // GROUP)
        def _(step):
            rows = pl.ds(pl.multiple_of(base + step * GROUP, GROUP), GROUP)
            inner = pl.ds(pl.multiple_of(step * GROUP, GROUP), GROUP)
            weights = mix[rows, :]
            for stream in range(4):
                mean = stats[rows, stream : stream + 1]
                scale = stats[rows, 4 + stream : 5 + stream]
                sum_e = jnp.zeros((GROUP, 128), F32)
                sum_ex = jnp.zeros((GROUP, 128), F32)
                for at in range(0, width, CHUNK):
                    cols = pl.ds(at, CHUNK)
                    unit_x = (stream_in[slot, stream, inner, cols] - mean) * scale
                    upstream = parts[stream, rows, cols].astype(F32)
                    e = upstream * gains[stream : stream + 1, cols]
                    gain = upstream * unit_x
                    gain_grad[stream, :, cols] += gain[:8] + gain[8:]
                    ex = e * unit_x
                    for lane_at in range(0, CHUNK, 128):
                        sum_e = sum_e + e[:, lane_at : lane_at + 128]
                        sum_ex = sum_ex + ex[:, lane_at : lane_at + 128]
                mean_e = jnp.sum(sum_e, axis=1, keepdims=True) * inverse
                mean_ex = jnp.sum(sum_ex, axis=1, keepdims=True) * inverse
                for at in range(0, width, CHUNK):
                    cols = pl.ds(at, CHUNK)
                    unit_x = (stream_in[slot, stream, inner, cols] - mean) * scale
                    e = parts[stream, rows, cols].astype(F32) * gains[stream : stream + 1, cols]
                    grad = scale * (e - mean_e - unit_x * mean_ex)
                    if stream == 3:
                        grad = grad + total_in[slot, inner, cols]
                    held[stream, :, cols] = grad
            for source in range(states):
                sums = [jnp.zeros((GROUP, 128), F32) for _ in range(4)]
                for at in range(0, width, CHUNK):
                    cols = pl.ds(at, CHUNK)
                    state = state_in[slot, source, inner, cols].astype(F32)
                    total = None
                    for stream in range(4):
                        k = stream * states + source
                        grad = held[stream, :, cols]
                        piece = weights[:, k : k + 1] * grad
                        total = piece if total is None else total + piece
                        product = state * grad
                        for lane_at in range(0, CHUNK, 128):
                            sums[stream] = sums[stream] + product[:, lane_at : lane_at + 128]
                    state_out[slot, source, inner, cols] = total.astype(BF16)
                for stream in range(4):
                    k = stream * states + source
                    mix_grad[rows, k : k + 1] = jnp.sum(sums[stream], axis=1, keepdims=True)

        unit_store(unit).start()

    def gain_copy(step):
        return pltpu.make_async_remote_copy(
            src_ref=gain_sent.at[step],
            dst_ref=gain_got.at[step],
            send_sem=gain_send.at[step],
            recv_sem=gain_recv.at[step],
            device_id=(partners[step], lane),
            device_id_type=MESH,
        )

    def gain_step(step):
        if step == 0:
            for stream in range(4):
                gain_sent[0, stream : stream + 1, :] = jnp.sum(
                    gain_grad[stream], axis=0, keepdims=True
                )
        else:
            gain_copy(step - 1).wait_recv()
            total = gain_sent[step - 1] + gain_got[step - 1]
            if step == steps:
                gain_sum[...] = total
            else:
                gain_sent[step] = total
        if step < steps:
            gain_copy(step).start()

    tasks = []
    for at in range(blocks):
        tasks.append((0.02 + 0.03 * at, to_link, at))
        tasks.append((0.19 + 0.16 * at, to_twin, at))
        tasks.append((0.23 + 0.16 * at, ready, at))
        for inner in range(per_block):
            tasks.append((0.24 + 0.16 * at + 0.035 * inner, run_unit, at * per_block + inner))
    for step in range(steps + 1):
        tasks.append((0.87 + 0.12 * step / steps, gain_step, step))
    tasks.sort(key=lambda item: item[0])
    first_part = 0.5 / (half - 0.5)
    for hop in range(1, half + 1):
        for piece in range(len(pieces)):
            passed = ((hop - 1.5 if hop > 1 else 0.0) + (piece + 1) / len(pieces) * (1 if hop > 1 else 0.5)) / (half - 0.5)
            cols = pl.ds(starts[piece], pieces[piece][2])
            for way in range(2):
                send(hop - 1, way, piece).wait_recv()
                if hop == half:
                    continue
                distance = (half - hop) * (1 - 2 * way)
                if hop == 1:
                    with_rows = pl.ds(way * cut, cut)
                    only_rows = pl.ds((1 - way) * cut, cut)
                    full = term(distance, piece)
                    got = ring[0, way, with_rows, cols].astype(F32)
                    ring[0, way, with_rows, cols] = (full[way * cut : way * cut + cut] + got).astype(BF16)
                    ring[0, way, only_rows, cols] = full[
                        (1 - way) * cut : (1 - way) * cut + cut
                    ].astype(BF16)
                else:
                    got = ring[hop - 1, way, :, cols].astype(F32)
                    ring[hop - 1, way, :, cols] = (term(distance, piece) + got).astype(BF16)
                send(hop, way, piece).start()
            if hop == half:
                total = (
                    term(0, piece)
                    + ring[hop - 1, 0, :, cols].astype(F32)
                    + ring[hop - 1, 1, :, cols].astype(F32)
                )
                which, at, count = pieces[piece]
                if which == 0:
                    grad_up[:, at : at + count] = total
                else:
                    (grad_query, grad_key, grad_value)[which - 1][...] = total
            while tasks and tasks[0][0] <= passed:
                _, run, value = tasks.pop(0)
                run(value)
    for _, run, value in tasks:
        run(value)
    for unit in range(max(units - 2, 0), units):
        unit_store(unit).wait()
    for step in range(steps):
        gain_copy(step).wait_send()
    for hop in range(half):
        for piece in range(len(pieces)):
            for way in range(2):
                send(hop, way, piece).wait_send()


def back_stage(size, normed, hidden_grad, qkv_low, stats, mix, gains, parts, history, streams, out_total):
    half = size // 2
    tokens, hidden = hidden_grad.shape
    states, _, width = history.shape
    shard = normed.shape[3]
    local = qkv_low.shape[1] // 3
    cols = hidden + 3 * local
    count = (hidden // 512 if half <= 4 else 1) + 3
    blocks = tokens // 128
    steps = size.bit_length() - 1
    vmem = pl.BlockSpec(memory_space=pltpu.VMEM)
    hbm = pl.BlockSpec(memory_space=pl.ANY)
    dma = pltpu.SemaphoreType.DMA
    small = jax.ShapeDtypeStruct((shard, local), F32)
    return pl.pallas_call(
        lambda *refs: back_kernel(size, *refs),
        in_specs=[vmem] * 6 + [hbm] * 4,
        out_specs=[vmem] * 4 + [hbm, vmem, vmem],
        out_shape=[
            jax.ShapeDtypeStruct((shard, hidden), F32),
            small,
            small,
            small,
            jax.ShapeDtypeStruct((states, tokens, width), BF16),
            jax.ShapeDtypeStruct((tokens, mix.shape[1]), F32),
            jax.ShapeDtypeStruct((4, width), F32),
        ],
        scratch_shapes=[
            pltpu.VMEM((4, 8, width), F32),
            pltpu.VMEM((steps, 4, width), F32),
            pltpu.VMEM((steps, 4, width), F32),
            pltpu.VMEM((4, tokens, width), BF16),
            pltpu.VMEM((blocks, 4, 64, width), BF16),
            pltpu.VMEM((blocks, 4, 64, width), BF16),
            pltpu.VMEM((shard, cols), BF16),
            pltpu.VMEM((half, 2, shard, cols), BF16),
            pltpu.VMEM((2, states, UNIT, width), BF16),
            pltpu.VMEM((2, 4, UNIT, width), F32),
            pltpu.VMEM((2, UNIT, width), F32),
            pltpu.VMEM((2, states, UNIT, width), BF16),
            pltpu.VMEM((4, GROUP, width), F32),
            dma((half, 2, count)),
            dma((half, 2, count)),
            dma((blocks,)),
            dma((blocks,)),
            dma((blocks,)),
            dma((blocks,)),
            dma((blocks,)),
            dma((blocks,)),
            dma(()),
            dma((2, 3)),
            dma((2,)),
            dma((steps,)),
            dma((steps,)),
            pltpu.SemaphoreType.REGULAR((blocks,)),
        ],
        cost_estimate=pl.CostEstimate(
            flops=tokens * width * 2000, bytes_accessed=tokens * width * 64, transcendentals=0
        ),
        compiler_params=pltpu.CompilerParams(
            collective_id=1, has_side_effects=True, vmem_limit_bytes=62 * MIB
        ),
        name="back_stage",
    )(normed, hidden_grad, qkv_low, stats, mix, gains, parts, history, streams, out_total)


TILE = 512


def unrotate(values, turn):
    return (
        values * turn[0]
        + pltpu.roll(values, HEAD_DIM - ROT // 2, 1) * turn[1]
        + pltpu.roll(values, ROT // 2, 1) * turn[2]
    )


def attention_probs(query, key, seg_col, seg_row):
    tokens = query.shape[0]
    scores = dot(query, key, ((1,), (1,))) * (HEAD_DIM ** (-0.5))
    later = lax.broadcasted_iota(jnp.int32, (tokens, tokens), 1) > lax.broadcasted_iota(
        jnp.int32, (tokens, tokens), 0
    )
    scores = jnp.where(jnp.logical_or(seg_col != seg_row, later), -1e30, scores)
    weights = jnp.exp(scores - jnp.max(scores, axis=1, keepdims=True))
    return weights / jnp.sum(weights, axis=1, keepdims=True)


def mid_kernel(
    size,
    low_t,
    grad_blocks,
    hidden,
    heads,
    turn,
    seg_col,
    seg_row,
    gen_grad,
    gen_gain,
    gen_mid,
    low_all,
    up_full,
    qkv_full,
    grad_out,
    grad_down,
    hidden_grad,
    qkv_low,
    parts,
    gen_sum,
    mid_sum,
    attended_grad,
    far,
    ring,
    low_tile,
    up_tile,
    qkv_tile,
    stage,
    gen_sent,
    gen_got,
    mid_sent,
    mid_got,
    ring_send,
    ring_recv,
    tile_sem,
    stage_sem,
    gen_send,
    gen_recv,
):
    half = size // 2
    rows_all, tokens = low_t.shape
    shard = grad_blocks.shape[2]
    local = heads.shape[1] // 3
    me = lax.axis_index("dp")
    lane = lax.axis_index("tensor")
    place = place_of(me, size)
    right = index_at(place + 1, size)
    left = index_at(place - 1, size)
    steps = size.bit_length() - 1
    partners = [me + (1 << step) * (1 - 2 * lax.rem(lax.div(me, 1 << step), 2)) for step in range(steps)]
    barrier = pltpu.get_barrier_semaphore()
    for there in [right, left] + partners:
        pl.semaphore_signal(barrier, inc=1, device_id=(there, lane), device_id_type=MESH)
    pl.semaphore_wait(barrier, 2 + steps)

    low_tiles = rows_all // TILE
    width_tiles = up_full.shape[0] // TILE
    order = (
        [("low", at) for at in range(low_tiles)]
        + [("up", at) for at in range(width_tiles)]
        + [("qkv", at) for at in range(width_tiles)]
    )

    def load(index):
        kind, at = order[index]
        slot = at % 2
        rows = pl.ds(at * TILE, TILE)
        if kind == "low":
            return pltpu.make_async_copy(low_all.at[:, rows, :], low_tile.at[slot], tile_sem.at[0, slot])
        if kind == "up":
            return pltpu.make_async_copy(up_full.at[rows, :], up_tile.at[slot], tile_sem.at[1, slot])
        return pltpu.make_async_copy(qkv_full.at[rows, :], qkv_tile.at[slot], tile_sem.at[2, slot])

    load(0).start()

    pieces = rows_all // TILE
    cut = TILE // 2

    def term(distance, piece):
        owner = index_at(place + distance, size)
        return jnp.dot(
            low_t[pl.ds(piece * TILE, TILE), :], grad_blocks[owner], preferred_element_type=F32
        )

    def send(hop, way, piece):
        if hop == 0:
            rows = pl.ds(piece * TILE + way * cut, cut)
            source = far.at[rows, :]
        else:
            rows = pl.ds(piece * TILE, TILE)
            source = ring.at[hop - 1, way, rows, :]
        return pltpu.make_async_remote_copy(
            src_ref=source,
            dst_ref=ring.at[hop, way, rows, :],
            send_sem=ring_send.at[hop, way, piece],
            recv_sem=ring_recv.at[hop, way, piece],
            device_id=((right, left)[way], lane),
            device_id_type=MESH,
        )

    for piece in range(pieces):
        far[pl.ds(piece * TILE, TILE), :] = term(half, piece).astype(BF16)
        for way in range(2):
            send(0, way, piece).start()

    def low_grad(at):
        index = at
        load(index + 1).start()
        load(index).wait()
        total = None
        for owner in range(size):
            part = dot(grad_blocks[owner], low_tile[at % 2, owner], ((1,), (1,)))
            total = part if total is None else total + part
        base = at * TILE
        if base < local:
            attended_grad[:, base : base + TILE] = total.astype(BF16)
        else:
            cols = slice(base - local, base - local + TILE)
            hidden_grad[:, cols] = (total * gelu_slope(hidden[:, cols])).astype(BF16)

    def head_grad(head):
        cols = slice(head * HEAD_DIM, (head + 1) * HEAD_DIM)
        key_cols = slice(local + head * HEAD_DIM, local + (head + 1) * HEAD_DIM)
        value_cols = slice(2 * local + head * HEAD_DIM, 2 * local + (head + 1) * HEAD_DIM)
        query, key, value = heads[:, cols], heads[:, key_cols], heads[:, value_cols]
        upstream = attended_grad[:, cols]
        probs = attention_probs(query, key, seg_col[...], seg_row[...])
        probs_grad = dot(upstream, value, ((1,), (1,)))
        qkv_low[:, value_cols] = dot(probs.astype(BF16), upstream, ((0,), (0,))).astype(BF16)
        row = jnp.sum(probs * probs_grad, axis=1, keepdims=True)
        scores_grad = (probs * (probs_grad - row)).astype(BF16)
        scale = HEAD_DIM ** (-0.5)
        turns = [turn[which] for which in range(3)]
        query_grad = dot(scores_grad, key, ((1,), (0,))) * scale
        qkv_low[:, cols] = unrotate(query_grad, turns).astype(BF16)
        key_grad = dot(scores_grad, query, ((0,), (0,))) * scale
        qkv_low[:, key_cols] = unrotate(key_grad, turns).astype(BF16)

    def part_store(stream, at):
        return pltpu.make_async_copy(
            stage.at[stream], parts.at[stream, :, pl.ds(at * TILE, TILE)], stage_sem.at[stream]
        )

    def up_part(at):
        index = low_tiles + at
        load(index + 1).start()
        load(index).wait()
        if at:
            part_store(3, at - 1).wait()
        stage[3] = dot(hidden_grad[...], up_tile[at % 2], ((1,), (1,))).astype(BF16)
        part_store(3, at).start()

    def qkv_part(at):
        index = low_tiles + width_tiles + at
        if index + 1 < len(order):
            load(index + 1).start()
        load(index).wait()
        for stream in range(3):
            if at:
                part_store(stream, at - 1).wait()
            cols = slice(stream * local, (stream + 1) * local)
            stage[stream] = dot(qkv_low[:, cols], qkv_tile[at % 2, :, cols], ((1,), (1,))).astype(BF16)
            part_store(stream, at).start()

    def gen_copies(step):
        return [
            pltpu.make_async_remote_copy(
                src_ref=sent.at[step],
                dst_ref=got.at[step],
                send_sem=gen_send.at[step, which],
                recv_sem=gen_recv.at[step, which],
                device_id=(partners[step], lane),
                device_id_type=MESH,
            )
            for which, (sent, got) in enumerate(((gen_sent, gen_got), (mid_sent, mid_got)))
        ]

    def gen_step(step):
        if step == 0:
            units = gen_grad.shape[0]
            gen_sent[0, :units, :] = gen_grad[...].astype(BF16)
            gen_sent[0, units:, :] = jnp.broadcast_to(
                gen_gain[...].astype(BF16), (gen_sent.shape[1] - units, gen_sent.shape[2])
            )
            mid_sent[0] = gen_mid[...]
        else:
            for copy in gen_copies(step - 1):
                copy.wait_recv()
            total = gen_sent[step - 1].astype(F32) + gen_got[step - 1].astype(F32)
            mid_total = mid_sent[step - 1] + mid_got[step - 1]
            if step == steps:
                gen_sum[...] = total
                mid_sum[...] = mid_total
            else:
                gen_sent[step] = total.astype(BF16)
                mid_sent[step] = mid_total
        if step < steps:
            for copy in gen_copies(step):
                copy.start()

    tasks = [(low_grad, at) for at in range(low_tiles)]
    tasks += [(head_grad, head) for head in range(local // HEAD_DIM)]
    tasks += [(up_part, at) for at in range(width_tiles)]
    tasks += [(qkv_part, at) for at in range(width_tiles)]
    for step in range(steps + 1):
        tasks.insert(2 + 5 * step if steps < 4 else 2 + 3 * step, (gen_step, step))
    count = len(tasks)
    slots = half * pieces
    slot = 0
    for hop in range(1, half + 1):
        for piece in range(pieces):
            rows = pl.ds(piece * TILE, TILE)
            for way in range(2):
                send(hop - 1, way, piece).wait_recv()
                if hop == half:
                    continue
                full = term((half - hop) * (1 - 2 * way), piece)
                if hop == 1:
                    with_rows = pl.ds(piece * TILE + way * cut, cut)
                    only_rows = pl.ds(piece * TILE + (1 - way) * cut, cut)
                    got = ring[0, way, with_rows, :].astype(F32)
                    ring[0, way, with_rows, :] = (full[way * cut : way * cut + cut] + got).astype(BF16)
                    ring[0, way, only_rows, :] = full[(1 - way) * cut : (1 - way) * cut + cut].astype(BF16)
                else:
                    got = ring[hop - 1, way, rows, :].astype(F32)
                    ring[hop - 1, way, rows, :] = (full + got).astype(BF16)
                send(hop, way, piece).start()
            if hop == half:
                total = (
                    term(0, piece)
                    + ring[hop - 1, 0, rows, :].astype(F32)
                    + ring[hop - 1, 1, rows, :].astype(F32)
                )
                base = piece * TILE
                if base < local:
                    grad_out[base : base + TILE, :] = total
                else:
                    grad_down[base - local : base - local + TILE, :] = total
            slot += 1
            while tasks and (slot == slots or len(tasks) * (slots - 2) > count * max(slots - 2 - slot, 0)):
                run, value = tasks.pop(0)
                run(value)
    for stream in range(4):
        part_store(stream, width_tiles - 1).wait()
    for step in range(steps):
        for copy in gen_copies(step):
            copy.wait_send()
    for hop in range(half):
        for piece in range(pieces):
            for way in range(2):
                send(hop, way, piece).wait_send()


def mid_stage(
    size,
    low_t,
    grad_blocks,
    hidden,
    heads,
    turn,
    seg_col,
    seg_row,
    gen_grad,
    gen_gain,
    gen_mid,
    low_all,
    up_full,
    qkv_full,
):
    half = size // 2
    rows_all, tokens = low_t.shape
    shard = grad_blocks.shape[2]
    hidden_cols = hidden.shape[1]
    local = heads.shape[1] // 3
    width = up_full.shape[0]
    pieces = rows_all // TILE
    steps = size.bit_length() - 1
    units = gen_grad.shape[0]
    vmem = pl.BlockSpec(memory_space=pltpu.VMEM)
    hbm = pl.BlockSpec(memory_space=pl.ANY)
    dma = pltpu.SemaphoreType.DMA
    return pl.pallas_call(
        lambda *refs: mid_kernel(size, *refs),
        in_specs=[vmem] * 10 + [hbm] * 3,
        out_specs=[vmem] * 4 + [hbm, vmem, vmem],
        out_shape=[
            jax.ShapeDtypeStruct((local, shard), F32),
            jax.ShapeDtypeStruct((hidden_cols, shard), F32),
            jax.ShapeDtypeStruct((tokens, hidden_cols), BF16),
            jax.ShapeDtypeStruct((tokens, 3 * local), BF16),
            jax.ShapeDtypeStruct((4, tokens, width), BF16),
            jax.ShapeDtypeStruct((units + 8, width), F32),
            jax.ShapeDtypeStruct(gen_mid.shape, F32),
        ],
        scratch_shapes=[
            pltpu.VMEM((tokens, local), BF16),
            pltpu.VMEM((rows_all, shard), BF16),
            pltpu.VMEM((half, 2, rows_all, shard), BF16),
            pltpu.VMEM((2, size, TILE, shard), BF16),
            pltpu.VMEM((2, TILE, hidden_cols), BF16),
            pltpu.VMEM((2, TILE, 3 * local), BF16),
            pltpu.VMEM((4, tokens, TILE), BF16),
            pltpu.VMEM((steps, units + 8, width), BF16),
            pltpu.VMEM((steps, units + 8, width), BF16),
            pltpu.VMEM((steps,) + gen_mid.shape, F32),
            pltpu.VMEM((steps,) + gen_mid.shape, F32),
            dma((half, 2, pieces)),
            dma((half, 2, pieces)),
            dma((3, 2)),
            dma((4,)),
            dma((steps, 2)),
            dma((steps, 2)),
        ],
        cost_estimate=pl.CostEstimate(
            flops=tokens * width * 4000, bytes_accessed=tokens * width * 40, transcendentals=0
        ),
        compiler_params=pltpu.CompilerParams(
            collective_id=2, has_side_effects=True, vmem_limit_bytes=62 * MIB
        ),
        name="mid_stage",
    )(
        low_t,
        grad_blocks,
        hidden,
        heads,
        turn,
        seg_col,
        seg_row,
        gen_grad,
        gen_gain,
        gen_mid,
        low_all,
        up_full,
        qkv_full,
    )


def front_kernel(
    size,
    mix,
    gains,
    turn,
    seg_col,
    seg_row,
    history,
    w_query,
    w_key,
    w_value,
    w_up,
    w_out,
    w_down,
    stats,
    heads,
    hidden,
    low_t,
    branch,
    normed_out,
    streams,
    qkv_all,
    up_all,
    low_all,
    normed,
    low,
    weight_tile,
    low_tile,
    state_in,
    stream_out,
    from_core,
    from_link,
    qkv_send,
    qkv_recv,
    up_send,
    up_recv,
    low_send,
    low_recv,
    own_sem,
    state_sem,
    stream_sem,
    normed_sem,
    weight_sem,
    tile_sem,
    core_send,
    core_recv,
    link_send,
    link_recv,
    twin_send,
    twin_recv,
    freed,
):
    half = size // 2
    states, tokens, width = history.shape
    shard = width // size
    local = w_query.shape[1]
    hidden_cols = w_up.shape[1]
    inverse = 1.0 / width
    me = lax.axis_index("dp")
    lane = lax.axis_index("tensor")
    place = place_of(me, size)
    right = index_at(place + 1, size)
    left = index_at(place - 1, size)
    core = lax.rem(lane, 2)
    chip = lax.div(lane, 2)
    twin = chip * 2 + 1 - core
    across = (1 - chip) * 2 + core
    rows_half = tokens // 2

    barrier = pltpu.get_barrier_semaphore()
    for there in ((right, lane), (left, lane), (me, twin), (me, across)):
        pl.semaphore_signal(barrier, inc=1, device_id=there, device_id_type=MESH)
    pl.semaphore_wait(barrier, 4)

    wide = TILE
    groups = [
        [(w_query, 0, 0), (w_key, 0, local), (w_value, 0, 2 * local)],
        [(w_up, at, at) for at in range(0, hidden_cols, wide)],
        [(w_out, at, at) for at in range(0, local, wide)]
        + [(w_down, at, local + at) for at in range(0, hidden_cols, wide)],
    ]
    sems = [(qkv_send, qkv_recv), (up_send, up_recv), (low_send, low_recv)]
    cut = (shard // 2, shard // 2, wide // 2)

    def own(group, piece, lo, count):
        source, at, _ = groups[group][piece]
        if group == 2:
            return source.at[pl.ds(at + lo, count), :]
        cols = local if group == 0 else wide
        return source.at[pl.ds(lo, count), pl.ds(at, cols)]

    def held(group, piece, owner, lo, count):
        _, _, at = groups[group][piece]
        if group == 2:
            return low_all.at[owner, pl.ds(at + lo, count), :]
        rows = pl.ds(pl.multiple_of(owner * shard + lo, cut[0]), count)
        if group == 0:
            return qkv_all.at[rows, pl.ds(at, local)]
        return up_all.at[rows, pl.ds(at, wide)]

    def send(group, hop, way, piece):
        owner = index_at(place + (hop - 1) * (2 * way - 1), size)
        whole = shard if group < 2 else wide
        lo, count = (0, whole) if hop < half else (way * cut[group], cut[group])
        target = held(group, piece, owner, lo, count)
        source = own(group, piece, lo, count) if hop == 1 else target
        send_sem, recv_sem = sems[group]
        return pltpu.make_async_remote_copy(
            src_ref=source,
            dst_ref=target,
            send_sem=send_sem.at[hop - 1, way, piece],
            recv_sem=recv_sem.at[hop - 1, way, piece],
            device_id=((right, left)[way], lane),
            device_id_type=MESH,
        )

    def own_copies(group):
        whole = shard if group < 2 else wide
        return [
            pltpu.make_async_copy(
                own(group, piece, 0, whole), held(group, piece, me, 0, whole), own_sem.at[group, piece]
            )
            for piece in range(len(groups[group]))
        ]

    units = tokens // UNIT

    def state_load(unit):
        return pltpu.make_async_copy(
            history.at[:, pl.ds(unit * UNIT, UNIT), :], state_in.at[unit % 2], state_sem.at[unit % 2]
        )

    def stream_store(unit):
        return pltpu.make_async_copy(
            stream_out.at[unit % 2], streams.at[:, pl.ds(unit * UNIT, UNIT), :], stream_sem.at[unit % 2]
        )

    def mix_unit(unit):
        slot = unit % 2
        if unit + 1 < units:
            state_load(unit + 1).start()
        state_load(unit).wait()
        if unit >= 2:
            stream_store(unit - 2).wait()

        @pl.loop(0, UNIT // GROUP)
        def _(step):
            rows = pl.ds(pl.multiple_of(unit * UNIT + step * GROUP, GROUP), GROUP)
            inner = pl.ds(pl.multiple_of(step * GROUP, GROUP), GROUP)
            weights = mix[rows, :]
            sums = [jnp.zeros((GROUP, 128), F32) for _ in range(4)]
            for at in range(0, width, CHUNK):
                cols = pl.ds(at, CHUNK)
                total = [None] * 4
                for source in range(states):
                    state = state_in[slot, source, inner, cols].astype(F32)
                    for stream in range(4):
                        k = stream * states + source
                        term = weights[:, k : k + 1] * state
                        total[stream] = term if source == 0 else total[stream] + term
                for stream in range(4):
                    stream_out[slot, stream, inner, cols] = total[stream]
                    for at_lane in range(0, CHUNK, 128):
                        sums[stream] = sums[stream] + total[stream][:, at_lane : at_lane + 128]
            for stream in range(4):
                mean = jnp.sum(sums[stream], axis=1, keepdims=True) * inverse
                square = jnp.zeros((GROUP, 128), F32)
                for at in range(0, width, CHUNK):
                    center = stream_out[slot, stream, inner, pl.ds(at, CHUNK)] - mean
                    center = center * center
                    for at_lane in range(0, CHUNK, 128):
                        square = square + center[:, at_lane : at_lane + 128]
                scale = lax.rsqrt(jnp.sum(square, axis=1, keepdims=True) * inverse + EPSILON)
                stats[rows, stream : stream + 1] = mean
                stats[rows, 4 + stream : 5 + stream] = scale
                for at in range(0, width, CHUNK):
                    cols = pl.ds(at, CHUNK)
                    center = stream_out[slot, stream, inner, cols] - mean
                    value = (center * scale * gains[stream : stream + 1, cols]).astype(BF16)
                    for owner in range(at // shard, (at + CHUNK) // shard):
                        base = owner * shard - at
                        normed[stream, owner, rows, :] = value[:, base : base + shard]

        stream_store(unit).start()
        if unit == units - 1:
            normed_store().start()

    def normed_store():
        return pltpu.make_async_copy(normed, normed_out, normed_sem)

    tiles = 3 + hidden_cols // wide

    def weight_load(tile):
        if tile < 3:
            source = qkv_all.at[:, pl.ds(tile * local, local)]
        else:
            source = up_all.at[:, pl.ds((tile - 3) * wide, wide)]
        return pltpu.make_async_copy(source, weight_tile.at[tile % 2], weight_sem.at[tile % 2])

    def arrived(group):
        for copy in own_copies(group):
            copy.wait()
        for piece in range(len(groups[group])):
            for way in range(2):
                send(group, half, way, piece).wait_recv()

    def tile_product(tile, stream):
        weight_load(tile).wait()
        total = None
        for owner in range(size):
            part = jnp.dot(
                normed[stream, owner],
                weight_tile[tile % 2, owner * shard : (owner + 1) * shard, :],
                preferred_element_type=F32,
            )
            total = part if total is None else total + part
        return total

    def qkv_task(which):
        if which == 0:
            arrived(0)
            weight_load(0).start()
        if which < 2:
            weight_load(which + 1).start()
        product = tile_product(which, which)
        for head in range(local // HEAD_DIM):
            at = head * HEAD_DIM
            part = product[:, at : at + HEAD_DIM]
            if which < 2:
                part = (
                    part * turn[0]
                    - pltpu.roll(part, HEAD_DIM - ROT // 2, 1) * turn[1]
                    - pltpu.roll(part, ROT // 2, 1) * turn[2]
                )
            heads[:, which * local + at : which * local + at + HEAD_DIM] = part.astype(BF16)

    def head_task(head):
        at = head * HEAD_DIM
        query = heads[:, at : at + HEAD_DIM]
        key = heads[:, local + at : local + at + HEAD_DIM]
        value = heads[:, 2 * local + at : 2 * local + at + HEAD_DIM]
        probs = attention_probs(query, key, seg_col[...], seg_row[...]).astype(BF16)
        attended = jnp.dot(probs, value, preferred_element_type=F32)
        low[:, at : at + HEAD_DIM] = attended.astype(BF16)
        low_t[at : at + HEAD_DIM, :] = attended.T.astype(BF16)

    def up_task(at):
        if at == 0:
            arrived(1)
            weight_load(3).start()
        if at + 1 < tiles - 3:
            weight_load(4 + at).start()
        product = tile_product(3 + at, 3)
        cols = slice(at * wide, (at + 1) * wide)
        hidden[:, cols] = product
        active = gelu(product)
        low[:, local + at * wide : local + (at + 1) * wide] = active.astype(BF16)
        low_t[local + at * wide : local + (at + 1) * wide, :] = active.T.astype(BF16)

    distances = [0]
    for hop in range(1, half):
        distances += [-hop, hop]
    distances += [half]

    def tile_load(index):
        owner = index_at(place + distances[index], size)
        return pltpu.make_async_copy(low_all.at[owner], low_tile.at[index % 2], tile_sem.at[index % 2])

    def mine(index):
        return pl.ds(pl.multiple_of(core * rows_half, rows_half), rows_half)

    def core_copy(index):
        owner = index_at(place + distances[index], size)
        rows = pl.ds(pl.multiple_of((1 - core) * rows_half, rows_half), rows_half)
        return pltpu.make_async_remote_copy(
            src_ref=branch.at[owner, rows, :],
            dst_ref=from_core.at[index],
            send_sem=core_send.at[index],
            recv_sem=core_recv.at[index],
            device_id=(me, twin),
            device_id_type=MESH,
        )

    def link_copy(index):
        owner = index_at(place + distances[index], size)
        return pltpu.make_async_remote_copy(
            src_ref=branch.at[owner, mine(index), :],
            dst_ref=from_link.at[index],
            send_sem=link_send.at[index],
            recv_sem=link_recv.at[index],
            device_id=(me, across),
            device_id_type=MESH,
        )

    def twin_copy(index):
        owner = index_at(place + distances[index], size)
        return pltpu.make_async_remote_copy(
            src_ref=branch.at[owner, mine(index), :],
            dst_ref=branch.at[owner, mine(index), :],
            send_sem=twin_send.at[index],
            recv_sem=twin_recv.at[index],
            device_id=(me, twin),
            device_id_type=MESH,
        )

    def low_task(index):
        if index == 0:
            for copy in own_copies(2):
                copy.wait()
        owner = index_at(place + distances[index], size)
        load = tile_load(index)
        load.start()
        load.wait()
        branch[owner] = jnp.dot(low[...], low_tile[index % 2], preferred_element_type=F32).astype(BF16)
        core_copy(index).start()

    def add_into(index, other):
        owner = index_at(place + distances[index], size)
        rows = mine(index)
        branch[owner, rows, :] = (
            branch[owner, rows, :].astype(F32) + other[index].astype(F32)
        ).astype(BF16)

    def link_task(index):
        copy = core_copy(index)
        copy.wait_send()
        pl.semaphore_signal(freed.at[index], inc=1, device_id=(me, twin), device_id_type=MESH)
        copy.wait_recv()
        add_into(index, from_core)
        link_copy(index).start()

    def twin_task(index):
        copy = link_copy(index)
        copy.wait_send()
        copy.wait_recv()
        add_into(index, from_link)
        pl.semaphore_wait(freed.at[index], 1)
        twin_copy(index).start()

    state_load(0).start()
    slots = [(group, hop) for group in range(3) for hop in range(1, half + 1)]
    counts = [len(pieces) for pieces in groups]
    first = [0, counts[0] * half, (counts[0] + counts[1]) * half]
    total_slots = sum(counts) * half
    tasks = []
    span = max(first[1] - 2, 1)
    for unit in range(units):
        tasks.append((counts[0] - 1 + unit * (first[1] - counts[0]) / units, mix_unit, unit))
    early = first[1] + counts[1]
    for which in range(3):
        tasks.append((early + which, qkv_task, which))
    for head in range(local // HEAD_DIM):
        tasks.append((early + 3 + head, head_task, head))
    middle = first[2] + counts[2]
    for at in range(tiles - 3):
        tasks.append((middle + at, up_task, at))
    for index in range(len(distances) - 1):
        due = max(first[2] + counts[2] * (abs(distances[index]) + 1) - 1, middle + tiles - 3) + 0.5 * (index % 2)
        tasks.append((due, low_task, index))
        tasks.append((due + 1, link_task, index))
        tasks.append((due + 3, twin_task, index))
    tasks.sort(key=lambda item: item[0])

    at_slot = 0
    for group, hop in slots:
        if hop == 1:
            for copy in own_copies(group):
                copy.start()
        for piece in range(counts[group]):
            for way in range(2):
                if hop > 1:
                    send(group, hop - 1, way, piece).wait_recv()
                if hop < half or True:
                    send(group, hop, way, piece).start()
            while tasks and tasks[0][0] <= at_slot and at_slot < total_slots - 1:
                _, run, value = tasks.pop(0)
                run(value)
            at_slot += 1
    for _, run, value in tasks:
        run(value)
    for piece in range(counts[2]):
        for way in range(2):
            send(2, half, way, piece).wait_recv()
    last = len(distances) - 1
    low_task(last)
    link_task(last)
    twin_task(last)
    for index in range(len(distances)):
        copy = twin_copy(index)
        copy.wait_send()
        copy.wait_recv()
    for unit in range(units - 2, units):
        stream_store(unit).wait()
    normed_store().wait()
    for group, hop in slots:
        for piece in range(counts[group]):
            for way in range(2):
                send(group, hop, way, piece).wait_send()


def front_stage(size, mix, gains, turn, seg_col, seg_row, history, w_query, w_key, w_value, w_up, w_out, w_down):
    half = size // 2
    states, tokens, width = history.shape
    shard = width // size
    local = w_query.shape[1]
    hidden_cols = w_up.shape[1]
    rows_all = local + hidden_cols
    vmem = pl.BlockSpec(memory_space=pltpu.VMEM)
    hbm = pl.BlockSpec(memory_space=pl.ANY)
    dma = pltpu.SemaphoreType.DMA
    up_pieces = hidden_cols // TILE
    low_pieces = rows_all // TILE
    return pl.pallas_call(
        lambda *refs: front_kernel(size, *refs),
        in_specs=[vmem] * 5 + [hbm] * 7,
        out_specs=[vmem] * 5 + [hbm] * 5,
        out_shape=[
            jax.ShapeDtypeStruct((tokens, 8), F32),
            jax.ShapeDtypeStruct((tokens, 3 * local), BF16),
            jax.ShapeDtypeStruct((tokens, hidden_cols), F32),
            jax.ShapeDtypeStruct((rows_all, tokens), BF16),
            jax.ShapeDtypeStruct((size, tokens, shard), BF16),
            jax.ShapeDtypeStruct((4, size, tokens, shard), BF16),
            jax.ShapeDtypeStruct((4, tokens, width), F32),
            jax.ShapeDtypeStruct((width, 3 * local), BF16),
            jax.ShapeDtypeStruct((width, hidden_cols), BF16),
            jax.ShapeDtypeStruct((size, rows_all, shard), BF16),
        ],
        scratch_shapes=[
            pltpu.VMEM((4, size, tokens, shard), BF16),
            pltpu.VMEM((tokens, rows_all), BF16),
            pltpu.VMEM((2, width, TILE), BF16),
            pltpu.VMEM((2, rows_all, shard), BF16),
            pltpu.VMEM((2, states, UNIT, width), BF16),
            pltpu.VMEM((2, 4, UNIT, width), F32),
            pltpu.VMEM((size, tokens // 2, shard), BF16),
            pltpu.VMEM((size, tokens // 2, shard), BF16),
            dma((half, 2, 3)),
            dma((half, 2, 3)),
            dma((half, 2, up_pieces)),
            dma((half, 2, up_pieces)),
            dma((half, 2, low_pieces)),
            dma((half, 2, low_pieces)),
            dma((3, low_pieces)),
            dma((2,)),
            dma((2,)),
            dma(()),
            dma((2,)),
            dma((2,)),
            dma((size,)),
            dma((size,)),
            dma((size,)),
            dma((size,)),
            dma((size,)),
            dma((size,)),
            pltpu.SemaphoreType.REGULAR((size,)),
        ],
        cost_estimate=pl.CostEstimate(
            flops=tokens * width * 8000, bytes_accessed=tokens * width * 80, transcendentals=0
        ),
        compiler_params=pltpu.CompilerParams(
            collective_id=3, has_side_effects=True, vmem_limit_bytes=62 * MIB
        ),
        name="front_stage",
    )(mix, gains, turn, seg_col, seg_row, history, w_query, w_key, w_value, w_up, w_out, w_down)


def body(
    sizes,
    history,
    mix_weights,
    segments,
    norm_gains,
    w_query,
    w_key,
    w_value,
    w_out,
    w_up,
    w_down,
    gen_in,
    gen_out,
    out_grad,
    next_grad,
):
    dp_size, tensor_size = sizes
    width = history.shape[2]
    tok_count = history.shape[1]
    mix_rows = mix_weights.T
    cos_row, sin_row = rotary_tables(segments)
    blank = jnp.zeros((tok_count, HEAD_DIM - ROT // 2), F32)
    turn = jnp.stack(
        [
            jnp.concatenate([cos_row, cos_row, blank[:, ROT // 2 :] + 1.0], axis=1),
            jnp.concatenate([sin_row, blank], axis=1),
            jnp.concatenate([blank[:, : ROT // 2], -sin_row, blank[:, ROT // 2 :]], axis=1),
        ]
    )
    seg_col, seg_row = segments[:, None], segments[None, :]
    stats, heads, hidden, low_t, branch, normed, streams, full_qkv, full_up, low_all = front_stage(
        dp_size,
        mix_rows,
        norm_gains,
        turn,
        seg_col,
        seg_row,
        history,
        w_query,
        w_key,
        w_value,
        w_up,
        w_out,
        w_down,
    )
    layer_out, next_mix, out_total, branch_grad, gain_gen_grad, grad_gen_in, grad_gen_out = gen_stage(
        dp_size, streams, branch, norm_gains, gen_in, gen_out, out_grad, next_grad.T
    )

    gen_units, gen_next = gen_out.shape
    gen_mid = jnp.pad(grad_gen_out, ((0, 0), (0, 128 - gen_next)))
    grad_out, grad_down, hidden_grad, qkv_low, parts, gen_sum, mid_sum = mid_stage(
        dp_size,
        low_t,
        branch_grad,
        hidden,
        heads,
        turn,
        seg_col,
        seg_row,
        grad_gen_in,
        gain_gen_grad,
        gen_mid,
        low_all,
        full_up,
        full_qkv,
    )
    grad_up, grad_query, grad_key, grad_value, history_grad, mix_grad, gain_sums = back_stage(
        dp_size,
        normed,
        hidden_grad,
        qkv_low,
        stats,
        mix_rows,
        norm_gains,
        parts,
        history,
        streams,
        out_total,
    )
    return (
        layer_out,
        next_mix.T,
        history_grad,
        mix_grad.T,
        jnp.concatenate([gain_sums, gen_sum[gen_units : gen_units + 1]], axis=0),
        grad_query,
        grad_key,
        grad_value,
        grad_out,
        grad_up,
        grad_down,
        gen_sum[:gen_units].T,
        mid_sum[:, :gen_next],
    )


def solution(mesh):
    sizes = (mesh.shape["dp"], mesh.shape["tensor"])
    in_specs = (
        P(None, "dp", None),
        P(None, "dp"),
        P("dp"),
        P(),
        P("dp", "tensor"),
        P("dp", "tensor"),
        P("dp", "tensor"),
        P("tensor", "dp"),
        P("dp", "tensor"),
        P("tensor", "dp"),
        P(),
        P(),
        P("dp", None),
        P(None, "dp"),
    )
    out_specs = (
        P("dp", None),
        P(None, "dp"),
        P(None, "dp", None),
        P(None, "dp"),
        P(),
        P("dp", "tensor"),
        P("dp", "tensor"),
        P("dp", "tensor"),
        P("tensor", "dp"),
        P("dp", "tensor"),
        P("tensor", "dp"),
        P(),
        P(),
    )

    def step(*arrays):
        return body(sizes, *arrays)

    return jax.shard_map(step, mesh=mesh, in_specs=in_specs, out_specs=out_specs, check_vma=False)
```

```python
import jax
import jax.numpy as jnp
import numpy as np
from jax import lax
from jax.experimental import pallas as pl
from jax.experimental.pallas import tpu as pltpu
from jax.sharding import PartitionSpec as P

HEAD_DIM = 128
ROT = 32


EPSILON = 1e-05
ROPE_BASE = 10000.0

F32 = jnp.float32
BF16 = jnp.bfloat16


MIB = 1 << 20
GROUP = 16
CHUNK = 512


def gelu(x):
    return 0.5 * x * (1.0 + lax.erf(x * (0.5**0.5)))


def gelu_slope(x):
    return 0.5 * (1.0 + lax.erf(x * (0.5**0.5))) + x * jnp.exp(-0.5 * x * x) * 0.3989422804014327


def dot(a, b, dims):
    return lax.dot_general(a, b, (dims, ((), ())), preferred_element_type=F32)


def gen_kernel(stream, branch, gain, gen_in, gen_out, out_grad, next_grad, layer_out, next_mix, out_total, branch_grad, gain_grad, in_grad, mid_grad):
    first = pl.program_id(0) == 0
    x = stream[0] + jnp.concatenate([branch[owner] for owner in range(branch.shape[0])], axis=1).astype(F32)
    layer_out[...] = x.astype(BF16)
    center = x - jnp.mean(x, axis=1, keepdims=True)
    scale = lax.rsqrt(jnp.mean(center * center, axis=1, keepdims=True) + EPSILON)
    unit = center * scale
    gains = gain[4:5, :]
    low = (unit * gains).astype(BF16)
    hidden = dot(low, gen_in[...], ((1,), (1,)))
    active = gelu(hidden).astype(BF16)
    next_mix[...] = dot(active, gen_out[...], ((1,), (0,))).T
    upstream = next_grad[...].T.astype(BF16)
    active_grad = dot(upstream, gen_out[...], ((1,), (1,)))
    hidden_grad = (active_grad * gelu_slope(hidden)).astype(BF16)
    y = dot(hidden_grad, gen_in[...], ((1,), (0,)))
    e = y * gains
    grad = scale * (
        e - jnp.mean(e, axis=1, keepdims=True) - unit * jnp.mean(e * unit, axis=1, keepdims=True)
    )
    total = out_grad[...].astype(F32) + grad
    out_total[...] = total
    low_total = total.astype(BF16)
    shard = branch_grad.shape[2]
    for owner in range(branch_grad.shape[0]):
        branch_grad[owner] = low_total[:, owner * shard : (owner + 1) * shard]
    gain_part = jnp.sum(y * unit, axis=0, keepdims=True)
    in_part = dot(hidden_grad, low, ((0,), (0,)))
    mid_part = dot(active, upstream, ((0,), (0,)))

    @pl.when(first)
    def _():
        gain_grad[...] = gain_part
        in_grad[...] = in_part
        mid_grad[...] = jnp.zeros_like(mid_grad)
        mid_grad[:, : mid_part.shape[1]] = mid_part

    @pl.when(jnp.logical_not(first))
    def _():
        gain_grad[...] += gain_part
        in_grad[...] += in_part
        mid_grad[:, : mid_part.shape[1]] += mid_part


def gen_stage(size, streams, branch, gains, gen_in, gen_out, out_grad, next_grad, block=128):
    _, tokens, width = streams.shape
    units = gen_in.shape[0]
    nxt = gen_out.shape[1]
    row = lambda i: (i, 0)
    fixed = lambda i: (0, 0)
    return pl.pallas_call(
        gen_kernel,
        grid=(tokens // block,),
        in_specs=[
            pl.BlockSpec((1, block, width), lambda i: (3, i, 0)),
            pl.BlockSpec((size, block, width // size), lambda i: (0, i, 0)),
            pl.BlockSpec(gains.shape, fixed),
            pl.BlockSpec(gen_in.shape, fixed),
            pl.BlockSpec(gen_out.shape, fixed),
            pl.BlockSpec((block, width), row),
            pl.BlockSpec((nxt, block), lambda i: (0, i)),
        ],
        out_specs=[
            pl.BlockSpec((block, width), row),
            pl.BlockSpec((nxt, block), lambda i: (0, i)),
            pl.BlockSpec((block, width), row),
            pl.BlockSpec((size, block, width // size), lambda i: (0, i, 0)),
            pl.BlockSpec((1, width), fixed),
            pl.BlockSpec((units, width), fixed),
            pl.BlockSpec((units, 128), fixed),
        ],
        out_shape=[
            jax.ShapeDtypeStruct((tokens, width), BF16),
            jax.ShapeDtypeStruct((nxt, tokens), F32),
            jax.ShapeDtypeStruct((tokens, width), F32),
            jax.ShapeDtypeStruct((size, tokens, width // size), BF16),
            jax.ShapeDtypeStruct((1, width), F32),
            jax.ShapeDtypeStruct((units, width), F32),
            jax.ShapeDtypeStruct((units, 128), F32),
        ],
        cost_estimate=pl.CostEstimate(
            flops=tokens * width * 300, bytes_accessed=tokens * width * 16, transcendentals=0
        ),
        compiler_params=pltpu.CompilerParams(vmem_limit_bytes=62 * MIB),
        name="gen_stage",
    )(streams, branch, gains, gen_in, gen_out, out_grad, next_grad)


MESH = pl.DeviceIdType.MESH


def place_of(me, size):
    odd = lax.rem(me, 2)
    at = lax.div(me, 2)
    return (1 - odd) * at + odd * (size - 1 - at)


def index_at(place, size):
    at = lax.rem(place + 2 * size, size)
    back = lax.div(at, size // 2)
    return (1 - back) * 2 * at + back * (2 * (size - 1 - at) + 1)


UNIT = 32


def back_kernel(
    size,
    stats,
    mix,
    gains,
    normed_in,
    hidden_grad_in,
    qkv_low_in,
    parts_in,
    history,
    streams,
    out_total,
    mix_grad,
    gain_sum,
    grad_up_out,
    grad_query_out,
    grad_key_out,
    grad_value_out,
    stream_grad,
    normed,
    hidden_grad,
    qkv_low,
    grad_up,
    grad_qkv,
    gain_grad,
    gain_sent,
    gain_got,
    parts,
    from_core,
    from_link,
    far,
    ring,
    state_in,
    stream_in,
    total_in,
    grad_out,
    held,
    flipped,
    in_sem,
    out_sem,
    ring_send,
    ring_recv,
    core_send,
    core_recv,
    link_send,
    link_recv,
    twin_send,
    twin_recv,
    load_sem,
    unit_sem,
    store_sem,
    gain_send,
    gain_recv,
    freed,
):
    half = size // 2
    shard = normed.shape[3]
    cut = shard // 2
    tokens, hidden_cols = hidden_grad.shape
    width = history.shape[2]
    inverse = 1.0 / width
    states = history.shape[0]
    me = lax.axis_index("dp")
    lane = lax.axis_index("tensor")
    place = place_of(me, size)
    right = index_at(place + 1, size)
    left = index_at(place - 1, size)
    core = lax.rem(lane, 2)
    chip = lax.div(lane, 2)
    twin = chip * 2 + 1 - core
    across = (1 - chip) * 2 + core

    loads = [
        pltpu.make_async_copy(hidden_grad_in, hidden_grad, in_sem.at[4]),
        pltpu.make_async_copy(normed_in.at[3], normed.at[3], in_sem.at[3]),
        pltpu.make_async_copy(qkv_low_in, qkv_low, in_sem.at[5]),
    ] + [
        pltpu.make_async_copy(normed_in.at[stream], normed.at[stream], in_sem.at[stream])
        for stream in range(3)
    ]
    for copy in loads:
        copy.start()

    barrier = pltpu.get_barrier_semaphore()
    steps = size.bit_length() - 1
    partners = [me + (1 << step) * (1 - 2 * lax.rem(lax.div(me, 1 << step), 2)) for step in range(steps)]
    for there in [(right, lane), (left, lane), (me, twin), (me, across)] + [(it, lane) for it in partners]:
        pl.semaphore_signal(barrier, inc=1, device_id=there, device_id_type=MESH)
    pl.semaphore_wait(barrier, 4 + steps)

    block = 64
    rows_half = tokens // 2
    blocks = rows_half // block
    load = pltpu.make_async_copy(parts_in, parts, load_sem)
    load.start()

    wide = 512 if half <= 4 else hidden_cols
    pieces = [(0, at, wide) for at in range(0, hidden_cols, wide)]
    local = qkv_low.shape[1] // 3
    pieces += [(1 + which, which * local, local) for which in range(3)]
    starts = []
    offset = 0
    for _, _, cols in pieces:
        starts.append(offset)
        offset += cols

    def flip(way, distance, some=(0, 1, 2, 3)):
        owner = index_at(place + distance, size)
        for stream in some:
            flipped[way, stream] = normed[stream, owner].T

    def term(way, piece, rows):
        which, at, cols = pieces[piece]
        stream = 3 if which == 0 else which - 1
        other = hidden_grad if which == 0 else qkv_low
        return jnp.dot(
            flipped[way, stream, rows, :], other[:, at : at + cols], preferred_element_type=F32
        )

    def send(hop, way, piece):
        cols = pl.ds(starts[piece], pieces[piece][2])
        if hop == 0:
            rows = pl.ds(way * cut, cut)
            source = far.at[rows, cols]
            target = ring.at[0, way, rows, cols]
        else:
            source = ring.at[hop - 1, way, :, cols]
            target = ring.at[hop, way, :, cols]
        return pltpu.make_async_remote_copy(
            src_ref=source,
            dst_ref=target,
            send_sem=ring_send.at[hop, way, piece],
            recv_sem=ring_recv.at[hop, way, piece],
            device_id=((right, left)[way], lane),
            device_id_type=MESH,
        )

    for copy in loads[:2]:
        copy.wait()
    flip(0, half, (3,))
    for piece in range(len(pieces)):
        if pieces[piece][0] == 1:
            for copy in loads[2:]:
                copy.wait()
            flip(0, half, (0, 1, 2))
        cols = pl.ds(starts[piece], pieces[piece][2])

        def far_rows(rows):
            far[rows, cols] = term(0, piece, rows).astype(BF16)

        row_loop(0, shard, far_rows)
        for way in range(2):
            send(0, way, piece).start()
        if piece == 0:
            load.wait()
            for at in range(blocks):
                rows = pl.ds(pl.multiple_of((1 - core) * rows_half + at * block, block), block)
                pltpu.make_async_remote_copy(
                    src_ref=parts.at[:, rows, :],
                    dst_ref=from_core.at[at],
                    send_sem=core_send.at[at],
                    recv_sem=core_recv.at[at],
                    device_id=(me, twin),
                    device_id_type=MESH,
                ).start()

    def mine(at):
        return pl.ds(pl.multiple_of(core * rows_half + at * block, block), block)

    def core_copy(at):
        rows = pl.ds(pl.multiple_of((1 - core) * rows_half + at * block, block), block)
        return pltpu.make_async_remote_copy(
            src_ref=parts.at[:, rows, :],
            dst_ref=from_core.at[at],
            send_sem=core_send.at[at],
            recv_sem=core_recv.at[at],
            device_id=(me, twin),
            device_id_type=MESH,
        )

    def link_copy(at):
        return pltpu.make_async_remote_copy(
            src_ref=parts.at[:, mine(at), :],
            dst_ref=from_link.at[at],
            send_sem=link_send.at[at],
            recv_sem=link_recv.at[at],
            device_id=(me, across),
            device_id_type=MESH,
        )

    def twin_copy(at):
        return pltpu.make_async_remote_copy(
            src_ref=parts.at[:, mine(at), :],
            dst_ref=parts.at[:, mine(at), :],
            send_sem=twin_send.at[at],
            recv_sem=twin_recv.at[at],
            device_id=(me, twin),
            device_id_type=MESH,
        )

    def add_into(at, other):
        base = core * rows_half + at * block

        @pl.loop(0, block // 16)
        def _(step):
            rows = pl.ds(pl.multiple_of(base + step * 16, 16), 16)
            theirs = pl.ds(pl.multiple_of(step * 16, 16), 16)
            for stream in range(4):
                total = parts[stream, rows, :].astype(F32) + other[at, stream, theirs, :].astype(F32)
                parts[stream, rows, :] = total.astype(BF16)

    def to_link(at):
        copy = core_copy(at)
        copy.wait_send()
        pl.semaphore_signal(freed.at[at], inc=1, device_id=(me, twin), device_id_type=MESH)
        copy.wait_recv()
        add_into(at, from_core)
        link_copy(at).start()

    def to_twin(at):
        copy = link_copy(at)
        copy.wait_send()
        copy.wait_recv()
        add_into(at, from_link)
        pl.semaphore_wait(freed.at[at], 1)
        twin_copy(at).start()

    def ready(at):
        copy = twin_copy(at)
        copy.wait_send()
        copy.wait_recv()

    def grad_copy(piece):
        which, at, count = pieces[piece]
        if which == 0:
            source = grad_up.at[:, pl.ds(at, count)]
            target = grad_up_out.at[:, pl.ds(at, count)]
        else:
            source = grad_qkv.at[which - 1]
            target = (grad_query_out, grad_key_out, grad_value_out)[which - 1]
        return pltpu.make_async_copy(source, target, out_sem.at[piece])

    def unit_loads(base, slot):
        rows = pl.ds(pl.multiple_of(base, UNIT), UNIT)
        return (
            pltpu.make_async_copy(history.at[:, rows, :], state_in.at[slot], unit_sem.at[slot, 0]),
            pltpu.make_async_copy(streams.at[:, rows, :], stream_in.at[slot], unit_sem.at[slot, 1]),
            pltpu.make_async_copy(out_total.at[rows, :], total_in.at[slot], unit_sem.at[slot, 2]),
        )

    def unit_store(base, slot):
        rows = pl.ds(pl.multiple_of(base, UNIT), UNIT)
        return pltpu.make_async_copy(grad_out.at[slot], stream_grad.at[:, rows, :], store_sem.at[slot])

    mixes = 2 * blocks

    def task_base(task):
        at, side = divmod(task, 2)
        return side * rows_half + at * block

    gain_grad[...] = jnp.zeros_like(gain_grad)
    mix_grad[...] = jnp.zeros_like(mix_grad)
    for copy in unit_loads(0, 0):
        copy.start()

    def mix_task(task):
        first = task_base(task)

        @pl.loop(0, 2)
        def _(slot):
            @pl.when(slot == 0)
            def _():
                for copy in unit_loads(first + UNIT, 1):
                    copy.start()

            if task + 1 < mixes:

                @pl.when(slot == 1)
                def _():
                    for copy in unit_loads(task_base(task + 1), 0):
                        copy.start()

            for copy in unit_loads(first + slot * UNIT, slot):
                copy.wait()
            if task > 0:
                unit_store(task_base(task - 1) + slot * UNIT, slot).wait()

            @pl.loop(0, UNIT // GROUP)
            def _(step):
                mix_group(first + slot * UNIT + step * GROUP, slot, step * GROUP)

            unit_store(first + slot * UNIT, slot).start()

    def mix_group(base, slot, inner_base):
        rows = pl.ds(pl.multiple_of(base, GROUP), GROUP)
        inner = pl.ds(pl.multiple_of(inner_base, GROUP), GROUP)
        zero = jnp.zeros((GROUP, 128), F32)
        chunks = width // CHUNK

        def window(at):
            return pl.ds(at * CHUNK, CHUNK)

        def lanes(total, value):
            for at_lane in range(0, CHUNK, 128):
                total = total + value[:, at_lane : at_lane + 128]
            return total

        for stream in range(4):
            mean = stats[rows, stream : stream + 1]
            scale = stats[rows, 4 + stream : 5 + stream]
            sum_e, sum_ex = zero, zero
            for at in range(chunks):
                cols = window(at)
                unit_x = (stream_in[slot, stream, inner, cols] - mean) * scale
                upstream = parts[stream, rows, cols].astype(F32)
                e = upstream * gains[stream : stream + 1, cols]
                gain = upstream * unit_x
                gain_grad[stream, :, cols] += gain[:8] + gain[8:]
                sum_e = lanes(sum_e, e)
                sum_ex = lanes(sum_ex, e * unit_x)
            mean_e = jnp.sum(sum_e, axis=1, keepdims=True) * inverse
            mean_ex = jnp.sum(sum_ex, axis=1, keepdims=True) * inverse
            for at in range(chunks):
                cols = window(at)
                unit_x = (stream_in[slot, stream, inner, cols] - mean) * scale
                e = parts[stream, rows, cols].astype(F32) * gains[stream : stream + 1, cols]
                grad = scale * (e - mean_e - unit_x * mean_ex)
                if stream == 3:
                    grad = grad + total_in[slot, inner, cols]
                held[stream, :, cols] = grad
                grad_out[slot, stream, inner, cols] = grad.astype(BF16)
        for source in range(states):
            sums = [zero] * 4
            for at in range(chunks):
                cols = window(at)
                state = state_in[slot, source, inner, cols].astype(F32)
                for stream in range(4):
                    sums[stream] = lanes(sums[stream], state * held[stream, :, cols])
            for stream in range(4):
                k = stream * states + source
                mix_grad[rows, k : k + 1] = jnp.sum(sums[stream], axis=1, keepdims=True)

    def gain_copy(step):
        return pltpu.make_async_remote_copy(
            src_ref=gain_sent.at[step],
            dst_ref=gain_got.at[step],
            send_sem=gain_send.at[step],
            recv_sem=gain_recv.at[step],
            device_id=(partners[step], lane),
            device_id_type=MESH,
        )

    def gain_step(step):
        if step == 0:
            for stream in range(4):
                gain_sent[0, stream : stream + 1, :] = jnp.sum(
                    gain_grad[stream], axis=0, keepdims=True
                )
        else:
            gain_copy(step - 1).wait_recv()
            total = gain_sent[step - 1] + gain_got[step - 1]
            if step == steps:
                gain_sum[...] = total
            else:
                gain_sent[step] = total
        if step < steps:
            gain_copy(step).start()

    tasks = []
    for at in range(blocks):
        tasks.append((0.02 + 0.03 * at, to_link, at))
        tasks.append((0.19 + 0.16 * at, to_twin, at))
        tasks.append((0.23 + 0.16 * at, ready, at))
        for side in range(2):
            tasks.append((0.24 + 0.16 * at + 0.07 * side, mix_task, 2 * at + side))
    for step in range(steps + 1):
        tasks.append((0.87 + 0.12 * step / steps, gain_step, step))
    tasks.sort(key=lambda item: item[0])
    for hop in range(1, half + 1):
        if hop == half:
            flip(0, 0)
        else:
            for way in range(2):
                flip(way, (half - hop) * (1 - 2 * way))
        for piece in range(len(pieces)):
            passed = ((hop - 1.5 if hop > 1 else 0.0) + (piece + 1) / len(pieces) * (1 if hop > 1 else 0.5)) / (half - 0.5)
            cols = pl.ds(starts[piece], pieces[piece][2])
            for way in range(2):
                send(hop - 1, way, piece).wait_recv()
                if hop == half:
                    continue

                def with_got(rows):
                    got = ring[hop - 1, way, rows, cols].astype(F32)
                    ring[hop - 1, way, rows, cols] = (term(way, piece, rows) + got).astype(BF16)

                def alone(rows):
                    ring[hop - 1, way, rows, cols] = term(way, piece, rows).astype(BF16)

                if hop == 1:
                    row_loop(way * cut, cut, with_got)
                    row_loop((1 - way) * cut, cut, alone)
                else:
                    row_loop(0, shard, with_got)
                send(hop, way, piece).start()
            if hop == half:

                def finish(rows):
                    total = (
                        term(0, piece, rows)
                        + ring[hop - 1, 0, rows, cols].astype(F32)
                        + ring[hop - 1, 1, rows, cols].astype(F32)
                    )
                    which, at, count = pieces[piece]
                    if which == 0:
                        grad_up[rows, at : at + count] = total
                    else:
                        grad_qkv[which - 1, rows, :] = total

                row_loop(0, shard, finish)
                grad_copy(piece).start()
            while tasks and tasks[0][0] <= passed:
                _, run, value = tasks.pop(0)
                run(value)
    for _, run, value in tasks:
        run(value)
    for piece in range(len(pieces)):
        grad_copy(piece).wait()
    for slot in range(2):
        unit_store(task_base(mixes - 1) + slot * UNIT, slot).wait()
    for step in range(steps):
        gain_copy(step).wait_send()
    for hop in range(half):
        for piece in range(len(pieces)):
            for way in range(2):
                send(hop, way, piece).wait_send()


def back_stage(size, normed, hidden_grad, qkv_low, stats, mix, gains, parts, history, streams, out_total):
    half = size // 2
    tokens, hidden = hidden_grad.shape
    states, _, width = history.shape
    shard = normed.shape[3]
    local = qkv_low.shape[1] // 3
    cols = hidden + 3 * local
    count = (hidden // 512 if half <= 4 else 1) + 3
    blocks = tokens // 128
    steps = size.bit_length() - 1
    vmem = pl.BlockSpec(memory_space=pltpu.VMEM)
    hbm = pl.BlockSpec(memory_space=pl.ANY)
    dma = pltpu.SemaphoreType.DMA
    small = jax.ShapeDtypeStruct((shard, local), F32)
    return pl.pallas_call(
        lambda *refs: back_kernel(size, *refs),
        in_specs=[vmem] * 3 + [hbm] * 7,
        out_specs=[vmem] * 2 + [hbm] * 5,
        out_shape=[
            jax.ShapeDtypeStruct((tokens, mix.shape[1]), F32),
            jax.ShapeDtypeStruct((4, width), F32),
            jax.ShapeDtypeStruct((shard, hidden), F32),
            small,
            small,
            small,
            jax.ShapeDtypeStruct((4, tokens, width), BF16),
        ],
        scratch_shapes=[
            pltpu.VMEM(normed.shape, BF16),
            pltpu.VMEM((tokens, hidden), BF16),
            pltpu.VMEM((tokens, 3 * local), BF16),
            pltpu.VMEM((shard, hidden), F32),
            pltpu.VMEM((3, shard, local), F32),
            pltpu.VMEM((4, 8, width), F32),
            pltpu.VMEM((steps, 4, width), F32),
            pltpu.VMEM((steps, 4, width), F32),
            pltpu.VMEM((4, tokens, width), BF16),
            pltpu.VMEM((blocks, 4, 64, width), BF16),
            pltpu.VMEM((blocks, 4, 64, width), BF16),
            pltpu.VMEM((shard, cols), BF16),
            pltpu.VMEM((half, 2, shard, cols), BF16),
            pltpu.VMEM((2, states, UNIT, width), BF16),
            pltpu.VMEM((2, 4, UNIT, width), F32),
            pltpu.VMEM((2, UNIT, width), F32),
            pltpu.VMEM((2, 4, UNIT, width), BF16),
            pltpu.VMEM((4, GROUP, width), F32),
            pltpu.VMEM((2, 4, shard, tokens), BF16),
            dma((6,)),
            dma((count,)),
            dma((half, 2, count)),
            dma((half, 2, count)),
            dma((blocks,)),
            dma((blocks,)),
            dma((blocks,)),
            dma((blocks,)),
            dma((blocks,)),
            dma((blocks,)),
            dma(()),
            dma((2, 3)),
            dma((2,)),
            dma((steps,)),
            dma((steps,)),
            pltpu.SemaphoreType.REGULAR((blocks,)),
        ],
        cost_estimate=pl.CostEstimate(
            flops=tokens * width * 2000, bytes_accessed=tokens * width * 64, transcendentals=0
        ),
        compiler_params=pltpu.CompilerParams(
            collective_id=1, has_side_effects=True, vmem_limit_bytes=62 * MIB
        ),
        name="back_stage",
    )(stats, mix, gains, normed, hidden_grad, qkv_low, parts, history, streams, out_total)


TILE = 512


def unrotate(values, turn):
    return (
        values * turn[0]
        + pltpu.roll(values, HEAD_DIM - ROT // 2, 1) * turn[1]
        + pltpu.roll(values, ROT // 2, 1) * turn[2]
    )


def row_loop(base, count, run, step=128):
    step = min(step, count)

    @pl.loop(0, count // step)
    def _(at):
        run(pl.ds(pl.multiple_of(base + at * step, step), step))


def attention_probs(query, key, two, first):
    shape = (query.shape[0], key.shape[0])
    middle = key.shape[0] // 2
    scores = dot(query, key, ((1,), (1,))) * (HEAD_DIM ** (-0.5))
    row = first + lax.broadcasted_iota(jnp.int32, shape, 0)
    col = lax.broadcasted_iota(jnp.int32, shape, 1)
    apart = jnp.where(row >= middle, jnp.where(col < middle, two, 0), 0)
    scores = jnp.where(jnp.logical_or(apart != 0, col > row), -1e30, scores)
    weights = jnp.exp(scores - jnp.max(scores, axis=1, keepdims=True))
    return weights / jnp.sum(weights, axis=1, keepdims=True)


def mid_kernel(
    size,
    turn,
    two,
    gen_grad,
    gen_gain,
    gen_mid,
    low_t_in,
    grad_blocks_in,
    hidden_in,
    heads_in,
    low_all,
    up_full,
    qkv_full,
    gen_sum,
    mid_sum,
    grad_out,
    grad_down,
    hidden_grad_out,
    qkv_low_out,
    parts,
    low_t,
    grad_blocks,
    hidden,
    heads,
    low_sum,
    hidden_grad,
    qkv_low,
    attended_grad,
    far,
    ring,
    low_tile,
    up_tile,
    qkv_tile,
    stage,
    gen_sent,
    gen_got,
    mid_sent,
    mid_got,
    value_sum,
    key_sum,
    in_sem,
    out_sem,
    ring_send,
    ring_recv,
    tile_sem,
    stage_sem,
    gen_send,
    gen_recv,
):
    half = size // 2
    rows_all, tokens = low_t.shape
    shard = grad_blocks.shape[2]
    local = heads.shape[1] // 3
    me = lax.axis_index("dp")
    lane = lax.axis_index("tensor")
    place = place_of(me, size)
    right = index_at(place + 1, size)
    left = index_at(place - 1, size)
    steps = size.bit_length() - 1
    partners = [me + (1 << step) * (1 - 2 * lax.rem(lax.div(me, 1 << step), 2)) for step in range(steps)]
    loads = [
        pltpu.make_async_copy(source, target, in_sem.at[at])
        for at, (source, target) in enumerate(
            ((low_t_in, low_t), (grad_blocks_in, grad_blocks), (hidden_in, hidden), (heads_in, heads))
        )
    ]
    for copy in loads:
        copy.start()
    barrier = pltpu.get_barrier_semaphore()
    for there in [right, left] + partners:
        pl.semaphore_signal(barrier, inc=1, device_id=(there, lane), device_id_type=MESH)
    pl.semaphore_wait(barrier, 2 + steps)

    low_tiles = rows_all // TILE
    width_tiles = up_full.shape[0] // TILE
    order = (
        [("low", at) for at in range(low_tiles)]
        + [("up", at) for at in range(width_tiles)]
        + [("qkv", at) for at in range(width_tiles)]
    )

    def load(index):
        kind, at = order[index]
        slot = at % 2
        rows = pl.ds(at * TILE, TILE)
        if kind == "low":
            return pltpu.make_async_copy(low_all.at[:, rows, :], low_tile.at[slot], tile_sem.at[0, slot])
        if kind == "up":
            return pltpu.make_async_copy(up_full.at[rows, :], up_tile.at[slot], tile_sem.at[1, slot])
        return pltpu.make_async_copy(qkv_full.at[rows, :], qkv_tile.at[slot], tile_sem.at[2, slot])

    load(0).start()

    pieces = rows_all // TILE
    cut = TILE // 2

    def term(owner, rows):
        return jnp.dot(low_t[rows, :], grad_blocks[owner], preferred_element_type=F32)

    def send(hop, way, piece):
        if hop == 0:
            rows = pl.ds(piece * TILE + way * cut, cut)
            source = far.at[rows, :]
        else:
            rows = pl.ds(piece * TILE, TILE)
            source = ring.at[hop - 1, way, rows, :]
        return pltpu.make_async_remote_copy(
            src_ref=source,
            dst_ref=ring.at[hop, way, rows, :],
            send_sem=ring_send.at[hop, way, piece],
            recv_sem=ring_recv.at[hop, way, piece],
            device_id=((right, left)[way], lane),
            device_id_type=MESH,
        )

    for copy in loads[:2]:
        copy.wait()
    for piece in range(pieces):

        def far_rows(rows):
            far[rows, :] = term(index_at(place + half, size), rows).astype(BF16)

        row_loop(piece * TILE, TILE, far_rows)
        for way in range(2):
            send(0, way, piece).start()

    for copy in loads[2:]:
        copy.wait()

    def grad_copy(piece):
        base = piece * TILE
        source = low_sum.at[pl.ds(base, TILE), :]
        if base < local:
            target = grad_out.at[pl.ds(base, TILE), :]
        else:
            target = grad_down.at[pl.ds(base - local, TILE), :]
        return pltpu.make_async_copy(source, target, out_sem.at[2 + piece])

    def hidden_copy():
        return pltpu.make_async_copy(hidden_grad, hidden_grad_out, out_sem.at[0])

    def qkv_copy():
        return pltpu.make_async_copy(qkv_low, qkv_low_out, out_sem.at[1])

    def low_grad(at):
        index = at
        load(index + 1).start()
        load(index).wait()
        base = at * TILE

        def run(rows):
            total = None
            for owner in range(size):
                part = dot(grad_blocks[owner, rows, :], low_tile[at % 2, owner], ((1,), (1,)))
                total = part if total is None else total + part
            if base < local:
                attended_grad[rows, base : base + TILE] = total.astype(BF16)
            else:
                cols = slice(base - local, base - local + TILE)
                hidden_grad[rows, cols] = (total * gelu_slope(hidden[rows, cols])).astype(BF16)

        row_loop(0, tokens, run, 256)
        if at + 1 == low_tiles:
            hidden_copy().start()

    def head_grad(head):
        cols = slice(head * HEAD_DIM, (head + 1) * HEAD_DIM)
        key_cols = slice(local + head * HEAD_DIM, local + (head + 1) * HEAD_DIM)
        value_cols = slice(2 * local + head * HEAD_DIM, 2 * local + (head + 1) * HEAD_DIM)
        scale = HEAD_DIM ** (-0.5)
        value_sum[...] = jnp.zeros_like(value_sum)
        key_sum[...] = jnp.zeros_like(key_sum)

        def run(rows):
            query, key, value = heads[rows, cols], heads[:, key_cols], heads[:, value_cols]
            upstream = attended_grad[rows, cols]
            probs = attention_probs(query, key, two[...], rows.start)
            probs_grad = dot(upstream, value, ((1,), (1,)))
            value_sum[...] += dot(probs.astype(BF16), upstream, ((0,), (0,)))
            row = jnp.sum(probs * probs_grad, axis=1, keepdims=True)
            scores_grad = (probs * (probs_grad - row)).astype(BF16)
            query_grad = dot(scores_grad, key, ((1,), (0,))) * scale
            turns = [turn[which, rows, :] for which in range(3)]
            qkv_low[rows, cols] = unrotate(query_grad, turns).astype(BF16)
            key_sum[...] += dot(scores_grad, query, ((0,), (0,)))

        row_loop(0, tokens, run)
        turns = [turn[which] for which in range(3)]
        qkv_low[:, value_cols] = value_sum[...].astype(BF16)
        qkv_low[:, key_cols] = unrotate(key_sum[...] * scale, turns).astype(BF16)
        if (head + 1) * HEAD_DIM == local:
            qkv_copy().start()

    def part_store(stream, at):
        return pltpu.make_async_copy(
            stage.at[stream], parts.at[stream, :, pl.ds(at * TILE, TILE)], stage_sem.at[stream]
        )

    def up_part(at):
        index = low_tiles + at
        load(index + 1).start()
        load(index).wait()
        if at:
            part_store(3, at - 1).wait()

        def run(rows):
            stage[3, rows, :] = dot(hidden_grad[rows, :], up_tile[at % 2], ((1,), (1,))).astype(BF16)

        row_loop(0, tokens, run, 256)
        part_store(3, at).start()

    def qkv_part(at):
        index = low_tiles + width_tiles + at
        if index + 1 < len(order):
            load(index + 1).start()
        load(index).wait()
        for stream in range(3):
            if at:
                part_store(stream, at - 1).wait()

        def run(rows):
            for stream in range(3):
                cols = slice(stream * local, (stream + 1) * local)
                stage[stream, rows, :] = dot(
                    qkv_low[rows, cols], qkv_tile[at % 2, :, cols], ((1,), (1,))
                ).astype(BF16)

        row_loop(0, tokens, run, 256)
        for stream in range(3):
            part_store(stream, at).start()

    def gen_copies(step):
        return [
            pltpu.make_async_remote_copy(
                src_ref=sent.at[step],
                dst_ref=got.at[step],
                send_sem=gen_send.at[step, which],
                recv_sem=gen_recv.at[step, which],
                device_id=(partners[step], lane),
                device_id_type=MESH,
            )
            for which, (sent, got) in enumerate(((gen_sent, gen_got), (mid_sent, mid_got)))
        ]

    def gen_step(step):
        if step == 0:
            units = gen_grad.shape[0]
            gen_sent[0, :units, :] = gen_grad[...].astype(BF16)
            gen_sent[0, units:, :] = jnp.broadcast_to(
                gen_gain[...].astype(BF16), (gen_sent.shape[1] - units, gen_sent.shape[2])
            )
            mid_sent[0] = gen_mid[...]
        else:
            for copy in gen_copies(step - 1):
                copy.wait_recv()
            total = gen_sent[step - 1].astype(F32) + gen_got[step - 1].astype(F32)
            mid_total = mid_sent[step - 1] + mid_got[step - 1]
            if step == steps:
                gen_sum[...] = total
                mid_sum[...] = mid_total
            else:
                gen_sent[step] = total.astype(BF16)
                mid_sent[step] = mid_total
        if step < steps:
            for copy in gen_copies(step):
                copy.start()

    tasks = [(low_grad, at) for at in range(low_tiles)]
    tasks += [(head_grad, head) for head in range(local // HEAD_DIM)]
    tasks += [(up_part, at) for at in range(width_tiles)]
    tasks += [(qkv_part, at) for at in range(width_tiles)]
    for step in range(steps + 1):
        tasks.insert(2 + 5 * step if steps < 4 else 2 + 3 * step, (gen_step, step))
    count = len(tasks)
    slots = half * pieces
    slot = 0
    for hop in range(1, half + 1):
        for piece in range(pieces):
            for way in range(2):
                send(hop - 1, way, piece).wait_recv()
                if hop == half:
                    continue
                owner = index_at(place + (half - hop) * (1 - 2 * way), size)

                def with_got(rows):
                    got = ring[hop - 1, way, rows, :].astype(F32)
                    ring[hop - 1, way, rows, :] = (term(owner, rows) + got).astype(BF16)

                def alone(rows):
                    ring[hop - 1, way, rows, :] = term(owner, rows).astype(BF16)

                if hop == 1:
                    row_loop(piece * TILE + way * cut, cut, with_got)
                    row_loop(piece * TILE + (1 - way) * cut, cut, alone)
                else:
                    row_loop(piece * TILE, TILE, with_got)
                send(hop, way, piece).start()
            if hop == half:

                def finish(rows):
                    low_sum[rows, :] = (
                        term(me, rows)
                        + ring[hop - 1, 0, rows, :].astype(F32)
                        + ring[hop - 1, 1, rows, :].astype(F32)
                    )

                row_loop(piece * TILE, TILE, finish)
                grad_copy(piece).start()
            slot += 1
            while tasks and (slot == slots or len(tasks) * (slots - 2) > count * max(slots - 2 - slot, 0)):
                run, value = tasks.pop(0)
                run(value)
    for stream in range(4):
        part_store(stream, width_tiles - 1).wait()
    hidden_copy().wait()
    qkv_copy().wait()
    for piece in range(pieces):
        grad_copy(piece).wait()
    for step in range(steps):
        for copy in gen_copies(step):
            copy.wait_send()
    for hop in range(half):
        for piece in range(pieces):
            for way in range(2):
                send(hop, way, piece).wait_send()


def mid_stage(
    size,
    low_t,
    grad_blocks,
    hidden,
    heads,
    turn,
    two,
    gen_grad,
    gen_gain,
    gen_mid,
    low_all,
    up_full,
    qkv_full,
):
    half = size // 2
    rows_all, tokens = low_t.shape
    shard = grad_blocks.shape[2]
    hidden_cols = hidden.shape[1]
    local = heads.shape[1] // 3
    width = up_full.shape[0]
    pieces = rows_all // TILE
    steps = size.bit_length() - 1
    units = gen_grad.shape[0]
    vmem = pl.BlockSpec(memory_space=pltpu.VMEM)
    hbm = pl.BlockSpec(memory_space=pl.ANY)
    dma = pltpu.SemaphoreType.DMA
    return pl.pallas_call(
        lambda *refs: mid_kernel(size, *refs),
        in_specs=[vmem] * 5 + [hbm] * 7,
        out_specs=[vmem] * 2 + [hbm] * 5,
        out_shape=[
            jax.ShapeDtypeStruct((units + 8, width), F32),
            jax.ShapeDtypeStruct(gen_mid.shape, F32),
            jax.ShapeDtypeStruct((local, shard), F32),
            jax.ShapeDtypeStruct((hidden_cols, shard), F32),
            jax.ShapeDtypeStruct((tokens, hidden_cols), BF16),
            jax.ShapeDtypeStruct((tokens, 3 * local), BF16),
            jax.ShapeDtypeStruct((4, tokens, width), BF16),
        ],
        scratch_shapes=[
            pltpu.VMEM((rows_all, tokens), BF16),
            pltpu.VMEM((size, tokens, shard), BF16),
            pltpu.VMEM((tokens, hidden_cols), F32),
            pltpu.VMEM((tokens, 3 * local), BF16),
            pltpu.VMEM((rows_all, shard), F32),
            pltpu.VMEM((tokens, hidden_cols), BF16),
            pltpu.VMEM((tokens, 3 * local), BF16),
            pltpu.VMEM((tokens, local), BF16),
            pltpu.VMEM((rows_all, shard), BF16),
            pltpu.VMEM((half, 2, rows_all, shard), BF16),
            pltpu.VMEM((2, size, TILE, shard), BF16),
            pltpu.VMEM((2, TILE, hidden_cols), BF16),
            pltpu.VMEM((2, TILE, 3 * local), BF16),
            pltpu.VMEM((4, tokens, TILE), BF16),
            pltpu.VMEM((steps, units + 8, width), BF16),
            pltpu.VMEM((steps, units + 8, width), BF16),
            pltpu.VMEM((steps,) + gen_mid.shape, F32),
            pltpu.VMEM((steps,) + gen_mid.shape, F32),
            pltpu.VMEM((tokens, HEAD_DIM), F32),
            pltpu.VMEM((tokens, HEAD_DIM), F32),
            dma((4,)),
            dma((2 + pieces,)),
            dma((half, 2, pieces)),
            dma((half, 2, pieces)),
            dma((3, 2)),
            dma((4,)),
            dma((steps, 2)),
            dma((steps, 2)),
        ],
        cost_estimate=pl.CostEstimate(
            flops=tokens * width * 4000, bytes_accessed=tokens * width * 40, transcendentals=0
        ),
        compiler_params=pltpu.CompilerParams(
            collective_id=2, has_side_effects=True, vmem_limit_bytes=62 * MIB
        ),
        name="mid_stage",
    )(
        turn,
        two,
        gen_grad,
        gen_gain,
        gen_mid,
        low_t,
        grad_blocks,
        hidden,
        heads,
        low_all,
        up_full,
        qkv_full,
    )


def front_kernel(
    size,
    mix_in,
    gains,
    segments,
    frequency,
    history,
    w_query,
    w_key,
    w_value,
    w_up,
    w_out,
    w_down,
    stats,
    branch,
    mix,
    turn,
    two,
    heads_out,
    hidden_out,
    low_t_out,
    normed_out,
    streams,
    qkv_all,
    up_all,
    low_all,
    heads,
    hidden,
    low_t,
    normed,
    low,
    weight_tile,
    low_tile,
    state_in,
    stream_out,
    from_core,
    from_link,
    qkv_send,
    qkv_recv,
    up_send,
    up_recv,
    low_send,
    low_recv,
    own_sem,
    state_sem,
    stream_sem,
    normed_sem,
    out_sem,
    weight_sem,
    tile_sem,
    core_send,
    core_recv,
    link_send,
    link_recv,
    twin_send,
    twin_recv,
    freed,
):
    half = size // 2
    states, tokens, width = history.shape
    shard = width // size
    local = w_query.shape[1]
    hidden_cols = w_up.shape[1]
    inverse = 1.0 / width
    me = lax.axis_index("dp")
    lane = lax.axis_index("tensor")
    place = place_of(me, size)
    right = index_at(place + 1, size)
    left = index_at(place - 1, size)
    core = lax.rem(lane, 2)
    chip = lax.div(lane, 2)
    twin = chip * 2 + 1 - core
    across = (1 - chip) * 2 + core
    rows_half = tokens // 2

    barrier = pltpu.get_barrier_semaphore()
    for there in ((right, lane), (left, lane), (me, twin), (me, across)):
        pl.semaphore_signal(barrier, inc=1, device_id=there, device_id_type=MESH)
    pl.semaphore_wait(barrier, 4)

    wide = TILE
    groups = [
        [(w_query, 0, 0), (w_key, 0, local), (w_value, 0, 2 * local)],
        [(w_up, at, at) for at in range(0, hidden_cols, wide)],
        [(w_out, at, at) for at in range(0, local, wide)]
        + [(w_down, at, local + at) for at in range(0, hidden_cols, wide)],
    ]
    sems = [(qkv_send, qkv_recv), (up_send, up_recv), (low_send, low_recv)]
    cut = (shard // 2, shard // 2, wide // 2)

    def own(group, piece, lo, count):
        source, at, _ = groups[group][piece]
        if group == 2:
            return source.at[pl.ds(at + lo, count), :]
        cols = local if group == 0 else wide
        return source.at[pl.ds(lo, count), pl.ds(at, cols)]

    def held(group, piece, owner, lo, count):
        _, _, at = groups[group][piece]
        if group == 2:
            return low_all.at[owner, pl.ds(at + lo, count), :]
        rows = pl.ds(pl.multiple_of(owner * shard + lo, cut[0]), count)
        if group == 0:
            return qkv_all.at[rows, pl.ds(at, local)]
        return up_all.at[rows, pl.ds(at, wide)]

    def send(group, hop, way, piece):
        owner = index_at(place + (hop - 1) * (2 * way - 1), size)
        whole = shard if group < 2 else wide
        lo, count = (0, whole) if hop < half else (way * cut[group], cut[group])
        target = held(group, piece, owner, lo, count)
        source = own(group, piece, lo, count) if hop == 1 else target
        send_sem, recv_sem = sems[group]
        return pltpu.make_async_remote_copy(
            src_ref=source,
            dst_ref=target,
            send_sem=send_sem.at[hop - 1, way, piece],
            recv_sem=recv_sem.at[hop - 1, way, piece],
            device_id=((right, left)[way], lane),
            device_id_type=MESH,
        )

    def own_copies(group):
        whole = shard if group < 2 else wide
        return [
            pltpu.make_async_copy(
                own(group, piece, 0, whole), held(group, piece, me, 0, whole), own_sem.at[group, piece]
            )
            for piece in range(len(groups[group]))
        ]

    units = tokens // UNIT

    def state_load(unit):
        rows = pl.ds(pl.multiple_of(unit * UNIT, UNIT), UNIT)
        slot = lax.rem(unit, 2)
        return pltpu.make_async_copy(history.at[:, rows, :], state_in.at[slot], state_sem.at[slot])

    def stream_store(unit):
        rows = pl.ds(pl.multiple_of(unit * UNIT, UNIT), UNIT)
        slot = lax.rem(unit, 2)
        return pltpu.make_async_copy(stream_out.at[slot], streams.at[:, rows, :], stream_sem.at[slot])

    per_task = 2

    def tables():
        count = mix_in.shape[0]
        padded = -(-count // 8) * 8
        mix[...] = jnp.concatenate(
            [mix_in[...], jnp.zeros((padded - count, tokens), F32)], axis=0
        ).T
        two[...] = jnp.broadcast_to(segments[0:1, tokens - 1 : tokens], (1, tokens))
        row = lax.broadcasted_iota(jnp.int32, (tokens, HEAD_DIM), 0)
        lanes = lax.broadcasted_iota(jnp.int32, (tokens, HEAD_DIM), 1)
        flag = jnp.broadcast_to(segments[0:1, tokens - 1 : tokens], (tokens, HEAD_DIM))
        place_in = row - jnp.where(row >= tokens // 2, jnp.where(flag != 0, tokens // 2, 0), 0)
        angles = place_in.astype(F32) * frequency[...]
        sine = jnp.sin(angles)
        turn[0] = jnp.cos(angles)
        turn[1] = jnp.where(lanes < ROT // 2, sine, 0.0)
        turn[2] = jnp.where(lanes < ROT // 2, 0.0, -sine)

    def out_copies():
        return [
            pltpu.make_async_copy(source, target, out_sem.at[at])
            for at, (source, target) in enumerate(
                ((heads, heads_out), (hidden, hidden_out), (low_t, low_t_out))
            )
        ]

    def mix_task(task):
        @pl.loop(0, per_task)
        def _(which):
            mix_unit(task * per_task + which, task)

        if (task + 1) * per_task == units:
            normed_store().start()

    def mix_unit(unit, task):
        slot = lax.rem(unit, 2)

        @pl.when(unit + 1 < units)
        def _():
            state_load(unit + 1).start()

        state_load(unit).wait()
        if task > 0:
            stream_store(unit - 2).wait()

        @pl.loop(0, UNIT // GROUP)
        def _(step):
            rows = pl.ds(pl.multiple_of(unit * UNIT + step * GROUP, GROUP), GROUP)
            inner = pl.ds(pl.multiple_of(step * GROUP, GROUP), GROUP)
            weights = mix[rows, :]

            sums = [jnp.zeros((GROUP, 128), F32) for _ in range(4)]
            for at in range(0, width, CHUNK):
                cols = pl.ds(at, CHUNK)
                total = [None] * 4
                for source in range(states):
                    state = state_in[slot, source, inner, cols].astype(F32)
                    for stream in range(4):
                        k = stream * states + source
                        term = weights[:, k : k + 1] * state
                        total[stream] = term if source == 0 else total[stream] + term
                for stream in range(4):
                    stream_out[slot, stream, inner, cols] = total[stream]
                    for at_lane in range(0, CHUNK, 128):
                        sums[stream] = sums[stream] + total[stream][:, at_lane : at_lane + 128]
            for stream in range(4):
                mean = jnp.sum(sums[stream], axis=1, keepdims=True) * inverse
                square = jnp.zeros((GROUP, 128), F32)
                for at in range(0, width, CHUNK):
                    center = stream_out[slot, stream, inner, pl.ds(at, CHUNK)] - mean
                    center = center * center
                    for at_lane in range(0, CHUNK, 128):
                        square = square + center[:, at_lane : at_lane + 128]
                scale = lax.rsqrt(jnp.sum(square, axis=1, keepdims=True) * inverse + EPSILON)
                stats[rows, stream : stream + 1] = mean
                stats[rows, 4 + stream : 5 + stream] = scale
                for at in range(0, width, CHUNK):
                    cols = pl.ds(at, CHUNK)
                    center = stream_out[slot, stream, inner, cols] - mean
                    value = (center * scale * gains[stream : stream + 1, cols]).astype(BF16)
                    for owner in range(at // shard, (at + CHUNK) // shard):
                        base = owner * shard - at
                        normed[stream, owner, rows, :] = value[:, base : base + shard]

        stream_store(unit).start()

    def normed_store():
        return pltpu.make_async_copy(normed, normed_out, normed_sem)

    tiles = 3 + hidden_cols // wide

    def weight_load(tile):
        if tile < 3:
            source = qkv_all.at[:, pl.ds(tile * local, local)]
        else:
            source = up_all.at[:, pl.ds((tile - 3) * wide, wide)]
        return pltpu.make_async_copy(source, weight_tile.at[tile % 2], weight_sem.at[tile % 2])

    def arrived(group):
        for copy in own_copies(group):
            copy.wait()
        for piece in range(len(groups[group])):
            for way in range(2):
                send(group, half, way, piece).wait_recv()

    def tile_product(tile, stream, rows):
        total = None
        for owner in range(size):
            part = jnp.dot(
                normed[stream, owner, rows, :],
                weight_tile[tile % 2, owner * shard : (owner + 1) * shard, :],
                preferred_element_type=F32,
            )
            total = part if total is None else total + part
        return total

    def qkv_task(which):
        if which == 0:
            arrived(0)
            weight_load(0).start()
        if which < 2:
            weight_load(which + 1).start()
        weight_load(which).wait()

        def run(rows):
            product = tile_product(which, which, rows)
            for head in range(local // HEAD_DIM):
                at = head * HEAD_DIM
                part = product[:, at : at + HEAD_DIM]
                if which < 2:
                    part = (
                        part * turn[0, rows, :]
                        - pltpu.roll(part, HEAD_DIM - ROT // 2, 1) * turn[1, rows, :]
                        - pltpu.roll(part, ROT // 2, 1) * turn[2, rows, :]
                    )
                heads[rows, which * local + at : which * local + at + HEAD_DIM] = part.astype(BF16)

        row_loop(0, tokens, run)

    def head_task(head):
        at = head * HEAD_DIM

        def run(rows):
            query = heads[rows, at : at + HEAD_DIM]
            key = heads[:, local + at : local + at + HEAD_DIM]
            value = heads[:, 2 * local + at : 2 * local + at + HEAD_DIM]
            probs = attention_probs(query, key, two[...], rows.start).astype(BF16)
            attended = jnp.dot(probs, value, preferred_element_type=F32)
            low[rows, at : at + HEAD_DIM] = attended.astype(BF16)
            low_t[at : at + HEAD_DIM, rows] = attended.T.astype(BF16)

        row_loop(0, tokens, run)

    def up_task(at):
        if at == 0:
            arrived(1)
            weight_load(3).start()
        if at + 1 < tiles - 3:
            weight_load(4 + at).start()
        weight_load(3 + at).wait()
        cols = slice(at * wide, (at + 1) * wide)
        low_cols = slice(local + at * wide, local + (at + 1) * wide)

        def run(rows):
            product = tile_product(3 + at, 3, rows)
            hidden[rows, cols] = product
            active = gelu(product)
            low[rows, low_cols] = active.astype(BF16)
            low_t[low_cols, rows] = active.T.astype(BF16)

        row_loop(0, tokens, run)
        if at + 1 == tiles - 3:
            for copy in out_copies():
                copy.start()

    distances = [0]
    for hop in range(1, half):
        distances += [-hop, hop]
    distances += [half]

    def tile_load(index):
        owner = index_at(place + distances[index], size)
        return pltpu.make_async_copy(low_all.at[owner], low_tile.at[index % 2], tile_sem.at[index % 2])

    def mine(index):
        return pl.ds(pl.multiple_of(core * rows_half, rows_half), rows_half)

    def core_copy(index):
        owner = index_at(place + distances[index], size)
        rows = pl.ds(pl.multiple_of((1 - core) * rows_half, rows_half), rows_half)
        return pltpu.make_async_remote_copy(
            src_ref=branch.at[owner, rows, :],
            dst_ref=from_core.at[index],
            send_sem=core_send.at[index],
            recv_sem=core_recv.at[index],
            device_id=(me, twin),
            device_id_type=MESH,
        )

    def link_copy(index):
        owner = index_at(place + distances[index], size)
        return pltpu.make_async_remote_copy(
            src_ref=branch.at[owner, mine(index), :],
            dst_ref=from_link.at[index],
            send_sem=link_send.at[index],
            recv_sem=link_recv.at[index],
            device_id=(me, across),
            device_id_type=MESH,
        )

    def twin_copy(index):
        owner = index_at(place + distances[index], size)
        return pltpu.make_async_remote_copy(
            src_ref=branch.at[owner, mine(index), :],
            dst_ref=branch.at[owner, mine(index), :],
            send_sem=twin_send.at[index],
            recv_sem=twin_recv.at[index],
            device_id=(me, twin),
            device_id_type=MESH,
        )

    def low_task(index):
        if index == 0:
            for copy in own_copies(2):
                copy.wait()
        owner = index_at(place + distances[index], size)
        load = tile_load(index)
        load.start()
        load.wait()

        def run(rows):
            branch[owner, rows, :] = jnp.dot(
                low[rows, :], low_tile[index % 2], preferred_element_type=F32
            ).astype(BF16)

        row_loop(0, tokens, run)
        core_copy(index).start()

    def add_into(index, other):
        owner = index_at(place + distances[index], size)
        rows = mine(index)
        branch[owner, rows, :] = (
            branch[owner, rows, :].astype(F32) + other[index].astype(F32)
        ).astype(BF16)

    def link_task(index):
        copy = core_copy(index)
        copy.wait_send()
        pl.semaphore_signal(freed.at[index], inc=1, device_id=(me, twin), device_id_type=MESH)
        copy.wait_recv()
        add_into(index, from_core)
        link_copy(index).start()

    def twin_task(index):
        copy = link_copy(index)
        copy.wait_send()
        copy.wait_recv()
        add_into(index, from_link)
        pl.semaphore_wait(freed.at[index], 1)
        twin_copy(index).start()

    state_load(0).start()
    slots = [(group, hop) for group in range(3) for hop in range(1, half + 1)]
    counts = [len(pieces) for pieces in groups]
    first = [0, counts[0] * half, (counts[0] + counts[1]) * half]
    total_slots = sum(counts) * half
    tasks = []
    mixes = units // per_task
    for task in range(mixes):
        tasks.append((counts[0] - 1 + task * (first[1] - counts[0]) / mixes, mix_task, task))
    early = first[1] + counts[1]
    for which in range(3):
        tasks.append((early + which, qkv_task, which))
    for head in range(local // HEAD_DIM):
        tasks.append((early + 3 + head, head_task, head))
    middle = first[2] + counts[2]
    for at in range(tiles - 3):
        tasks.append((middle + at, up_task, at))
    for index in range(len(distances) - 1):
        due = max(first[2] + counts[2] * (abs(distances[index]) + 1) - 1, middle + tiles - 3) + 0.5 * (index % 2)
        tasks.append((due, low_task, index))
        tasks.append((due + 1, link_task, index))
        tasks.append((due + 3, twin_task, index))
    tasks.sort(key=lambda item: item[0])

    at_slot = 0
    for group, hop in slots:
        if hop == 1:
            for copy in own_copies(group):
                copy.start()
        for piece in range(counts[group]):
            for way in range(2):
                if hop > 1:
                    send(group, hop - 1, way, piece).wait_recv()
                send(group, hop, way, piece).start()
            if at_slot == 0:
                tables()
            while tasks and tasks[0][0] <= at_slot and at_slot < total_slots - 1:
                _, run, value = tasks.pop(0)
                run(value)
            at_slot += 1
    for _, run, value in tasks:
        run(value)
    for piece in range(counts[2]):
        for way in range(2):
            send(2, half, way, piece).wait_recv()
    last = len(distances) - 1
    low_task(last)
    link_task(last)
    twin_task(last)
    for index in range(len(distances)):
        copy = twin_copy(index)
        copy.wait_send()
        copy.wait_recv()
    for unit in range(units - 2, units):
        stream_store(unit).wait()
    normed_store().wait()
    for copy in out_copies():
        copy.wait()
    for group, hop in slots:
        for piece in range(counts[group]):
            for way in range(2):
                send(group, hop, way, piece).wait_send()


def front_stage(size, mix, gains, segments, frequency, history, w_query, w_key, w_value, w_up, w_out, w_down):
    half = size // 2
    states, tokens, width = history.shape
    shard = width // size
    local = w_query.shape[1]
    hidden_cols = w_up.shape[1]
    rows_all = local + hidden_cols
    vmem = pl.BlockSpec(memory_space=pltpu.VMEM)
    hbm = pl.BlockSpec(memory_space=pl.ANY)
    dma = pltpu.SemaphoreType.DMA
    up_pieces = hidden_cols // TILE
    low_pieces = rows_all // TILE
    return pl.pallas_call(
        lambda *refs: front_kernel(size, *refs),
        in_specs=[vmem] * 4 + [hbm] * 7,
        out_specs=[vmem] * 5 + [hbm] * 8,
        out_shape=[
            jax.ShapeDtypeStruct((tokens, 8), F32),
            jax.ShapeDtypeStruct((size, tokens, shard), BF16),
            jax.ShapeDtypeStruct((tokens, -(-mix.shape[0] // 8) * 8), F32),
            jax.ShapeDtypeStruct((3, tokens, HEAD_DIM), F32),
            jax.ShapeDtypeStruct((1, tokens), jnp.int32),
            jax.ShapeDtypeStruct((tokens, 3 * local), BF16),
            jax.ShapeDtypeStruct((tokens, hidden_cols), F32),
            jax.ShapeDtypeStruct((rows_all, tokens), BF16),
            jax.ShapeDtypeStruct((4, size, tokens, shard), BF16),
            jax.ShapeDtypeStruct((4, tokens, width), F32),
            jax.ShapeDtypeStruct((width, 3 * local), BF16),
            jax.ShapeDtypeStruct((width, hidden_cols), BF16),
            jax.ShapeDtypeStruct((size, rows_all, shard), BF16),
        ],
        scratch_shapes=[
            pltpu.VMEM((tokens, 3 * local), BF16),
            pltpu.VMEM((tokens, hidden_cols), F32),
            pltpu.VMEM((rows_all, tokens), BF16),
            pltpu.VMEM((4, size, tokens, shard), BF16),
            pltpu.VMEM((tokens, rows_all), BF16),
            pltpu.VMEM((2, width, TILE), BF16),
            pltpu.VMEM((2, rows_all, shard), BF16),
            pltpu.VMEM((2, states, UNIT, width), BF16),
            pltpu.VMEM((2, 4, UNIT, width), F32),
            pltpu.VMEM((size, tokens // 2, shard), BF16),
            pltpu.VMEM((size, tokens // 2, shard), BF16),
            dma((half, 2, 3)),
            dma((half, 2, 3)),
            dma((half, 2, up_pieces)),
            dma((half, 2, up_pieces)),
            dma((half, 2, low_pieces)),
            dma((half, 2, low_pieces)),
            dma((3, low_pieces)),
            dma((2,)),
            dma((2,)),
            dma(()),
            dma((3,)),
            dma((2,)),
            dma((2,)),
            dma((size,)),
            dma((size,)),
            dma((size,)),
            dma((size,)),
            dma((size,)),
            dma((size,)),
            pltpu.SemaphoreType.REGULAR((size,)),
        ],
        cost_estimate=pl.CostEstimate(
            flops=tokens * width * 8000, bytes_accessed=tokens * width * 80, transcendentals=0
        ),
        compiler_params=pltpu.CompilerParams(
            collective_id=3, has_side_effects=True, vmem_limit_bytes=62 * MIB
        ),
        name="front_stage",
    )(mix, gains, segments, frequency, history, w_query, w_key, w_value, w_up, w_out, w_down)


def finish_kernel(count, mix, grads, mix_grad, gain_sum, gen_gain, *refs):
    sources = refs[:count]
    history_grad, mix_out, gain_out = refs[count : count + 3]
    targets = refs[count + 3 : 2 * count + 3]
    spread = refs[2 * count + 3]
    states, tokens, width = history_grad.shape
    step = pl.program_id(0)
    for source, target in zip(sources, targets):
        target[...] = source[...]

    @pl.when(step == 0)
    def _():
        gain_out[:4, :] = gain_sum[...]
        gain_out[4:5, :] = gen_gain[0:1, :]
        mix_out[...] = mix_grad[...].T[: mix_out.shape[0], :]

    own = lax.broadcasted_iota(jnp.int32, (tokens, tokens), 0) == lax.broadcasted_iota(
        jnp.int32, (tokens, tokens), 1
    )
    weights = mix[...]
    for source in range(states):
        parts = [
            jnp.where(own, weights[:, stream * states + source : stream * states + source + 1], 0.0)
            for stream in range(4)
        ]
        spread[source * tokens : (source + 1) * tokens, :] = jnp.concatenate(parts, axis=1).astype(BF16)

    @pl.loop(0, width // 512)
    def _(at):
        cols = pl.ds(pl.multiple_of(at * 512, 512), 512)
        grad = jnp.concatenate([grads[stream, :, cols] for stream in range(4)], axis=0)
        mixed = jnp.dot(spread[...], grad, preferred_element_type=F32)
        for source in range(states):
            history_grad[source, :, cols] = mixed[source * tokens : (source + 1) * tokens].astype(BF16)


def finish_stage(states, mixes, mix, grads, mix_grad, gain_sum, gen_sum, sources, block=64):
    _, tokens, width = grads.shape
    steps = tokens // block
    row = lambda i: (i, 0)
    passed = [pl.BlockSpec((source.shape[0] // steps, source.shape[1]), row) for source in sources]
    fixed = lambda i: (0, 0)
    units = gen_sum.shape[0] - 8
    return pl.pallas_call(
        lambda *refs: finish_kernel(len(sources), *refs),
        grid=(steps,),
        in_specs=[
            pl.BlockSpec((block, mix.shape[1]), lambda i: (i, 0)),
            pl.BlockSpec((4, block, width), lambda i: (0, i, 0)),
            pl.BlockSpec(mix_grad.shape, fixed),
            pl.BlockSpec(gain_sum.shape, fixed),
            pl.BlockSpec((8, width), lambda i: (units // 8, 0)),
        ]
        + passed,
        out_specs=[
            pl.BlockSpec((states, block, width), lambda i: (0, i, 0)),
            pl.BlockSpec((mixes, tokens), fixed),
            pl.BlockSpec((5, width), fixed),
        ]
        + passed,
        out_shape=[
            jax.ShapeDtypeStruct((states, tokens, width), BF16),
            jax.ShapeDtypeStruct((mixes, tokens), F32),
            jax.ShapeDtypeStruct((5, width), F32),
        ]
        + [jax.ShapeDtypeStruct(source.shape, source.dtype) for source in sources],
        scratch_shapes=[
            pltpu.VMEM((states * block, 4 * block), BF16),
        ],
        cost_estimate=pl.CostEstimate(
            flops=tokens * width * 72, bytes_accessed=tokens * width * 26, transcendentals=0
        ),
        compiler_params=pltpu.CompilerParams(vmem_limit_bytes=62 * MIB),
        name="finish_stage",
    )(mix, grads, mix_grad, gain_sum, gen_sum, *sources)


def body(
    sizes,
    history,
    mix_weights,
    segments,
    norm_gains,
    w_query,
    w_key,
    w_value,
    w_out,
    w_up,
    w_down,
    gen_in,
    gen_out,
    out_grad,
    next_grad,
):
    dp_size, tensor_size = sizes
    places = np.arange(HEAD_DIM)
    frequency = np.where(
        places < ROT, np.float32(ROPE_BASE) ** (-2.0 * (places % (ROT // 2)).astype(np.float32) / ROT), 0.0
    ).astype(np.float32)
    stats, branch, mix_rows, turn, two, heads, hidden, low_t, normed, streams, full_qkv, full_up, low_all = front_stage(
        dp_size,
        mix_weights,
        norm_gains,
        segments[None, :],
        jnp.asarray(frequency)[None, :],
        history,
        w_query,
        w_key,
        w_value,
        w_up,
        w_out,
        w_down,
    )
    layer_out, next_mix, out_total, branch_grad, gain_gen_grad, grad_gen_in, grad_gen_out = gen_stage(
        dp_size, streams, branch, norm_gains, gen_in.T, gen_out, out_grad, next_grad
    )

    gen_units, gen_next = gen_out.shape
    gen_sum, mid_sum, grad_out, grad_down, hidden_grad, qkv_low, parts = mid_stage(
        dp_size,
        low_t,
        branch_grad,
        hidden,
        heads,
        turn,
        two,
        grad_gen_in,
        gain_gen_grad,
        grad_gen_out,
        low_all,
        full_up,
        full_qkv,
    )
    mix_grad, gain_sums, grad_up, grad_query, grad_key, grad_value, stream_grad = back_stage(
        dp_size,
        normed,
        hidden_grad,
        qkv_low,
        stats,
        mix_rows,
        norm_gains,
        parts,
        history,
        streams,
        out_total,
    )
    history_grad, mix_grad, grad_gains, grad_up, grad_query, grad_key, grad_value, grad_out, grad_down = finish_stage(
        history.shape[0],
        mix_weights.shape[0],
        mix_rows,
        stream_grad,
        mix_grad,
        gain_sums,
        gen_sum,
        (grad_up, grad_query, grad_key, grad_value, grad_out, grad_down),
    )
    return (
        layer_out,
        next_mix,
        history_grad,
        mix_grad,
        grad_gains,
        grad_query,
        grad_key,
        grad_value,
        grad_out,
        grad_up,
        grad_down,
        gen_sum[:gen_units].T,
        mid_sum[:, :gen_next],
    )


def solution(mesh):
    sizes = (mesh.shape["dp"], mesh.shape["tensor"])
    in_specs = (
        P(None, "dp", None),
        P(None, "dp"),
        P("dp"),
        P(),
        P("dp", "tensor"),
        P("dp", "tensor"),
        P("dp", "tensor"),
        P("tensor", "dp"),
        P("dp", "tensor"),
        P("tensor", "dp"),
        P(),
        P(),
        P("dp", None),
        P(None, "dp"),
    )
    out_specs = (
        P("dp", None),
        P(None, "dp"),
        P(None, "dp", None),
        P(None, "dp"),
        P(),
        P("dp", "tensor"),
        P("dp", "tensor"),
        P("dp", "tensor"),
        P("tensor", "dp"),
        P("dp", "tensor"),
        P("tensor", "dp"),
        P(),
        P(),
    )

    def step(*arrays):
        return body(sizes, *arrays)

    return jax.shard_map(step, mesh=mesh, in_specs=in_specs, out_specs=out_specs, check_vma=False)
```

```python
import jax
import jax.numpy as jnp
import numpy as np
from jax import lax
from jax.experimental import pallas as pl
from jax.experimental.pallas import tpu as pltpu
from jax.sharding import PartitionSpec as P

HEAD_DIM = 128
ROT = 32


EPSILON = 1e-05
ROPE_BASE = 10000.0

F32 = jnp.float32
BF16 = jnp.bfloat16


MIB = 1 << 20
GROUP = 16
CHUNK = 512


def gelu(x):
    return 0.5 * x * (1.0 + lax.erf(x * (0.5**0.5)))


def gelu_slope(x):
    return 0.5 * (1.0 + lax.erf(x * (0.5**0.5))) + x * jnp.exp(-0.5 * x * x) * 0.3989422804014327


def dot(a, b, dims):
    return lax.dot_general(a, b, (dims, ((), ())), preferred_element_type=F32)


def gen_kernel(stream, branch, gain, gen_in, gen_out, out_grad, next_grad, layer_out, next_mix, out_total, branch_grad, gain_grad, in_grad, mid_grad):
    first = pl.program_id(0) == 0
    x = stream[0] + jnp.concatenate([branch[owner] for owner in range(branch.shape[0])], axis=1).astype(F32)
    layer_out[...] = x.astype(BF16)
    center = x - jnp.mean(x, axis=1, keepdims=True)
    scale = lax.rsqrt(jnp.mean(center * center, axis=1, keepdims=True) + EPSILON)
    unit = center * scale
    gains = gain[4:5, :]
    low = (unit * gains).astype(BF16)
    hidden = dot(low, gen_in[...], ((1,), (1,)))
    active = gelu(hidden).astype(BF16)
    next_mix[...] = dot(active, gen_out[...], ((1,), (0,))).T
    upstream = next_grad[...].T.astype(BF16)
    active_grad = dot(upstream, gen_out[...], ((1,), (1,)))
    hidden_grad = (active_grad * gelu_slope(hidden)).astype(BF16)
    y = dot(hidden_grad, gen_in[...], ((1,), (0,)))
    e = y * gains
    grad = scale * (
        e - jnp.mean(e, axis=1, keepdims=True) - unit * jnp.mean(e * unit, axis=1, keepdims=True)
    )
    total = out_grad[...].astype(F32) + grad
    out_total[...] = total
    low_total = total.astype(BF16)
    shard = branch_grad.shape[2]
    for owner in range(branch_grad.shape[0]):
        branch_grad[owner] = low_total[:, owner * shard : (owner + 1) * shard]
    gain_part = jnp.sum(y * unit, axis=0, keepdims=True)
    in_part = dot(hidden_grad, low, ((0,), (0,)))
    mid_part = dot(active, upstream, ((0,), (0,)))

    @pl.when(first)
    def _():
        gain_grad[...] = gain_part
        in_grad[...] = in_part
        mid_grad[...] = jnp.zeros_like(mid_grad)
        mid_grad[:, : mid_part.shape[1]] = mid_part

    @pl.when(jnp.logical_not(first))
    def _():
        gain_grad[...] += gain_part
        in_grad[...] += in_part
        mid_grad[:, : mid_part.shape[1]] += mid_part


def gen_stage(size, streams, branch, gains, gen_in, gen_out, out_grad, next_grad, block=128):
    _, tokens, width = streams.shape
    units = gen_in.shape[0]
    nxt = gen_out.shape[1]
    row = lambda i: (i, 0)
    fixed = lambda i: (0, 0)
    return pl.pallas_call(
        gen_kernel,
        grid=(tokens // block,),
        in_specs=[
            pl.BlockSpec((1, block, width), lambda i: (3, i, 0)),
            pl.BlockSpec((size, block, width // size), lambda i: (0, i, 0)),
            pl.BlockSpec(gains.shape, fixed),
            pl.BlockSpec(gen_in.shape, fixed),
            pl.BlockSpec(gen_out.shape, fixed),
            pl.BlockSpec((block, width), row),
            pl.BlockSpec((nxt, block), lambda i: (0, i)),
        ],
        out_specs=[
            pl.BlockSpec((block, width), row),
            pl.BlockSpec((nxt, block), lambda i: (0, i)),
            pl.BlockSpec((block, width), row),
            pl.BlockSpec((size, block, width // size), lambda i: (0, i, 0)),
            pl.BlockSpec((1, width), fixed),
            pl.BlockSpec((units, width), fixed),
            pl.BlockSpec((units, 128), fixed),
        ],
        out_shape=[
            jax.ShapeDtypeStruct((tokens, width), BF16),
            jax.ShapeDtypeStruct((nxt, tokens), F32),
            jax.ShapeDtypeStruct((tokens, width), F32),
            jax.ShapeDtypeStruct((size, tokens, width // size), BF16),
            jax.ShapeDtypeStruct((1, width), F32),
            jax.ShapeDtypeStruct((units, width), F32),
            jax.ShapeDtypeStruct((units, 128), F32),
        ],
        cost_estimate=pl.CostEstimate(
            flops=tokens * width * 300, bytes_accessed=tokens * width * 16, transcendentals=0
        ),
        compiler_params=pltpu.CompilerParams(vmem_limit_bytes=62 * MIB),
        name="gen_stage",
    )(streams, branch, gains, gen_in, gen_out, out_grad, next_grad)


MESH = pl.DeviceIdType.MESH


def place_of(me, size):
    odd = lax.rem(me, 2)
    at = lax.div(me, 2)
    return (1 - odd) * at + odd * (size - 1 - at)


def index_at(place, size):
    at = lax.rem(place + 2 * size, size)
    back = lax.div(at, size // 2)
    return (1 - back) * 2 * at + back * (2 * (size - 1 - at) + 1)


UNIT = 32


def back_kernel(
    size,
    stats,
    mix,
    gains,
    normed_in,
    hidden_grad_in,
    qkv_low_in,
    parts_in,
    history,
    streams,
    out_total,
    mix_grad,
    gain_sum,
    grad_up_out,
    grad_query_out,
    grad_key_out,
    grad_value_out,
    stream_grad,
    normed,
    hidden_grad,
    qkv_low,
    grad_up,
    grad_qkv,
    gain_grad,
    gain_sent,
    gain_got,
    parts,
    from_core,
    from_link,
    far,
    ring,
    state_in,
    stream_in,
    total_in,
    grad_out,
    held,
    flipped,
    in_sem,
    out_sem,
    ring_send,
    ring_recv,
    core_send,
    core_recv,
    link_send,
    link_recv,
    twin_send,
    twin_recv,
    load_sem,
    unit_sem,
    store_sem,
    gain_send,
    gain_recv,
    freed,
):
    half = size // 2
    shard = normed.shape[3]
    cut = shard // 2
    tokens, hidden_cols = hidden_grad.shape
    width = history.shape[2]
    inverse = 1.0 / width
    states = history.shape[0]
    me = lax.axis_index("dp")
    lane = lax.axis_index("tensor")
    place = place_of(me, size)
    right = index_at(place + 1, size)
    left = index_at(place - 1, size)
    core = lax.rem(lane, 2)
    chip = lax.div(lane, 2)
    twin = chip * 2 + 1 - core
    across = (1 - chip) * 2 + core

    loads = [
        pltpu.make_async_copy(hidden_grad_in, hidden_grad, in_sem.at[4]),
        pltpu.make_async_copy(normed_in.at[3], normed.at[3], in_sem.at[3]),
        pltpu.make_async_copy(qkv_low_in, qkv_low, in_sem.at[5]),
    ] + [
        pltpu.make_async_copy(normed_in.at[stream], normed.at[stream], in_sem.at[stream])
        for stream in range(3)
    ]
    for copy in loads:
        copy.start()

    barrier = pltpu.get_barrier_semaphore()
    steps = size.bit_length() - 1
    partners = [me + (1 << step) * (1 - 2 * lax.rem(lax.div(me, 1 << step), 2)) for step in range(steps)]
    for there in [(right, lane), (left, lane), (me, twin), (me, across)] + [(it, lane) for it in partners]:
        pl.semaphore_signal(barrier, inc=1, device_id=there, device_id_type=MESH)
    pl.semaphore_wait(barrier, 4 + steps)

    block = 64
    rows_half = tokens // 2
    blocks = rows_half // block
    load = pltpu.make_async_copy(parts_in, parts, load_sem)
    load.start()

    wide = 512 if half <= 4 else hidden_cols
    pieces = [(0, at, wide) for at in range(0, hidden_cols, wide)]
    local = qkv_low.shape[1] // 3
    pieces += [(1 + which, which * local, local) for which in range(3)]
    starts = []
    offset = 0
    for _, _, cols in pieces:
        starts.append(offset)
        offset += cols

    def flip(way, distance, some=(0, 1, 2, 3)):
        owner = index_at(place + distance, size)
        for stream in some:
            flipped[way, stream] = normed[stream, owner].T

    def term(way, piece, rows):
        which, at, cols = pieces[piece]
        stream = 3 if which == 0 else which - 1
        other = hidden_grad if which == 0 else qkv_low
        return jnp.dot(
            flipped[way, stream, rows, :], other[:, at : at + cols], preferred_element_type=F32
        )

    def send(hop, way, piece):
        cols = pl.ds(starts[piece], pieces[piece][2])
        if hop == 0:
            rows = pl.ds(way * cut, cut)
            source = far.at[rows, cols]
            target = ring.at[0, way, rows, cols]
        else:
            source = ring.at[hop - 1, way, :, cols]
            target = ring.at[hop, way, :, cols]
        return pltpu.make_async_remote_copy(
            src_ref=source,
            dst_ref=target,
            send_sem=ring_send.at[hop, way, piece],
            recv_sem=ring_recv.at[hop, way, piece],
            device_id=((right, left)[way], lane),
            device_id_type=MESH,
        )

    def open_ring(some):
        for piece in some:
            far_term(piece)
            for way in range(2):
                send(0, way, piece).start()

    def far_term(piece):
        cols = pl.ds(starts[piece], pieces[piece][2])

        def far_rows(rows):
            far[rows, cols] = term(0, piece, rows).astype(BF16)

        row_loop(0, shard, far_rows)

    early = len(pieces) // 2
    for copy in loads[:2]:
        copy.wait()
    flip(0, half, (3,))
    open_ring(range(early))
    load.wait()
    for at in range(blocks):
        rows = pl.ds(pl.multiple_of((1 - core) * rows_half + at * block, block), block)
        pltpu.make_async_remote_copy(
            src_ref=parts.at[:, rows, :],
            dst_ref=from_core.at[at],
            send_sem=core_send.at[at],
            recv_sem=core_recv.at[at],
            device_id=(me, twin),
            device_id_type=MESH,
        ).start()
    for copy in loads[2:]:
        copy.wait()
    flip(0, half, (0, 1, 2))
    for piece in range(early, len(pieces)):
        far_term(piece)

    def mine(at):
        return pl.ds(pl.multiple_of(core * rows_half + at * block, block), block)

    def core_copy(at):
        rows = pl.ds(pl.multiple_of((1 - core) * rows_half + at * block, block), block)
        return pltpu.make_async_remote_copy(
            src_ref=parts.at[:, rows, :],
            dst_ref=from_core.at[at],
            send_sem=core_send.at[at],
            recv_sem=core_recv.at[at],
            device_id=(me, twin),
            device_id_type=MESH,
        )

    def link_copy(at):
        return pltpu.make_async_remote_copy(
            src_ref=parts.at[:, mine(at), :],
            dst_ref=from_link.at[at],
            send_sem=link_send.at[at],
            recv_sem=link_recv.at[at],
            device_id=(me, across),
            device_id_type=MESH,
        )

    def twin_copy(at):
        return pltpu.make_async_remote_copy(
            src_ref=parts.at[:, mine(at), :],
            dst_ref=parts.at[:, mine(at), :],
            send_sem=twin_send.at[at],
            recv_sem=twin_recv.at[at],
            device_id=(me, twin),
            device_id_type=MESH,
        )

    def add_into(at, other):
        base = core * rows_half + at * block

        @pl.loop(0, block // 16)
        def _(step):
            rows = pl.ds(pl.multiple_of(base + step * 16, 16), 16)
            theirs = pl.ds(pl.multiple_of(step * 16, 16), 16)
            for stream in range(4):
                total = parts[stream, rows, :].astype(F32) + other[at, stream, theirs, :].astype(F32)
                parts[stream, rows, :] = total.astype(BF16)

    def to_link(at):
        copy = core_copy(at)
        copy.wait_send()
        pl.semaphore_signal(freed.at[at], inc=1, device_id=(me, twin), device_id_type=MESH)
        copy.wait_recv()
        add_into(at, from_core)
        link_copy(at).start()

    def to_twin(at):
        copy = link_copy(at)
        copy.wait_send()
        copy.wait_recv()
        add_into(at, from_link)
        pl.semaphore_wait(freed.at[at], 1)
        twin_copy(at).start()

    def ready(at):
        copy = twin_copy(at)
        copy.wait_send()
        copy.wait_recv()

    def grad_copy(piece):
        which, at, count = pieces[piece]
        if which == 0:
            source = grad_up.at[:, pl.ds(at, count)]
            target = grad_up_out.at[:, pl.ds(at, count)]
        else:
            source = grad_qkv.at[which - 1]
            target = (grad_query_out, grad_key_out, grad_value_out)[which - 1]
        return pltpu.make_async_copy(source, target, out_sem.at[piece])

    def unit_loads(base, slot):
        rows = pl.ds(pl.multiple_of(base, UNIT), UNIT)
        return (
            pltpu.make_async_copy(history.at[:, rows, :], state_in.at[slot], unit_sem.at[slot, 0]),
            pltpu.make_async_copy(streams.at[:, rows, :], stream_in.at[slot], unit_sem.at[slot, 1]),
            pltpu.make_async_copy(out_total.at[rows, :], total_in.at[slot], unit_sem.at[slot, 2]),
        )

    def unit_store(base, slot):
        rows = pl.ds(pl.multiple_of(base, UNIT), UNIT)
        return pltpu.make_async_copy(grad_out.at[slot], stream_grad.at[:, rows, :], store_sem.at[slot])

    mixes = 2 * blocks

    def task_base(task):
        at, side = divmod(task, 2)
        return side * rows_half + at * block

    gain_grad[...] = jnp.zeros_like(gain_grad)
    mix_grad[...] = jnp.zeros_like(mix_grad)
    for copy in unit_loads(0, 0):
        copy.start()

    def mix_task(task):
        first = task_base(task)

        @pl.loop(0, 2)
        def _(slot):
            @pl.when(slot == 0)
            def _():
                for copy in unit_loads(first + UNIT, 1):
                    copy.start()

            if task + 1 < mixes:

                @pl.when(slot == 1)
                def _():
                    for copy in unit_loads(task_base(task + 1), 0):
                        copy.start()

            for copy in unit_loads(first + slot * UNIT, slot):
                copy.wait()
            if task > 0:
                unit_store(task_base(task - 1) + slot * UNIT, slot).wait()

            @pl.loop(0, UNIT // GROUP)
            def _(step):
                mix_group(first + slot * UNIT + step * GROUP, slot, step * GROUP)

            unit_store(first + slot * UNIT, slot).start()

    def mix_group(base, slot, inner_base):
        rows = pl.ds(pl.multiple_of(base, GROUP), GROUP)
        inner = pl.ds(pl.multiple_of(inner_base, GROUP), GROUP)
        zero = jnp.zeros((GROUP, 128), F32)
        chunks = width // CHUNK

        def window(at):
            return pl.ds(at * CHUNK, CHUNK)

        def lanes(total, value):
            for at_lane in range(0, CHUNK, 128):
                total = total + value[:, at_lane : at_lane + 128]
            return total

        for stream in range(4):
            mean = stats[rows, stream : stream + 1]
            scale = stats[rows, 4 + stream : 5 + stream]
            sum_e, sum_ex = zero, zero
            for at in range(chunks):
                cols = window(at)
                unit_x = (stream_in[slot, stream, inner, cols] - mean) * scale
                upstream = parts[stream, rows, cols].astype(F32)
                e = upstream * gains[stream : stream + 1, cols]
                gain = upstream * unit_x
                gain_grad[stream, :, cols] += gain[:8] + gain[8:]
                sum_e = lanes(sum_e, e)
                sum_ex = lanes(sum_ex, e * unit_x)
            mean_e = jnp.sum(sum_e, axis=1, keepdims=True) * inverse
            mean_ex = jnp.sum(sum_ex, axis=1, keepdims=True) * inverse
            for at in range(chunks):
                cols = window(at)
                unit_x = (stream_in[slot, stream, inner, cols] - mean) * scale
                e = parts[stream, rows, cols].astype(F32) * gains[stream : stream + 1, cols]
                grad = scale * (e - mean_e - unit_x * mean_ex)
                if stream == 3:
                    grad = grad + total_in[slot, inner, cols]
                held[stream, :, cols] = grad
                grad_out[slot, stream, inner, cols] = grad.astype(BF16)
        for source in range(states):
            sums = [zero] * 4
            for at in range(chunks):
                cols = window(at)
                state = state_in[slot, source, inner, cols].astype(F32)
                for stream in range(4):
                    sums[stream] = lanes(sums[stream], state * held[stream, :, cols])
            for stream in range(4):
                k = stream * states + source
                mix_grad[rows, k : k + 1] = jnp.sum(sums[stream], axis=1, keepdims=True)

    def gain_copy(step):
        return pltpu.make_async_remote_copy(
            src_ref=gain_sent.at[step],
            dst_ref=gain_got.at[step],
            send_sem=gain_send.at[step],
            recv_sem=gain_recv.at[step],
            device_id=(partners[step], lane),
            device_id_type=MESH,
        )

    def gain_step(step):
        if step == 0:
            for stream in range(4):
                gain_sent[0, stream : stream + 1, :] = jnp.sum(
                    gain_grad[stream], axis=0, keepdims=True
                )
        else:
            gain_copy(step - 1).wait_recv()
            total = gain_sent[step - 1] + gain_got[step - 1]
            if step == steps:
                gain_sum[...] = total
            else:
                gain_sent[step] = total
        if step < steps:
            gain_copy(step).start()

    tasks = []
    for at in range(blocks):
        tasks.append((0.02 + 0.03 * at, to_link, at))
        tasks.append((0.19 + 0.16 * at, to_twin, at))
        tasks.append((0.23 + 0.16 * at, ready, at))
        for side in range(2):
            tasks.append((0.24 + 0.16 * at + 0.07 * side, mix_task, 2 * at + side))
    for step in range(steps + 1):
        tasks.append((0.87 + 0.12 * step / steps, gain_step, step))
    tasks.sort(key=lambda item: item[0])
    for hop in range(1, half + 1):
        if hop == half:
            flip(0, 0)
        else:
            for way in range(2):
                flip(way, (half - hop) * (1 - 2 * way))
        for piece in range(len(pieces)):
            passed = ((hop - 1.5 if hop > 1 else 0.0) + (piece + 1) / len(pieces) * (1 if hop > 1 else 0.5)) / (half - 0.5)
            cols = pl.ds(starts[piece], pieces[piece][2])
            for way in range(2):
                send(hop - 1, way, piece).wait_recv()
                if hop == half:
                    continue

                def with_got(rows):
                    got = ring[hop - 1, way, rows, cols].astype(F32)
                    ring[hop - 1, way, rows, cols] = (term(way, piece, rows) + got).astype(BF16)

                def alone(rows):
                    ring[hop - 1, way, rows, cols] = term(way, piece, rows).astype(BF16)

                if hop == 1:
                    row_loop(way * cut, cut, with_got)
                    row_loop((1 - way) * cut, cut, alone)
                else:
                    row_loop(0, shard, with_got)
                send(hop, way, piece).start()
            if hop == half:

                def finish(rows):
                    total = (
                        term(0, piece, rows)
                        + ring[hop - 1, 0, rows, cols].astype(F32)
                        + ring[hop - 1, 1, rows, cols].astype(F32)
                    )
                    which, at, count = pieces[piece]
                    if which == 0:
                        grad_up[rows, at : at + count] = total.astype(BF16)
                    else:
                        grad_qkv[which - 1, rows, :] = total.astype(BF16)

                row_loop(0, shard, finish)
                grad_copy(piece).start()
            if hop == 1 and piece == early - 1:
                for late in range(early, len(pieces)):
                    for way in range(2):
                        send(0, way, late).start()
            while tasks and tasks[0][0] <= passed:
                _, run, value = tasks.pop(0)
                run(value)
    for _, run, value in tasks:
        run(value)
    for piece in range(len(pieces)):
        grad_copy(piece).wait()
    for slot in range(2):
        unit_store(task_base(mixes - 1) + slot * UNIT, slot).wait()
    for step in range(steps):
        gain_copy(step).wait_send()
    for hop in range(half):
        for piece in range(len(pieces)):
            for way in range(2):
                send(hop, way, piece).wait_send()


def back_stage(size, normed, hidden_grad, qkv_low, stats, mix, gains, parts, history, streams, out_total):
    half = size // 2
    tokens, hidden = hidden_grad.shape
    states, _, width = history.shape
    shard = normed.shape[3]
    local = qkv_low.shape[1] // 3
    cols = hidden + 3 * local
    count = (hidden // 512 if half <= 4 else 1) + 3
    blocks = tokens // 128
    steps = size.bit_length() - 1
    vmem = pl.BlockSpec(memory_space=pltpu.VMEM)
    hbm = pl.BlockSpec(memory_space=pl.ANY)
    dma = pltpu.SemaphoreType.DMA
    small = jax.ShapeDtypeStruct((shard, local), BF16)
    return pl.pallas_call(
        lambda *refs: back_kernel(size, *refs),
        in_specs=[vmem] * 3 + [hbm] * 7,
        out_specs=[vmem] * 2 + [hbm] * 5,
        out_shape=[
            jax.ShapeDtypeStruct((tokens, mix.shape[1]), F32),
            jax.ShapeDtypeStruct((4, width), F32),
            jax.ShapeDtypeStruct((shard, hidden), BF16),
            small,
            small,
            small,
            jax.ShapeDtypeStruct((4, tokens, width), BF16),
        ],
        scratch_shapes=[
            pltpu.VMEM(normed.shape, BF16),
            pltpu.VMEM((tokens, hidden), BF16),
            pltpu.VMEM((tokens, 3 * local), BF16),
            pltpu.VMEM((shard, hidden), BF16),
            pltpu.VMEM((3, shard, local), BF16),
            pltpu.VMEM((4, 8, width), F32),
            pltpu.VMEM((steps, 4, width), F32),
            pltpu.VMEM((steps, 4, width), F32),
            pltpu.VMEM((4, tokens, width), BF16),
            pltpu.VMEM((blocks, 4, 64, width), BF16),
            pltpu.VMEM((blocks, 4, 64, width), BF16),
            pltpu.VMEM((shard, cols), BF16),
            pltpu.VMEM((half, 2, shard, cols), BF16),
            pltpu.VMEM((2, states, UNIT, width), BF16),
            pltpu.VMEM((2, 4, UNIT, width), F32),
            pltpu.VMEM((2, UNIT, width), F32),
            pltpu.VMEM((2, 4, UNIT, width), BF16),
            pltpu.VMEM((4, GROUP, width), F32),
            pltpu.VMEM((2, 4, shard, tokens), BF16),
            dma((6,)),
            dma((count,)),
            dma((half, 2, count)),
            dma((half, 2, count)),
            dma((blocks,)),
            dma((blocks,)),
            dma((blocks,)),
            dma((blocks,)),
            dma((blocks,)),
            dma((blocks,)),
            dma(()),
            dma((2, 3)),
            dma((2,)),
            dma((steps,)),
            dma((steps,)),
            pltpu.SemaphoreType.REGULAR((blocks,)),
        ],
        cost_estimate=pl.CostEstimate(
            flops=tokens * width * 2000, bytes_accessed=tokens * width * 64, transcendentals=0
        ),
        compiler_params=pltpu.CompilerParams(
            collective_id=1, has_side_effects=True, vmem_limit_bytes=62 * MIB
        ),
        name="back_stage",
    )(stats, mix, gains, normed, hidden_grad, qkv_low, parts, history, streams, out_total)


TILE = 512


def unrotate(values, turn):
    return (
        values * turn[0]
        + pltpu.roll(values, HEAD_DIM - ROT // 2, 1) * turn[1]
        + pltpu.roll(values, ROT // 2, 1) * turn[2]
    )


def row_loop(base, count, run, step=128):
    step = min(step, count)

    @pl.loop(0, count // step)
    def _(at):
        run(pl.ds(pl.multiple_of(base + at * step, step), step))


def attention_probs(query, key, two, first):
    shape = (query.shape[0], key.shape[0])
    middle = key.shape[0] // 2
    scores = dot(query, key, ((1,), (1,))) * (HEAD_DIM ** (-0.5))
    row = first + lax.broadcasted_iota(jnp.int32, shape, 0)
    col = lax.broadcasted_iota(jnp.int32, shape, 1)
    apart = jnp.where(row >= middle, jnp.where(col < middle, two, 0), 0)
    scores = jnp.where(jnp.logical_or(apart != 0, col > row), -1e30, scores)
    weights = jnp.exp(scores - jnp.max(scores, axis=1, keepdims=True))
    return weights / jnp.sum(weights, axis=1, keepdims=True)


def mid_kernel(
    size,
    turn,
    two,
    gen_grad,
    gen_gain,
    gen_mid,
    low_t_in,
    grad_blocks_in,
    hidden_in,
    heads_in,
    low_all,
    up_full,
    qkv_full,
    gen_sum,
    mid_sum,
    grad_out,
    grad_down,
    hidden_grad_out,
    qkv_low_out,
    parts,
    low_t,
    grad_blocks,
    hidden,
    heads,
    low_sum,
    hidden_grad,
    qkv_low,
    attended_grad,
    far,
    ring,
    low_tile,
    up_tile,
    qkv_tile,
    stage,
    gen_sent,
    gen_got,
    mid_sent,
    mid_got,
    value_sum,
    key_sum,
    gen_all,
    share_sem,
    in_sem,
    out_sem,
    ring_send,
    ring_recv,
    tile_sem,
    stage_sem,
    gen_send,
    gen_recv,
):
    half = size // 2
    rows_all, tokens = low_t.shape
    shard = grad_blocks.shape[2]
    local = heads.shape[1] // 3
    me = lax.axis_index("dp")
    lane = lax.axis_index("tensor")
    place = place_of(me, size)
    right = index_at(place + 1, size)
    left = index_at(place - 1, size)
    steps = size.bit_length() - 1
    partners = [me + (1 << step) * (1 - 2 * lax.rem(lax.div(me, 1 << step), 2)) for step in range(steps)]
    loads = [
        pltpu.make_async_copy(source, target, in_sem.at[at])
        for at, (source, target) in enumerate(
            ((low_t_in, low_t), (grad_blocks_in, grad_blocks), (hidden_in, hidden), (heads_in, heads))
        )
    ]
    for copy in loads:
        copy.start()
    core = lax.rem(lane, 2)
    chip = lax.div(lane, 2)
    twin = chip * 2 + 1 - core
    across = (1 - chip) * 2 + core
    barrier = pltpu.get_barrier_semaphore()
    for there in [(it, lane) for it in [right, left] + partners] + [(me, twin), (me, across)]:
        pl.semaphore_signal(barrier, inc=1, device_id=there, device_id_type=MESH)
    pl.semaphore_wait(barrier, 4 + steps)

    low_tiles = rows_all // TILE
    width_tiles = up_full.shape[0] // TILE
    order = (
        [("low", at) for at in range(low_tiles)]
        + [("up", at) for at in range(width_tiles)]
        + [("qkv", at) for at in range(width_tiles)]
    )

    def load(index):
        kind, at = order[index]
        slot = at % 2
        rows = pl.ds(at * TILE, TILE)
        if kind == "low":
            return pltpu.make_async_copy(low_all.at[:, rows, :], low_tile.at[slot], tile_sem.at[0, slot])
        if kind == "up":
            return pltpu.make_async_copy(up_full.at[rows, :], up_tile.at[slot], tile_sem.at[1, slot])
        return pltpu.make_async_copy(qkv_full.at[rows, :], qkv_tile.at[slot], tile_sem.at[2, slot])

    load(0).start()

    pieces = rows_all // TILE
    cut = TILE // 2

    def term(owner, rows):
        return jnp.dot(low_t[rows, :], grad_blocks[owner], preferred_element_type=F32)

    def send(hop, way, piece):
        if hop == 0:
            rows = pl.ds(piece * TILE + way * cut, cut)
            source = far.at[rows, :]
        else:
            rows = pl.ds(piece * TILE, TILE)
            source = ring.at[hop - 1, way, rows, :]
        return pltpu.make_async_remote_copy(
            src_ref=source,
            dst_ref=ring.at[hop, way, rows, :],
            send_sem=ring_send.at[hop, way, piece],
            recv_sem=ring_recv.at[hop, way, piece],
            device_id=((right, left)[way], lane),
            device_id_type=MESH,
        )

    for copy in loads[:2]:
        copy.wait()
    def far_term(piece):
        def far_rows(rows):
            far[rows, :] = term(index_at(place + half, size), rows).astype(BF16)

        row_loop(piece * TILE, TILE, far_rows)

    early = pieces // 2
    for piece in range(early):
        far_term(piece)
        for way in range(2):
            send(0, way, piece).start()
    for piece in range(early, pieces):
        far_term(piece)
    for copy in loads[2:]:
        copy.wait()

    def grad_copy(piece):
        base = piece * TILE
        source = low_sum.at[pl.ds(base, TILE), :]
        if base < local:
            target = grad_out.at[pl.ds(base, TILE), :]
        else:
            target = grad_down.at[pl.ds(base - local, TILE), :]
        return pltpu.make_async_copy(source, target, out_sem.at[2 + piece])

    def hidden_copy():
        return pltpu.make_async_copy(hidden_grad, hidden_grad_out, out_sem.at[0])

    def qkv_copy():
        return pltpu.make_async_copy(qkv_low, qkv_low_out, out_sem.at[1])

    def low_grad(at):
        index = at
        load(index + 1).start()
        load(index).wait()
        base = at * TILE

        def run(rows):
            total = None
            for owner in range(size):
                part = dot(grad_blocks[owner, rows, :], low_tile[at % 2, owner], ((1,), (1,)))
                total = part if total is None else total + part
            if base < local:
                attended_grad[rows, base : base + TILE] = total.astype(BF16)
            else:
                cols = slice(base - local, base - local + TILE)
                hidden_grad[rows, cols] = (total * gelu_slope(hidden[rows, cols])).astype(BF16)

        row_loop(0, tokens, run, 256)
        if at + 1 == low_tiles:
            hidden_copy().start()

    def head_grad(head):
        cols = slice(head * HEAD_DIM, (head + 1) * HEAD_DIM)
        key_cols = slice(local + head * HEAD_DIM, local + (head + 1) * HEAD_DIM)
        value_cols = slice(2 * local + head * HEAD_DIM, 2 * local + (head + 1) * HEAD_DIM)
        scale = HEAD_DIM ** (-0.5)
        value_sum[...] = jnp.zeros_like(value_sum)
        key_sum[...] = jnp.zeros_like(key_sum)

        def run(rows):
            query, key, value = heads[rows, cols], heads[:, key_cols], heads[:, value_cols]
            upstream = attended_grad[rows, cols]
            probs = attention_probs(query, key, two[...], rows.start)
            probs_grad = dot(upstream, value, ((1,), (1,)))
            value_sum[...] += dot(probs.astype(BF16), upstream, ((0,), (0,)))
            row = jnp.sum(probs * probs_grad, axis=1, keepdims=True)
            scores_grad = (probs * (probs_grad - row)).astype(BF16)
            query_grad = dot(scores_grad, key, ((1,), (0,))) * scale
            turns = [turn[which, rows, :] for which in range(3)]
            qkv_low[rows, cols] = unrotate(query_grad, turns).astype(BF16)
            key_sum[...] += dot(scores_grad, query, ((0,), (0,)))

        row_loop(0, tokens, run)
        turns = [turn[which] for which in range(3)]
        qkv_low[:, value_cols] = value_sum[...].astype(BF16)
        qkv_low[:, key_cols] = unrotate(key_sum[...] * scale, turns).astype(BF16)
        if (head + 1) * HEAD_DIM == local:
            qkv_copy().start()

    def part_store(stream, at):
        return pltpu.make_async_copy(
            stage.at[stream], parts.at[stream, :, pl.ds(at * TILE, TILE)], stage_sem.at[stream]
        )

    def up_part(at):
        index = low_tiles + at
        load(index + 1).start()
        load(index).wait()
        if at:
            part_store(3, at - 1).wait()

        def run(rows):
            stage[3, rows, :] = dot(hidden_grad[rows, :], up_tile[at % 2], ((1,), (1,))).astype(BF16)

        row_loop(0, tokens, run, 256)
        part_store(3, at).start()

    def qkv_part(at):
        index = low_tiles + width_tiles + at
        if index + 1 < len(order):
            load(index + 1).start()
        load(index).wait()
        for stream in range(3):
            if at:
                part_store(stream, at - 1).wait()

        def run(rows):
            for stream in range(3):
                cols = slice(stream * local, (stream + 1) * local)
                stage[stream, rows, :] = dot(
                    qkv_low[rows, cols], qkv_tile[at % 2, :, cols], ((1,), (1,))
                ).astype(BF16)

        row_loop(0, tokens, run, 256)
        for stream in range(3):
            part_store(stream, at).start()

    def gen_copies(step):
        return [
            pltpu.make_async_remote_copy(
                src_ref=sent.at[step],
                dst_ref=got.at[step],
                send_sem=gen_send.at[step, which],
                recv_sem=gen_recv.at[step, which],
                device_id=(partners[step], lane),
                device_id_type=MESH,
            )
            for which, (sent, got) in enumerate(((gen_sent, gen_got), (mid_sent, mid_got)))
        ]

    quarter = gen_sent.shape[2]

    def share(which):
        if which == 0:
            cols = pl.ds(pl.multiple_of(lane * quarter, quarter), quarter)
            there = (me, twin)
        else:
            cols = pl.ds(pl.multiple_of(chip * 2 * quarter, 2 * quarter), 2 * quarter)
            there = (me, across)
        return pltpu.make_async_remote_copy(
            src_ref=gen_all.at[:, cols],
            dst_ref=gen_all.at[:, cols],
            send_sem=share_sem.at[0, which],
            recv_sem=share_sem.at[1, which],
            device_id=there,
            device_id_type=MESH,
        )

    def gen_step(step):
        cols = pl.ds(pl.multiple_of(lane * quarter, quarter), quarter)
        if step == 0:
            units = gen_grad.shape[0]
            gen_sent[0, :units, :] = gen_grad[:, cols].astype(BF16)
            gen_sent[0, units:, :] = jnp.broadcast_to(
                gen_gain[:, cols].astype(BF16), (gen_sent.shape[1] - units, quarter)
            )
            mid_sent[0] = gen_mid[...]
        elif step <= steps:
            for copy in gen_copies(step - 1):
                copy.wait_recv()
            total = gen_sent[step - 1].astype(F32) + gen_got[step - 1].astype(F32)
            mid_total = mid_sent[step - 1] + mid_got[step - 1]
            if step == steps:
                gen_all[:, cols] = total
                mid_sum[...] = mid_total
                share(0).start()
            else:
                gen_sent[step] = total.astype(BF16)
                mid_sent[step] = mid_total
        elif step == steps + 1:
            share(0).wait_recv()
            share(1).start()
        else:
            share(1).wait_recv()
            gen_sum[...] = gen_all[...]
        if step < steps:
            for copy in gen_copies(step):
                copy.start()

    tasks = [(low_grad, at) for at in range(low_tiles)]
    tasks += [(head_grad, head) for head in range(local // HEAD_DIM)]
    tasks += [(up_part, at) for at in range(width_tiles)]
    tasks += [(qkv_part, at) for at in range(width_tiles)]
    for step in range(steps + 3):
        tasks.insert(2 + 3 * step, (gen_step, step))
    count = len(tasks)
    slots = half * pieces
    slot = 0
    for hop in range(1, half + 1):
        for piece in range(pieces):
            for way in range(2):
                send(hop - 1, way, piece).wait_recv()
                if hop == half:
                    continue
                owner = index_at(place + (half - hop) * (1 - 2 * way), size)

                def with_got(rows):
                    got = ring[hop - 1, way, rows, :].astype(F32)
                    ring[hop - 1, way, rows, :] = (term(owner, rows) + got).astype(BF16)

                def alone(rows):
                    ring[hop - 1, way, rows, :] = term(owner, rows).astype(BF16)

                if hop == 1:
                    row_loop(piece * TILE + way * cut, cut, with_got)
                    row_loop(piece * TILE + (1 - way) * cut, cut, alone)
                else:
                    row_loop(piece * TILE, TILE, with_got)
                send(hop, way, piece).start()
            if hop == half:

                def finish(rows):
                    low_sum[rows, :] = (
                        term(me, rows)
                        + ring[hop - 1, 0, rows, :].astype(F32)
                        + ring[hop - 1, 1, rows, :].astype(F32)
                    ).astype(BF16)

                row_loop(piece * TILE, TILE, finish)
                grad_copy(piece).start()
            if hop == 1 and piece == early - 1:
                for late in range(early, pieces):
                    for way in range(2):
                        send(0, way, late).start()
            slot += 1
            while tasks and (slot == slots or len(tasks) * (slots - 2) > count * max(slots - 2 - slot, 0)):
                run, value = tasks.pop(0)
                run(value)
    for stream in range(4):
        part_store(stream, width_tiles - 1).wait()
    hidden_copy().wait()
    qkv_copy().wait()
    for piece in range(pieces):
        grad_copy(piece).wait()
    for step in range(steps):
        for copy in gen_copies(step):
            copy.wait_send()
    for which in range(2):
        share(which).wait_send()
    for hop in range(half):
        for piece in range(pieces):
            for way in range(2):
                send(hop, way, piece).wait_send()


def mid_stage(
    size,
    low_t,
    grad_blocks,
    hidden,
    heads,
    turn,
    two,
    gen_grad,
    gen_gain,
    gen_mid,
    low_all,
    up_full,
    qkv_full,
):
    half = size // 2
    rows_all, tokens = low_t.shape
    shard = grad_blocks.shape[2]
    hidden_cols = hidden.shape[1]
    local = heads.shape[1] // 3
    width = up_full.shape[0]
    pieces = rows_all // TILE
    steps = size.bit_length() - 1
    units = gen_grad.shape[0]
    vmem = pl.BlockSpec(memory_space=pltpu.VMEM)
    hbm = pl.BlockSpec(memory_space=pl.ANY)
    dma = pltpu.SemaphoreType.DMA
    return pl.pallas_call(
        lambda *refs: mid_kernel(size, *refs),
        in_specs=[vmem] * 5 + [hbm] * 7,
        out_specs=[vmem] * 2 + [hbm] * 5,
        out_shape=[
            jax.ShapeDtypeStruct((units + 8, width), F32),
            jax.ShapeDtypeStruct(gen_mid.shape, F32),
            jax.ShapeDtypeStruct((local, shard), BF16),
            jax.ShapeDtypeStruct((hidden_cols, shard), BF16),
            jax.ShapeDtypeStruct((tokens, hidden_cols), BF16),
            jax.ShapeDtypeStruct((tokens, 3 * local), BF16),
            jax.ShapeDtypeStruct((4, tokens, width), BF16),
        ],
        scratch_shapes=[
            pltpu.VMEM((rows_all, tokens), BF16),
            pltpu.VMEM((size, tokens, shard), BF16),
            pltpu.VMEM((tokens, hidden_cols), F32),
            pltpu.VMEM((tokens, 3 * local), BF16),
            pltpu.VMEM((rows_all, shard), BF16),
            pltpu.VMEM((tokens, hidden_cols), BF16),
            pltpu.VMEM((tokens, 3 * local), BF16),
            pltpu.VMEM((tokens, local), BF16),
            pltpu.VMEM((rows_all, shard), BF16),
            pltpu.VMEM((half, 2, rows_all, shard), BF16),
            pltpu.VMEM((2, size, TILE, shard), BF16),
            pltpu.VMEM((2, TILE, hidden_cols), BF16),
            pltpu.VMEM((2, TILE, 3 * local), BF16),
            pltpu.VMEM((4, tokens, TILE), BF16),
            pltpu.VMEM((steps, units + 8, width // 4), BF16),
            pltpu.VMEM((steps, units + 8, width // 4), BF16),
            pltpu.VMEM((steps,) + gen_mid.shape, F32),
            pltpu.VMEM((steps,) + gen_mid.shape, F32),
            pltpu.VMEM((tokens, HEAD_DIM), F32),
            pltpu.VMEM((tokens, HEAD_DIM), F32),
            pltpu.VMEM((units + 8, width), F32),
            dma((2, 2)),
            dma((4,)),
            dma((2 + pieces,)),
            dma((half, 2, pieces)),
            dma((half, 2, pieces)),
            dma((3, 2)),
            dma((4,)),
            dma((steps, 2)),
            dma((steps, 2)),
        ],
        cost_estimate=pl.CostEstimate(
            flops=tokens * width * 4000, bytes_accessed=tokens * width * 40, transcendentals=0
        ),
        compiler_params=pltpu.CompilerParams(
            collective_id=2, has_side_effects=True, vmem_limit_bytes=62 * MIB
        ),
        name="mid_stage",
    )(
        turn,
        two,
        gen_grad,
        gen_gain,
        gen_mid,
        low_t,
        grad_blocks,
        hidden,
        heads,
        low_all,
        up_full,
        qkv_full,
    )


def front_kernel(
    size,
    mix_in,
    gains,
    segments,
    frequency,
    history,
    w_query,
    w_key,
    w_value,
    w_up,
    w_out,
    w_down,
    stats,
    branch,
    mix,
    turn,
    two,
    heads_out,
    hidden_out,
    low_t_out,
    normed_out,
    streams,
    qkv_all,
    up_all,
    low_all,
    heads,
    hidden,
    low_t,
    normed,
    low,
    weight_tile,
    low_tile,
    state_in,
    stream_out,
    from_core,
    from_link,
    qkv_send,
    qkv_recv,
    up_send,
    up_recv,
    low_send,
    low_recv,
    own_sem,
    state_sem,
    stream_sem,
    normed_sem,
    out_sem,
    weight_sem,
    tile_sem,
    core_send,
    core_recv,
    link_send,
    link_recv,
    twin_send,
    twin_recv,
    freed,
):
    half = size // 2
    states, tokens, width = history.shape
    shard = width // size
    local = w_query.shape[1]
    hidden_cols = w_up.shape[1]
    inverse = 1.0 / width
    me = lax.axis_index("dp")
    lane = lax.axis_index("tensor")
    place = place_of(me, size)
    right = index_at(place + 1, size)
    left = index_at(place - 1, size)
    core = lax.rem(lane, 2)
    chip = lax.div(lane, 2)
    twin = chip * 2 + 1 - core
    across = (1 - chip) * 2 + core
    rows_half = tokens // 2

    barrier = pltpu.get_barrier_semaphore()
    for there in ((right, lane), (left, lane), (me, twin), (me, across)):
        pl.semaphore_signal(barrier, inc=1, device_id=there, device_id_type=MESH)
    pl.semaphore_wait(barrier, 4)

    wide = TILE
    groups = [
        [(w_query, 0, 0), (w_key, 0, local), (w_value, 0, 2 * local)],
        [(w_up, at, at) for at in range(0, hidden_cols, wide)],
        [(w_out, at, at) for at in range(0, local, wide)]
        + [(w_down, at, local + at) for at in range(0, hidden_cols, wide)],
    ]
    sems = [(qkv_send, qkv_recv), (up_send, up_recv), (low_send, low_recv)]
    cut = (shard // 2, shard // 2, wide // 2)

    def own(group, piece, lo, count):
        source, at, _ = groups[group][piece]
        if group == 2:
            return source.at[pl.ds(at + lo, count), :]
        cols = local if group == 0 else wide
        return source.at[pl.ds(lo, count), pl.ds(at, cols)]

    def held(group, piece, owner, lo, count):
        _, _, at = groups[group][piece]
        if group == 2:
            return low_all.at[owner, pl.ds(at + lo, count), :]
        rows = pl.ds(pl.multiple_of(owner * shard + lo, cut[0]), count)
        if group == 0:
            return qkv_all.at[rows, pl.ds(at, local)]
        return up_all.at[rows, pl.ds(at, wide)]

    def send(group, hop, way, piece):
        owner = index_at(place + (hop - 1) * (2 * way - 1), size)
        whole = shard if group < 2 else wide
        lo, count = (0, whole) if hop < half else (way * cut[group], cut[group])
        target = held(group, piece, owner, lo, count)
        source = own(group, piece, lo, count) if hop == 1 else target
        send_sem, recv_sem = sems[group]
        return pltpu.make_async_remote_copy(
            src_ref=source,
            dst_ref=target,
            send_sem=send_sem.at[hop - 1, way, piece],
            recv_sem=recv_sem.at[hop - 1, way, piece],
            device_id=((right, left)[way], lane),
            device_id_type=MESH,
        )

    def own_copies(group):
        whole = shard if group < 2 else wide
        return [
            pltpu.make_async_copy(
                own(group, piece, 0, whole), held(group, piece, me, 0, whole), own_sem.at[group, piece]
            )
            for piece in range(len(groups[group]))
        ]

    units = tokens // UNIT

    def state_load(unit):
        rows = pl.ds(pl.multiple_of(unit * UNIT, UNIT), UNIT)
        slot = lax.rem(unit, 2)
        return pltpu.make_async_copy(history.at[:, rows, :], state_in.at[slot], state_sem.at[slot])

    def stream_store(unit):
        rows = pl.ds(pl.multiple_of(unit * UNIT, UNIT), UNIT)
        slot = lax.rem(unit, 2)
        return pltpu.make_async_copy(stream_out.at[slot], streams.at[:, rows, :], stream_sem.at[slot])

    per_task = 2

    def tables():
        count = mix_in.shape[0]
        padded = -(-count // 8) * 8
        mix[...] = jnp.concatenate(
            [mix_in[...], jnp.zeros((padded - count, tokens), F32)], axis=0
        ).T
        two[...] = jnp.broadcast_to(segments[0:1, tokens - 1 : tokens], (1, tokens))
        row = lax.broadcasted_iota(jnp.int32, (tokens, HEAD_DIM), 0)
        lanes = lax.broadcasted_iota(jnp.int32, (tokens, HEAD_DIM), 1)
        flag = jnp.broadcast_to(segments[0:1, tokens - 1 : tokens], (tokens, HEAD_DIM))
        place_in = row - jnp.where(row >= tokens // 2, jnp.where(flag != 0, tokens // 2, 0), 0)
        angles = place_in.astype(F32) * frequency[...]
        sine = jnp.sin(angles)
        turn[0] = jnp.cos(angles)
        turn[1] = jnp.where(lanes < ROT // 2, sine, 0.0)
        turn[2] = jnp.where(lanes < ROT // 2, 0.0, -sine)

    def out_copies():
        return [
            pltpu.make_async_copy(source, target, out_sem.at[at])
            for at, (source, target) in enumerate(
                ((heads, heads_out), (hidden, hidden_out), (low_t, low_t_out))
            )
        ]

    def mix_task(task):
        @pl.loop(0, per_task)
        def _(which):
            mix_unit(task * per_task + which, task)

        if (task + 1) * per_task == units:
            normed_store().start()

    def mix_unit(unit, task):
        slot = lax.rem(unit, 2)

        @pl.when(unit + 1 < units)
        def _():
            state_load(unit + 1).start()

        state_load(unit).wait()
        if task > 0:
            stream_store(unit - 2).wait()

        @pl.loop(0, UNIT // GROUP)
        def _(step):
            rows = pl.ds(pl.multiple_of(unit * UNIT + step * GROUP, GROUP), GROUP)
            inner = pl.ds(pl.multiple_of(step * GROUP, GROUP), GROUP)
            weights = mix[rows, :]

            sums = [jnp.zeros((GROUP, 128), F32) for _ in range(4)]
            for at in range(0, width, CHUNK):
                cols = pl.ds(at, CHUNK)
                total = [None] * 4
                for source in range(states):
                    state = state_in[slot, source, inner, cols].astype(F32)
                    for stream in range(4):
                        k = stream * states + source
                        term = weights[:, k : k + 1] * state
                        total[stream] = term if source == 0 else total[stream] + term
                for stream in range(4):
                    stream_out[slot, stream, inner, cols] = total[stream]
                    for at_lane in range(0, CHUNK, 128):
                        sums[stream] = sums[stream] + total[stream][:, at_lane : at_lane + 128]
            for stream in range(4):
                mean = jnp.sum(sums[stream], axis=1, keepdims=True) * inverse
                square = jnp.zeros((GROUP, 128), F32)
                for at in range(0, width, CHUNK):
                    center = stream_out[slot, stream, inner, pl.ds(at, CHUNK)] - mean
                    center = center * center
                    for at_lane in range(0, CHUNK, 128):
                        square = square + center[:, at_lane : at_lane + 128]
                scale = lax.rsqrt(jnp.sum(square, axis=1, keepdims=True) * inverse + EPSILON)
                stats[rows, stream : stream + 1] = mean
                stats[rows, 4 + stream : 5 + stream] = scale
                for at in range(0, width, CHUNK):
                    cols = pl.ds(at, CHUNK)
                    center = stream_out[slot, stream, inner, cols] - mean
                    value = (center * scale * gains[stream : stream + 1, cols]).astype(BF16)
                    for owner in range(at // shard, (at + CHUNK) // shard):
                        base = owner * shard - at
                        normed[stream, owner, rows, :] = value[:, base : base + shard]

        stream_store(unit).start()

    def normed_store():
        return pltpu.make_async_copy(normed, normed_out, normed_sem)

    tiles = 3 + hidden_cols // wide

    def weight_load(tile):
        if tile < 3:
            source = qkv_all.at[:, pl.ds(tile * local, local)]
        else:
            source = up_all.at[:, pl.ds((tile - 3) * wide, wide)]
        return pltpu.make_async_copy(source, weight_tile.at[tile % 2], weight_sem.at[tile % 2])

    def arrived(group):
        for copy in own_copies(group):
            copy.wait()
        for piece in range(len(groups[group])):
            for way in range(2):
                send(group, half, way, piece).wait_recv()

    def tile_product(tile, stream, rows):
        total = None
        for owner in range(size):
            part = jnp.dot(
                normed[stream, owner, rows, :],
                weight_tile[tile % 2, owner * shard : (owner + 1) * shard, :],
                preferred_element_type=F32,
            )
            total = part if total is None else total + part
        return total

    def qkv_task(which):
        if which == 0:
            arrived(0)
            weight_load(0).start()
        if which < 2:
            weight_load(which + 1).start()
        weight_load(which).wait()

        def run(rows):
            product = tile_product(which, which, rows)
            for head in range(local // HEAD_DIM):
                at = head * HEAD_DIM
                part = product[:, at : at + HEAD_DIM]
                if which < 2:
                    part = (
                        part * turn[0, rows, :]
                        - pltpu.roll(part, HEAD_DIM - ROT // 2, 1) * turn[1, rows, :]
                        - pltpu.roll(part, ROT // 2, 1) * turn[2, rows, :]
                    )
                heads[rows, which * local + at : which * local + at + HEAD_DIM] = part.astype(BF16)

        row_loop(0, tokens, run)

    def head_task(head):
        at = head * HEAD_DIM

        def run(rows):
            query = heads[rows, at : at + HEAD_DIM]
            key = heads[:, local + at : local + at + HEAD_DIM]
            value = heads[:, 2 * local + at : 2 * local + at + HEAD_DIM]
            probs = attention_probs(query, key, two[...], rows.start).astype(BF16)
            attended = jnp.dot(probs, value, preferred_element_type=F32)
            low[rows, at : at + HEAD_DIM] = attended.astype(BF16)
            low_t[at : at + HEAD_DIM, rows] = attended.T.astype(BF16)

        row_loop(0, tokens, run)

    def up_task(at):
        if at == 0:
            arrived(1)
            weight_load(3).start()
        if at + 1 < tiles - 3:
            weight_load(4 + at).start()
        weight_load(3 + at).wait()
        cols = slice(at * wide, (at + 1) * wide)
        low_cols = slice(local + at * wide, local + (at + 1) * wide)

        def run(rows):
            product = tile_product(3 + at, 3, rows)
            hidden[rows, cols] = product
            active = gelu(product)
            low[rows, low_cols] = active.astype(BF16)
            low_t[low_cols, rows] = active.T.astype(BF16)

        row_loop(0, tokens, run)
        if at + 1 == tiles - 3:
            for copy in out_copies():
                copy.start()

    distances = [0]
    for hop in range(1, half):
        distances += [-hop, hop]
    distances += [half]

    def tile_load(index):
        owner = index_at(place + distances[index], size)
        return pltpu.make_async_copy(low_all.at[owner], low_tile.at[index % 2], tile_sem.at[index % 2])

    def mine(index):
        return pl.ds(pl.multiple_of(core * rows_half, rows_half), rows_half)

    def core_copy(index):
        owner = index_at(place + distances[index], size)
        rows = pl.ds(pl.multiple_of((1 - core) * rows_half, rows_half), rows_half)
        return pltpu.make_async_remote_copy(
            src_ref=branch.at[owner, rows, :],
            dst_ref=from_core.at[index],
            send_sem=core_send.at[index],
            recv_sem=core_recv.at[index],
            device_id=(me, twin),
            device_id_type=MESH,
        )

    def link_copy(index):
        owner = index_at(place + distances[index], size)
        return pltpu.make_async_remote_copy(
            src_ref=branch.at[owner, mine(index), :],
            dst_ref=from_link.at[index],
            send_sem=link_send.at[index],
            recv_sem=link_recv.at[index],
            device_id=(me, across),
            device_id_type=MESH,
        )

    def twin_copy(index):
        owner = index_at(place + distances[index], size)
        return pltpu.make_async_remote_copy(
            src_ref=branch.at[owner, mine(index), :],
            dst_ref=branch.at[owner, mine(index), :],
            send_sem=twin_send.at[index],
            recv_sem=twin_recv.at[index],
            device_id=(me, twin),
            device_id_type=MESH,
        )

    def low_task(index):
        if index == 0:
            for copy in own_copies(2):
                copy.wait()
        owner = index_at(place + distances[index], size)
        load = tile_load(index)
        load.start()
        load.wait()

        def run(rows):
            branch[owner, rows, :] = jnp.dot(
                low[rows, :], low_tile[index % 2], preferred_element_type=F32
            ).astype(BF16)

        row_loop(0, tokens, run)
        core_copy(index).start()

    def add_into(index, other):
        owner = index_at(place + distances[index], size)
        rows = mine(index)
        branch[owner, rows, :] = (
            branch[owner, rows, :].astype(F32) + other[index].astype(F32)
        ).astype(BF16)

    def link_task(index):
        copy = core_copy(index)
        copy.wait_send()
        pl.semaphore_signal(freed.at[index], inc=1, device_id=(me, twin), device_id_type=MESH)
        copy.wait_recv()
        add_into(index, from_core)
        link_copy(index).start()

    def twin_task(index):
        copy = link_copy(index)
        copy.wait_send()
        copy.wait_recv()
        add_into(index, from_link)
        pl.semaphore_wait(freed.at[index], 1)
        twin_copy(index).start()

    state_load(0).start()
    slots = [(group, hop) for group in range(3) for hop in range(1, half + 1)]
    counts = [len(pieces) for pieces in groups]
    first = [0, counts[0] * half, (counts[0] + counts[1]) * half]
    total_slots = sum(counts) * half
    tasks = []
    mixes = units // per_task
    for task in range(mixes):
        tasks.append((counts[0] - 1 + task * (first[1] - counts[0]) / mixes, mix_task, task))
    early = first[1] + counts[1]
    for which in range(3):
        tasks.append((early + which, qkv_task, which))
    for head in range(local // HEAD_DIM):
        tasks.append((early + 3 + head, head_task, head))
    middle = first[2] + counts[2]
    for at in range(tiles - 3):
        tasks.append((middle + at, up_task, at))
    for index in range(len(distances) - 1):
        due = max(first[2] + counts[2] * (abs(distances[index]) + 1) - 1, middle + tiles - 3) + 0.5 * (index % 2)
        tasks.append((due, low_task, index))
        tasks.append((due + 1, link_task, index))
        tasks.append((due + 3, twin_task, index))
    tasks.sort(key=lambda item: item[0])

    at_slot = 0
    for group, hop in slots:
        if hop == 1:
            for copy in own_copies(group):
                copy.start()
        for piece in range(counts[group]):
            for way in range(2):
                if hop > 1:
                    send(group, hop - 1, way, piece).wait_recv()
                send(group, hop, way, piece).start()
            if at_slot == 0:
                tables()
            while tasks and tasks[0][0] <= at_slot and at_slot < total_slots - 1:
                _, run, value = tasks.pop(0)
                run(value)
            at_slot += 1
    for _, run, value in tasks:
        run(value)
    for piece in range(counts[2]):
        for way in range(2):
            send(2, half, way, piece).wait_recv()
    last = len(distances) - 1
    low_task(last)
    link_task(last)
    twin_task(last)
    for index in range(len(distances)):
        copy = twin_copy(index)
        copy.wait_send()
        copy.wait_recv()
    for unit in range(units - 2, units):
        stream_store(unit).wait()
    normed_store().wait()
    for copy in out_copies():
        copy.wait()
    for group, hop in slots:
        for piece in range(counts[group]):
            for way in range(2):
                send(group, hop, way, piece).wait_send()


def front_stage(size, mix, gains, segments, frequency, history, w_query, w_key, w_value, w_up, w_out, w_down):
    half = size // 2
    states, tokens, width = history.shape
    shard = width // size
    local = w_query.shape[1]
    hidden_cols = w_up.shape[1]
    rows_all = local + hidden_cols
    vmem = pl.BlockSpec(memory_space=pltpu.VMEM)
    hbm = pl.BlockSpec(memory_space=pl.ANY)
    dma = pltpu.SemaphoreType.DMA
    up_pieces = hidden_cols // TILE
    low_pieces = rows_all // TILE
    return pl.pallas_call(
        lambda *refs: front_kernel(size, *refs),
        in_specs=[vmem] * 4 + [hbm] * 7,
        out_specs=[vmem] * 5 + [hbm] * 8,
        out_shape=[
            jax.ShapeDtypeStruct((tokens, 8), F32),
            jax.ShapeDtypeStruct((size, tokens, shard), BF16),
            jax.ShapeDtypeStruct((tokens, -(-mix.shape[0] // 8) * 8), F32),
            jax.ShapeDtypeStruct((3, tokens, HEAD_DIM), F32),
            jax.ShapeDtypeStruct((1, tokens), jnp.int32),
            jax.ShapeDtypeStruct((tokens, 3 * local), BF16),
            jax.ShapeDtypeStruct((tokens, hidden_cols), F32),
            jax.ShapeDtypeStruct((rows_all, tokens), BF16),
            jax.ShapeDtypeStruct((4, size, tokens, shard), BF16),
            jax.ShapeDtypeStruct((4, tokens, width), F32),
            jax.ShapeDtypeStruct((width, 3 * local), BF16),
            jax.ShapeDtypeStruct((width, hidden_cols), BF16),
            jax.ShapeDtypeStruct((size, rows_all, shard), BF16),
        ],
        scratch_shapes=[
            pltpu.VMEM((tokens, 3 * local), BF16),
            pltpu.VMEM((tokens, hidden_cols), F32),
            pltpu.VMEM((rows_all, tokens), BF16),
            pltpu.VMEM((4, size, tokens, shard), BF16),
            pltpu.VMEM((tokens, rows_all), BF16),
            pltpu.VMEM((2, width, TILE), BF16),
            pltpu.VMEM((2, rows_all, shard), BF16),
            pltpu.VMEM((2, states, UNIT, width), BF16),
            pltpu.VMEM((2, 4, UNIT, width), F32),
            pltpu.VMEM((size, tokens // 2, shard), BF16),
            pltpu.VMEM((size, tokens // 2, shard), BF16),
            dma((half, 2, 3)),
            dma((half, 2, 3)),
            dma((half, 2, up_pieces)),
            dma((half, 2, up_pieces)),
            dma((half, 2, low_pieces)),
            dma((half, 2, low_pieces)),
            dma((3, low_pieces)),
            dma((2,)),
            dma((2,)),
            dma(()),
            dma((3,)),
            dma((2,)),
            dma((2,)),
            dma((size,)),
            dma((size,)),
            dma((size,)),
            dma((size,)),
            dma((size,)),
            dma((size,)),
            pltpu.SemaphoreType.REGULAR((size,)),
        ],
        cost_estimate=pl.CostEstimate(
            flops=tokens * width * 8000, bytes_accessed=tokens * width * 80, transcendentals=0
        ),
        compiler_params=pltpu.CompilerParams(
            collective_id=3, has_side_effects=True, vmem_limit_bytes=62 * MIB
        ),
        name="front_stage",
    )(mix, gains, segments, frequency, history, w_query, w_key, w_value, w_up, w_out, w_down)


def finish_kernel(count, mix, grads, mix_grad, gain_sum, gen_gain, *refs):
    sources = refs[:count]
    history_grad, mix_out, gain_out = refs[count : count + 3]
    targets = refs[count + 3 : 2 * count + 3]
    spread = refs[2 * count + 3]
    states, tokens, width = history_grad.shape
    step = pl.program_id(0)
    for source, target in zip(sources, targets):
        target[...] = source[...].astype(F32)

    @pl.when(step == 0)
    def _():
        gain_out[:4, :] = gain_sum[...]
        gain_out[4:5, :] = gen_gain[0:1, :]
        mix_out[...] = mix_grad[...].T[: mix_out.shape[0], :]

    own = lax.broadcasted_iota(jnp.int32, (tokens, tokens), 0) == lax.broadcasted_iota(
        jnp.int32, (tokens, tokens), 1
    )
    weights = mix[...]
    for source in range(states):
        parts = [
            jnp.where(own, weights[:, stream * states + source : stream * states + source + 1], 0.0)
            for stream in range(4)
        ]
        spread[source * tokens : (source + 1) * tokens, :] = jnp.concatenate(parts, axis=1).astype(BF16)

    @pl.loop(0, width // 512)
    def _(at):
        cols = pl.ds(pl.multiple_of(at * 512, 512), 512)
        grad = jnp.concatenate([grads[stream, :, cols] for stream in range(4)], axis=0)
        mixed = jnp.dot(spread[...], grad, preferred_element_type=F32)
        for source in range(states):
            history_grad[source, :, cols] = mixed[source * tokens : (source + 1) * tokens].astype(BF16)


def finish_stage(states, mixes, mix, grads, mix_grad, gain_sum, gen_sum, sources, block=64):
    _, tokens, width = grads.shape
    steps = tokens // block
    row = lambda i: (i, 0)
    passed = [pl.BlockSpec((source.shape[0] // steps, source.shape[1]), row) for source in sources]
    fixed = lambda i: (0, 0)
    units = gen_sum.shape[0] - 8
    return pl.pallas_call(
        lambda *refs: finish_kernel(len(sources), *refs),
        grid=(steps,),
        in_specs=[
            pl.BlockSpec((block, mix.shape[1]), lambda i: (i, 0)),
            pl.BlockSpec((4, block, width), lambda i: (0, i, 0)),
            pl.BlockSpec(mix_grad.shape, fixed),
            pl.BlockSpec(gain_sum.shape, fixed),
            pl.BlockSpec((8, width), lambda i: (units // 8, 0)),
        ]
        + passed,
        out_specs=[
            pl.BlockSpec((states, block, width), lambda i: (0, i, 0)),
            pl.BlockSpec((mixes, tokens), fixed),
            pl.BlockSpec((5, width), fixed),
        ]
        + passed,
        out_shape=[
            jax.ShapeDtypeStruct((states, tokens, width), BF16),
            jax.ShapeDtypeStruct((mixes, tokens), F32),
            jax.ShapeDtypeStruct((5, width), F32),
        ]
        + [jax.ShapeDtypeStruct(source.shape, F32) for source in sources],
        scratch_shapes=[
            pltpu.VMEM((states * block, 4 * block), BF16),
        ],
        cost_estimate=pl.CostEstimate(
            flops=tokens * width * 72, bytes_accessed=tokens * width * 26, transcendentals=0
        ),
        compiler_params=pltpu.CompilerParams(vmem_limit_bytes=62 * MIB),
        name="finish_stage",
    )(mix, grads, mix_grad, gain_sum, gen_sum, *sources)


def body(
    sizes,
    history,
    mix_weights,
    segments,
    norm_gains,
    w_query,
    w_key,
    w_value,
    w_out,
    w_up,
    w_down,
    gen_in,
    gen_out,
    out_grad,
    next_grad,
):
    dp_size, tensor_size = sizes
    places = np.arange(HEAD_DIM)
    frequency = np.where(
        places < ROT, np.float32(ROPE_BASE) ** (-2.0 * (places % (ROT // 2)).astype(np.float32) / ROT), 0.0
    ).astype(np.float32)
    stats, branch, mix_rows, turn, two, heads, hidden, low_t, normed, streams, full_qkv, full_up, low_all = front_stage(
        dp_size,
        mix_weights,
        norm_gains,
        segments[None, :],
        jnp.asarray(frequency)[None, :],
        history,
        w_query,
        w_key,
        w_value,
        w_up,
        w_out,
        w_down,
    )
    layer_out, next_mix, out_total, branch_grad, gain_gen_grad, grad_gen_in, grad_gen_out = gen_stage(
        dp_size, streams, branch, norm_gains, gen_in.T, gen_out, out_grad, next_grad
    )

    gen_units, gen_next = gen_out.shape
    gen_sum, mid_sum, grad_out, grad_down, hidden_grad, qkv_low, parts = mid_stage(
        dp_size,
        low_t,
        branch_grad,
        hidden,
        heads,
        turn,
        two,
        grad_gen_in,
        gain_gen_grad,
        grad_gen_out,
        low_all,
        full_up,
        full_qkv,
    )
    mix_grad, gain_sums, grad_up, grad_query, grad_key, grad_value, stream_grad = back_stage(
        dp_size,
        normed,
        hidden_grad,
        qkv_low,
        stats,
        mix_rows,
        norm_gains,
        parts,
        history,
        streams,
        out_total,
    )
    history_grad, mix_grad, grad_gains, grad_up, grad_query, grad_key, grad_value, grad_out, grad_down = finish_stage(
        history.shape[0],
        mix_weights.shape[0],
        mix_rows,
        stream_grad,
        mix_grad,
        gain_sums,
        gen_sum,
        (grad_up, grad_query, grad_key, grad_value, grad_out, grad_down),
    )
    return (
        layer_out,
        next_mix,
        history_grad,
        mix_grad,
        grad_gains,
        grad_query,
        grad_key,
        grad_value,
        grad_out,
        grad_up,
        grad_down,
        gen_sum[:gen_units].T,
        mid_sum[:, :gen_next],
    )


def solution(mesh):
    sizes = (mesh.shape["dp"], mesh.shape["tensor"])
    in_specs = (
        P(None, "dp", None),
        P(None, "dp"),
        P("dp"),
        P(),
        P("dp", "tensor"),
        P("dp", "tensor"),
        P("dp", "tensor"),
        P("tensor", "dp"),
        P("dp", "tensor"),
        P("tensor", "dp"),
        P(),
        P(),
        P("dp", None),
        P(None, "dp"),
    )
    out_specs = (
        P("dp", None),
        P(None, "dp"),
        P(None, "dp", None),
        P(None, "dp"),
        P(),
        P("dp", "tensor"),
        P("dp", "tensor"),
        P("dp", "tensor"),
        P("tensor", "dp"),
        P("dp", "tensor"),
        P("tensor", "dp"),
        P(),
        P(),
    )

    def step(*arrays):
        return body(sizes, *arrays)

    return jax.shard_map(step, mesh=mesh, in_specs=in_specs, out_specs=out_specs, check_vma=False)
```

```python
import jax
import jax.numpy as jnp
import numpy as np
from jax import lax
from jax.experimental import pallas as pl
from jax.experimental.pallas import tpu as pltpu
from jax.sharding import PartitionSpec as P

HEAD_DIM = 128
ROT = 32


EPSILON = 1e-05
ROPE_BASE = 10000.0

F32 = jnp.float32
BF16 = jnp.bfloat16


MIB = 1 << 20
GROUP = 16
CHUNK = 512


def gelu(x):
    return 0.5 * x * (1.0 + lax.erf(x * (0.5**0.5)))


def gelu_slope(x):
    return 0.5 * (1.0 + lax.erf(x * (0.5**0.5))) + x * jnp.exp(-0.5 * x * x) * 0.3989422804014327


def dot(a, b, dims):
    return lax.dot_general(a, b, (dims, ((), ())), preferred_element_type=F32)


def gen_kernel(stream, branch, gain, gen_in, gen_out, out_grad, next_grad, layer_out, next_mix, out_total, branch_grad, gain_grad, in_grad, mid_grad):
    first = pl.program_id(0) == 0
    x = stream[0] + jnp.concatenate([branch[owner] for owner in range(branch.shape[0])], axis=1).astype(F32)
    layer_out[...] = x.astype(BF16)
    center = x - jnp.mean(x, axis=1, keepdims=True)
    scale = lax.rsqrt(jnp.mean(center * center, axis=1, keepdims=True) + EPSILON)
    unit = center * scale
    gains = gain[4:5, :]
    low = (unit * gains).astype(BF16)
    hidden = dot(low, gen_in[...], ((1,), (1,)))
    active = gelu(hidden).astype(BF16)
    next_mix[...] = dot(active, gen_out[...], ((1,), (0,))).T
    upstream = next_grad[...].T.astype(BF16)
    active_grad = dot(upstream, gen_out[...], ((1,), (1,)))
    hidden_grad = (active_grad * gelu_slope(hidden)).astype(BF16)
    y = dot(hidden_grad, gen_in[...], ((1,), (0,)))
    e = y * gains
    grad = scale * (
        e - jnp.mean(e, axis=1, keepdims=True) - unit * jnp.mean(e * unit, axis=1, keepdims=True)
    )
    total = out_grad[...].astype(F32) + grad
    out_total[...] = total
    low_total = total.astype(BF16)
    shard = branch_grad.shape[2]
    for owner in range(branch_grad.shape[0]):
        branch_grad[owner] = low_total[:, owner * shard : (owner + 1) * shard]
    gain_part = jnp.sum(y * unit, axis=0, keepdims=True)
    in_part = dot(hidden_grad, low, ((0,), (0,)))
    mid_part = dot(active, upstream, ((0,), (0,)))

    @pl.when(first)
    def _():
        gain_grad[...] = gain_part
        in_grad[...] = in_part
        mid_grad[...] = jnp.zeros_like(mid_grad)
        mid_grad[:, : mid_part.shape[1]] = mid_part

    @pl.when(jnp.logical_not(first))
    def _():
        gain_grad[...] += gain_part
        in_grad[...] += in_part
        mid_grad[:, : mid_part.shape[1]] += mid_part


def gen_stage(size, streams, branch, gains, gen_in, gen_out, out_grad, next_grad, block=128):
    _, tokens, width = streams.shape
    units = gen_in.shape[0]
    nxt = gen_out.shape[1]
    row = lambda i: (i, 0)
    fixed = lambda i: (0, 0)
    return pl.pallas_call(
        gen_kernel,
        grid=(tokens // block,),
        in_specs=[
            pl.BlockSpec((1, block, width), lambda i: (3, i, 0)),
            pl.BlockSpec((size, block, width // size), lambda i: (0, i, 0)),
            pl.BlockSpec(gains.shape, fixed),
            pl.BlockSpec(gen_in.shape, fixed),
            pl.BlockSpec(gen_out.shape, fixed),
            pl.BlockSpec((block, width), row),
            pl.BlockSpec((nxt, block), lambda i: (0, i)),
        ],
        out_specs=[
            pl.BlockSpec((block, width), row),
            pl.BlockSpec((nxt, block), lambda i: (0, i)),
            pl.BlockSpec((block, width), row),
            pl.BlockSpec((size, block, width // size), lambda i: (0, i, 0)),
            pl.BlockSpec((1, width), fixed),
            pl.BlockSpec((units, width), fixed),
            pl.BlockSpec((units, 128), fixed),
        ],
        out_shape=[
            jax.ShapeDtypeStruct((tokens, width), BF16),
            jax.ShapeDtypeStruct((nxt, tokens), F32),
            jax.ShapeDtypeStruct((tokens, width), F32),
            jax.ShapeDtypeStruct((size, tokens, width // size), BF16),
            jax.ShapeDtypeStruct((1, width), F32),
            jax.ShapeDtypeStruct((units, width), F32),
            jax.ShapeDtypeStruct((units, 128), F32),
        ],
        cost_estimate=pl.CostEstimate(
            flops=tokens * width * 300, bytes_accessed=tokens * width * 16, transcendentals=0
        ),
        compiler_params=pltpu.CompilerParams(vmem_limit_bytes=62 * MIB),
        name="gen_stage",
    )(streams, branch, gains, gen_in, gen_out, out_grad, next_grad)


MESH = pl.DeviceIdType.MESH


def place_of(me, size):
    odd = lax.rem(me, 2)
    at = lax.div(me, 2)
    return (1 - odd) * at + odd * (size - 1 - at)


def index_at(place, size):
    at = lax.rem(place + 2 * size, size)
    back = lax.div(at, size // 2)
    return (1 - back) * 2 * at + back * (2 * (size - 1 - at) + 1)


UNIT = 32


def back_kernel(
    size,
    stats,
    mix,
    gains,
    normed_in,
    hidden_grad_in,
    qkv_low_in,
    parts_in,
    history,
    streams,
    out_total,
    mix_grad,
    gain_sum,
    grad_up_out,
    grad_query_out,
    grad_key_out,
    grad_value_out,
    stream_grad,
    normed,
    hidden_grad,
    qkv_low,
    grad_up,
    grad_qkv,
    gain_grad,
    gain_sent,
    gain_got,
    parts,
    from_core,
    from_link,
    far,
    ring,
    state_in,
    stream_in,
    total_in,
    grad_out,
    held,
    flipped,
    in_sem,
    out_sem,
    ring_send,
    ring_recv,
    core_send,
    core_recv,
    link_send,
    link_recv,
    twin_send,
    twin_recv,
    load_sem,
    unit_sem,
    store_sem,
    gain_send,
    gain_recv,
    freed,
):
    half = size // 2
    shard = normed.shape[3]
    cut = shard // 2
    tokens, hidden_cols = hidden_grad.shape
    width = history.shape[2]
    inverse = 1.0 / width
    states = history.shape[0]
    me = lax.axis_index("dp")
    lane = lax.axis_index("tensor")
    place = place_of(me, size)
    right = index_at(place + 1, size)
    left = index_at(place - 1, size)
    core = lax.rem(lane, 2)
    chip = lax.div(lane, 2)
    twin = chip * 2 + 1 - core
    across = (1 - chip) * 2 + core

    loads = [
        pltpu.make_async_copy(hidden_grad_in, hidden_grad, in_sem.at[4]),
        pltpu.make_async_copy(normed_in.at[3], normed.at[3], in_sem.at[3]),
        pltpu.make_async_copy(qkv_low_in, qkv_low, in_sem.at[5]),
    ] + [
        pltpu.make_async_copy(normed_in.at[stream], normed.at[stream], in_sem.at[stream])
        for stream in range(3)
    ]
    for copy in loads:
        copy.start()

    barrier = pltpu.get_barrier_semaphore()
    steps = size.bit_length() - 1
    partners = [me + (1 << step) * (1 - 2 * lax.rem(lax.div(me, 1 << step), 2)) for step in range(steps)]
    for there in [(right, lane), (left, lane), (me, twin), (me, across)] + [(it, lane) for it in partners]:
        pl.semaphore_signal(barrier, inc=1, device_id=there, device_id_type=MESH)
    pl.semaphore_wait(barrier, 4 + steps)

    block = 64
    rows_half = tokens // 2
    blocks = rows_half // block
    load = pltpu.make_async_copy(parts_in, parts, load_sem)
    load.start()

    wide = 512 if half <= 4 else hidden_cols
    pieces = [(0, at, wide) for at in range(0, hidden_cols, wide)]
    local = qkv_low.shape[1] // 3
    pieces += [(1 + which, which * local, local) for which in range(3)]
    starts = []
    offset = 0
    for _, _, cols in pieces:
        starts.append(offset)
        offset += cols

    def flip(way, distance, some=(0, 1, 2, 3)):
        owner = index_at(place + distance, size)
        for stream in some:
            flipped[way, stream] = normed[stream, owner].T

    def term(way, piece, rows):
        which, at, cols = pieces[piece]
        stream = 3 if which == 0 else which - 1
        other = hidden_grad if which == 0 else qkv_low
        return jnp.dot(
            flipped[way, stream, rows, :], other[:, at : at + cols], preferred_element_type=F32
        )

    def send(hop, way, piece):
        cols = pl.ds(starts[piece], pieces[piece][2])
        if hop == 0:
            rows = pl.ds(pl.multiple_of(way * cut, cut), cut)
            source = far.at[rows, cols]
            target = ring.at[0, way, rows, cols]
        else:
            source = ring.at[hop - 1, way, :, cols]
            target = ring.at[hop, way, :, cols]
        return pltpu.make_async_remote_copy(
            src_ref=source,
            dst_ref=target,
            send_sem=ring_send.at[hop, way, piece],
            recv_sem=ring_recv.at[hop, way, piece],
            device_id=(right + way * (left - right), lane),
            device_id_type=MESH,
        )

    def open_ring(some):
        for piece in some:
            far_term(piece)
            for way in range(2):
                send(0, way, piece).start()

    def far_term(piece):
        cols = pl.ds(starts[piece], pieces[piece][2])

        def far_rows(rows):
            far[rows, cols] = term(0, piece, rows).astype(BF16)

        row_loop(0, shard, far_rows)

    early = len(pieces) // 2
    for copy in loads[:2]:
        copy.wait()
    flip(0, half, (3,))
    open_ring(range(early))
    load.wait()
    for at in range(blocks):
        rows = pl.ds(pl.multiple_of((1 - core) * rows_half + at * block, block), block)
        pltpu.make_async_remote_copy(
            src_ref=parts.at[:, rows, :],
            dst_ref=from_core.at[at],
            send_sem=core_send.at[at],
            recv_sem=core_recv.at[at],
            device_id=(me, twin),
            device_id_type=MESH,
        ).start()
    for copy in loads[2:]:
        copy.wait()
    flip(0, half, (0, 1, 2))
    for piece in range(early, len(pieces)):
        far_term(piece)

    def mine(at):
        return pl.ds(pl.multiple_of(core * rows_half + at * block, block), block)

    def core_copy(at):
        rows = pl.ds(pl.multiple_of((1 - core) * rows_half + at * block, block), block)
        return pltpu.make_async_remote_copy(
            src_ref=parts.at[:, rows, :],
            dst_ref=from_core.at[at],
            send_sem=core_send.at[at],
            recv_sem=core_recv.at[at],
            device_id=(me, twin),
            device_id_type=MESH,
        )

    def link_copy(at):
        return pltpu.make_async_remote_copy(
            src_ref=parts.at[:, mine(at), :],
            dst_ref=from_link.at[at],
            send_sem=link_send.at[at],
            recv_sem=link_recv.at[at],
            device_id=(me, across),
            device_id_type=MESH,
        )

    def twin_copy(at):
        return pltpu.make_async_remote_copy(
            src_ref=parts.at[:, mine(at), :],
            dst_ref=parts.at[:, mine(at), :],
            send_sem=twin_send.at[at],
            recv_sem=twin_recv.at[at],
            device_id=(me, twin),
            device_id_type=MESH,
        )

    def add_into(at, other):
        base = core * rows_half + at * block

        @pl.loop(0, block // 16)
        def _(step):
            rows = pl.ds(pl.multiple_of(base + step * 16, 16), 16)
            theirs = pl.ds(pl.multiple_of(step * 16, 16), 16)
            for stream in range(4):
                total = parts[stream, rows, :].astype(F32) + other[at, stream, theirs, :].astype(F32)
                parts[stream, rows, :] = total.astype(BF16)

    def to_link(at):
        copy = core_copy(at)
        copy.wait_send()
        pl.semaphore_signal(freed.at[at], inc=1, device_id=(me, twin), device_id_type=MESH)
        copy.wait_recv()
        add_into(at, from_core)
        link_copy(at).start()

    def to_twin(at):
        copy = link_copy(at)
        copy.wait_send()
        copy.wait_recv()
        add_into(at, from_link)
        pl.semaphore_wait(freed.at[at], 1)
        twin_copy(at).start()

    def ready(at):
        copy = twin_copy(at)
        copy.wait_send()
        copy.wait_recv()

    def grad_copy(piece):
        which, at, count = pieces[piece]
        if which == 0:
            source = grad_up.at[:, pl.ds(at, count)]
            target = grad_up_out.at[:, pl.ds(at, count)]
        else:
            source = grad_qkv.at[which - 1]
            target = (grad_query_out, grad_key_out, grad_value_out)[which - 1]
        return pltpu.make_async_copy(source, target, out_sem.at[piece])

    def unit_loads(base, slot):
        rows = pl.ds(pl.multiple_of(base, UNIT), UNIT)
        return (
            pltpu.make_async_copy(history.at[:, rows, :], state_in.at[slot], unit_sem.at[slot, 0]),
            pltpu.make_async_copy(streams.at[:, rows, :], stream_in.at[slot], unit_sem.at[slot, 1]),
            pltpu.make_async_copy(out_total.at[rows, :], total_in.at[slot], unit_sem.at[slot, 2]),
        )

    def unit_store(base, slot):
        rows = pl.ds(pl.multiple_of(base, UNIT), UNIT)
        return pltpu.make_async_copy(grad_out.at[slot], stream_grad.at[:, rows, :], store_sem.at[slot])

    def unit_base(at, unit):
        return lax.div(unit, 2) * rows_half + at * block + lax.rem(unit, 2) * UNIT

    gain_grad[...] = jnp.zeros_like(gain_grad)
    mix_grad[...] = jnp.zeros_like(mix_grad)
    for copy in unit_loads(0, 0):
        copy.start()

    def mix_task(at):
        @pl.loop(0, 4)
        def _(unit):
            slot = lax.rem(unit, 2)
            base = unit_base(at, unit)

            @pl.when(unit < 3)
            def _():
                for copy in unit_loads(unit_base(at, unit + 1), 1 - slot):
                    copy.start()

            if at + 1 < blocks:

                @pl.when(unit == 3)
                def _():
                    for copy in unit_loads((at + 1) * block, 0):
                        copy.start()

            for copy in unit_loads(base, slot):
                copy.wait()
            if at > 0:
                unit_store(base, slot).wait()
            else:

                @pl.when(unit >= 2)
                def _():
                    unit_store(base, slot).wait()

            @pl.loop(0, UNIT // GROUP)
            def _(step):
                mix_group(base + step * GROUP, slot, step * GROUP)

            unit_store(base, slot).start()

    def mix_group(base, slot, inner_base):
        rows = pl.ds(pl.multiple_of(base, GROUP), GROUP)
        inner = pl.ds(pl.multiple_of(inner_base, GROUP), GROUP)
        zero = jnp.zeros((GROUP, 128), F32)
        chunks = width // CHUNK

        def window(at):
            return pl.ds(at * CHUNK, CHUNK)

        def lanes(total, value):
            for at_lane in range(0, CHUNK, 128):
                total = total + value[:, at_lane : at_lane + 128]
            return total

        for stream in range(4):
            mean = stats[rows, stream : stream + 1]
            scale = stats[rows, 4 + stream : 5 + stream]
            sum_e, sum_ex = zero, zero
            for at in range(chunks):
                cols = window(at)
                unit_x = (stream_in[slot, stream, inner, cols] - mean) * scale
                upstream = parts[stream, rows, cols].astype(F32)
                e = upstream * gains[stream : stream + 1, cols]
                gain = upstream * unit_x
                gain_grad[stream, :, cols] += gain[:8] + gain[8:]
                sum_e = lanes(sum_e, e)
                sum_ex = lanes(sum_ex, e * unit_x)
            mean_e = jnp.sum(sum_e, axis=1, keepdims=True) * inverse
            mean_ex = jnp.sum(sum_ex, axis=1, keepdims=True) * inverse
            for at in range(chunks):
                cols = window(at)
                unit_x = (stream_in[slot, stream, inner, cols] - mean) * scale
                e = parts[stream, rows, cols].astype(F32) * gains[stream : stream + 1, cols]
                grad = scale * (e - mean_e - unit_x * mean_ex)
                if stream == 3:
                    grad = grad + total_in[slot, inner, cols]
                held[stream, :, cols] = grad
                grad_out[slot, stream, inner, cols] = grad.astype(BF16)
        for source in range(states):
            sums = [zero] * 4
            for at in range(chunks):
                cols = window(at)
                state = state_in[slot, source, inner, cols].astype(F32)
                for stream in range(4):
                    sums[stream] = lanes(sums[stream], state * held[stream, :, cols])
            for stream in range(4):
                k = stream * states + source
                mix_grad[rows, k : k + 1] = jnp.sum(sums[stream], axis=1, keepdims=True)

    def gain_copy(step):
        return pltpu.make_async_remote_copy(
            src_ref=gain_sent.at[step],
            dst_ref=gain_got.at[step],
            send_sem=gain_send.at[step],
            recv_sem=gain_recv.at[step],
            device_id=(partners[step], lane),
            device_id_type=MESH,
        )

    def gain_step(step):
        if step == 0:
            for stream in range(4):
                gain_sent[0, stream : stream + 1, :] = jnp.sum(
                    gain_grad[stream], axis=0, keepdims=True
                )
        else:
            gain_copy(step - 1).wait_recv()
            total = gain_sent[step - 1] + gain_got[step - 1]
            if step == steps:
                gain_sum[...] = total
            else:
                gain_sent[step] = total
        if step < steps:
            gain_copy(step).start()

    tasks = []
    for at in range(blocks):
        tasks.append((0.02 + 0.03 * at, to_link, at))
        tasks.append((0.19 + 0.16 * at, to_twin, at))
        tasks.append((0.23 + 0.16 * at, ready, at))
        tasks.append((0.24 + 0.16 * at, mix_task, at))
    for step in range(steps + 1):
        tasks.append((0.87 + 0.12 * step / steps, gain_step, step))
    tasks.sort(key=lambda item: item[0])
    for hop in range(1, half + 1):
        if hop == half:
            flip(0, 0)
        else:

            @pl.loop(0, 2)
            def _(way):
                flip(way, (half - hop) * (1 - 2 * way))

        for piece in range(len(pieces)):
            passed = ((hop - 1.5 if hop > 1 else 0.0) + (piece + 1) / len(pieces) * (1 if hop > 1 else 0.5)) / (half - 0.5)
            cols = pl.ds(starts[piece], pieces[piece][2])

            @pl.loop(0, 2)
            def _(way):
                send(hop - 1, way, piece).wait_recv()

                def with_got(rows):
                    got = ring[hop - 1, way, rows, cols].astype(F32)
                    ring[hop - 1, way, rows, cols] = (term(way, piece, rows) + got).astype(BF16)

                def alone(rows):
                    ring[hop - 1, way, rows, cols] = term(way, piece, rows).astype(BF16)

                if hop == 1:
                    row_loop(way * cut, cut, with_got)
                    row_loop((1 - way) * cut, cut, alone)
                elif hop < half:
                    row_loop(0, shard, with_got)
                if hop < half:
                    send(hop, way, piece).start()

            if hop == half:

                def finish(rows):
                    total = (
                        term(0, piece, rows)
                        + ring[hop - 1, 0, rows, cols].astype(F32)
                        + ring[hop - 1, 1, rows, cols].astype(F32)
                    )
                    which, at, count = pieces[piece]
                    if which == 0:
                        grad_up[rows, at : at + count] = total.astype(BF16)
                    else:
                        grad_qkv[which - 1, rows, :] = total.astype(BF16)

                row_loop(0, shard, finish)
                grad_copy(piece).start()
            if hop == 1 and piece == early - 1:
                for late in range(early, len(pieces)):
                    for way in range(2):
                        send(0, way, late).start()
            while tasks and tasks[0][0] <= passed:
                _, run, value = tasks.pop(0)
                run(value)
    for _, run, value in tasks:
        run(value)
    for piece in range(len(pieces)):
        grad_copy(piece).wait()
    for slot in range(2):
        unit_store((blocks - 1) * block, slot).wait()
    for step in range(steps):
        gain_copy(step).wait_send()
    for hop in range(half):
        for piece in range(len(pieces)):
            for way in range(2):
                send(hop, way, piece).wait_send()


def back_stage(size, normed, hidden_grad, qkv_low, stats, mix, gains, parts, history, streams, out_total):
    half = size // 2
    tokens, hidden = hidden_grad.shape
    states, _, width = history.shape
    shard = normed.shape[3]
    local = qkv_low.shape[1] // 3
    cols = hidden + 3 * local
    count = (hidden // 512 if half <= 4 else 1) + 3
    blocks = tokens // 128
    steps = size.bit_length() - 1
    vmem = pl.BlockSpec(memory_space=pltpu.VMEM)
    hbm = pl.BlockSpec(memory_space=pl.ANY)
    dma = pltpu.SemaphoreType.DMA
    small = jax.ShapeDtypeStruct((shard, local), BF16)
    return pl.pallas_call(
        lambda *refs: back_kernel(size, *refs),
        in_specs=[vmem] * 3 + [hbm] * 7,
        out_specs=[vmem] * 2 + [hbm] * 5,
        out_shape=[
            jax.ShapeDtypeStruct((tokens, mix.shape[1]), F32),
            jax.ShapeDtypeStruct((4, width), F32),
            jax.ShapeDtypeStruct((shard, hidden), BF16),
            small,
            small,
            small,
            jax.ShapeDtypeStruct((4, tokens, width), BF16),
        ],
        scratch_shapes=[
            pltpu.VMEM(normed.shape, BF16),
            pltpu.VMEM((tokens, hidden), BF16),
            pltpu.VMEM((tokens, 3 * local), BF16),
            pltpu.VMEM((shard, hidden), BF16),
            pltpu.VMEM((3, shard, local), BF16),
            pltpu.VMEM((4, 8, width), F32),
            pltpu.VMEM((steps, 4, width), F32),
            pltpu.VMEM((steps, 4, width), F32),
            pltpu.VMEM((4, tokens, width), BF16),
            pltpu.VMEM((blocks, 4, 64, width), BF16),
            pltpu.VMEM((blocks, 4, 64, width), BF16),
            pltpu.VMEM((shard, cols), BF16),
            pltpu.VMEM((half, 2, shard, cols), BF16),
            pltpu.VMEM((2, states, UNIT, width), BF16),
            pltpu.VMEM((2, 4, UNIT, width), F32),
            pltpu.VMEM((2, UNIT, width), F32),
            pltpu.VMEM((2, 4, UNIT, width), BF16),
            pltpu.VMEM((4, GROUP, width), F32),
            pltpu.VMEM((2, 4, shard, tokens), BF16),
            dma((6,)),
            dma((count,)),
            dma((half, 2, count)),
            dma((half, 2, count)),
            dma((blocks,)),
            dma((blocks,)),
            dma((blocks,)),
            dma((blocks,)),
            dma((blocks,)),
            dma((blocks,)),
            dma(()),
            dma((2, 3)),
            dma((2,)),
            dma((steps,)),
            dma((steps,)),
            pltpu.SemaphoreType.REGULAR((blocks,)),
        ],
        cost_estimate=pl.CostEstimate(
            flops=tokens * width * 2000, bytes_accessed=tokens * width * 64, transcendentals=0
        ),
        compiler_params=pltpu.CompilerParams(
            collective_id=1, has_side_effects=True, vmem_limit_bytes=62 * MIB
        ),
        name="back_stage",
    )(stats, mix, gains, normed, hidden_grad, qkv_low, parts, history, streams, out_total)


TILE = 512


def unrotate(values, turn):
    return (
        values * turn[0]
        + pltpu.roll(values, HEAD_DIM - ROT // 2, 1) * turn[1]
        + pltpu.roll(values, ROT // 2, 1) * turn[2]
    )


def row_loop(base, count, run, step=128):
    step = min(step, count)

    @pl.loop(0, count // step)
    def _(at):
        run(pl.ds(pl.multiple_of(base + at * step, step), step))


def attention_probs(query, key, two, first):
    shape = (query.shape[0], key.shape[0])
    middle = key.shape[0] // 2
    scores = dot(query, key, ((1,), (1,))) * (HEAD_DIM ** (-0.5))
    row = first + lax.broadcasted_iota(jnp.int32, shape, 0)
    col = lax.broadcasted_iota(jnp.int32, shape, 1)
    apart = jnp.where(row >= middle, jnp.where(col < middle, two, 0), 0)
    scores = jnp.where(jnp.logical_or(apart != 0, col > row), -1e30, scores)
    weights = jnp.exp(scores - jnp.max(scores, axis=1, keepdims=True))
    return weights / jnp.sum(weights, axis=1, keepdims=True)


def mid_kernel(
    size,
    turn,
    two,
    gen_grad,
    gen_gain,
    gen_mid,
    low_t_in,
    grad_blocks_in,
    hidden_in,
    heads_in,
    low_all,
    up_full,
    qkv_full,
    gen_sum,
    mid_sum,
    grad_out,
    grad_down,
    hidden_grad_out,
    qkv_low_out,
    parts,
    low_t,
    grad_blocks,
    hidden,
    heads,
    low_sum,
    hidden_grad,
    qkv_low,
    attended_grad,
    far,
    ring,
    low_tile,
    up_tile,
    qkv_tile,
    stage,
    gen_sent,
    gen_got,
    mid_sent,
    mid_got,
    value_sum,
    key_sum,
    gen_all,
    slope_in,
    share_sem,
    in_sem,
    out_sem,
    ring_send,
    ring_recv,
    tile_sem,
    stage_sem,
    gen_send,
    gen_recv,
):
    half = size // 2
    rows_all, tokens = low_t.shape
    shard = grad_blocks.shape[2]
    local = heads.shape[1] // 3
    me = lax.axis_index("dp")
    lane = lax.axis_index("tensor")
    place = place_of(me, size)
    right = index_at(place + 1, size)
    left = index_at(place - 1, size)
    steps = size.bit_length() - 1
    partners = [me + (1 << step) * (1 - 2 * lax.rem(lax.div(me, 1 << step), 2)) for step in range(steps)]
    loads = [
        pltpu.make_async_copy(source, target, in_sem.at[at])
        for at, (source, target) in enumerate(
            ((low_t_in, low_t), (grad_blocks_in, grad_blocks), (hidden_in, hidden), (heads_in, heads))
        )
    ]
    for copy in loads:
        copy.start()
    core = lax.rem(lane, 2)
    chip = lax.div(lane, 2)
    twin = chip * 2 + 1 - core
    across = (1 - chip) * 2 + core
    barrier = pltpu.get_barrier_semaphore()
    for there in [(it, lane) for it in [right, left] + partners] + [(me, twin), (me, across)]:
        pl.semaphore_signal(barrier, inc=1, device_id=there, device_id_type=MESH)
    pl.semaphore_wait(barrier, 4 + steps)

    low_tiles = rows_all // TILE
    width_tiles = up_full.shape[0] // TILE
    order = (
        [("low", at) for at in range(low_tiles)]
        + [("up", at) for at in range(width_tiles)]
        + [("qkv", at) for at in range(width_tiles)]
    )

    def load(index):
        kind, at = order[index]
        slot = at % 2
        rows = pl.ds(at * TILE, TILE)
        if kind == "low":
            return pltpu.make_async_copy(low_all.at[:, rows, :], low_tile.at[slot], tile_sem.at[0, slot])
        if kind == "up":
            return pltpu.make_async_copy(up_full.at[rows, :], up_tile.at[slot], tile_sem.at[1, slot])
        return pltpu.make_async_copy(qkv_full.at[rows, :], qkv_tile.at[slot], tile_sem.at[2, slot])

    load(0).start()

    pieces = rows_all // TILE
    cut = TILE // 2

    def term(owner, rows):
        return jnp.dot(low_t[rows, :], grad_blocks[owner], preferred_element_type=F32)

    def send(hop, way, piece):
        if hop == 0:
            rows = pl.ds(pl.multiple_of(piece * TILE + way * cut, cut), cut)
            source = far.at[rows, :]
        else:
            rows = pl.ds(piece * TILE, TILE)
            source = ring.at[hop - 1, way, rows, :]
        return pltpu.make_async_remote_copy(
            src_ref=source,
            dst_ref=ring.at[hop, way, rows, :],
            send_sem=ring_send.at[hop, way, piece],
            recv_sem=ring_recv.at[hop, way, piece],
            device_id=(right + way * (left - right), lane),
            device_id_type=MESH,
        )

    for copy in loads[:2]:
        copy.wait()
    def far_term(piece):
        def far_rows(rows):
            far[rows, :] = term(index_at(place + half, size), rows).astype(BF16)

        row_loop(piece * TILE, TILE, far_rows)

    early = pieces // 2
    for piece in range(early):
        far_term(piece)
        for way in range(2):
            send(0, way, piece).start()
    for piece in range(early, pieces):
        far_term(piece)
    for copy in loads[2:]:
        copy.wait()

    def grad_copy(piece):
        base = piece * TILE
        source = low_sum.at[pl.ds(base, TILE), :]
        if base < local:
            target = grad_out.at[pl.ds(base, TILE), :]
        else:
            target = grad_down.at[pl.ds(base - local, TILE), :]
        return pltpu.make_async_copy(source, target, out_sem.at[2 + piece])

    def hidden_copy():
        return pltpu.make_async_copy(hidden_grad, hidden_grad_out, out_sem.at[0])

    def qkv_copy():
        return pltpu.make_async_copy(qkv_low, qkv_low_out, out_sem.at[1])

    def low_grad(at):
        index = at
        load(index + 1).start()
        load(index).wait()
        base = at * TILE

        def run(rows):
            total = None
            for owner in range(size):
                part = dot(grad_blocks[owner, rows, :], low_tile[at % 2, owner], ((1,), (1,)))
                total = part if total is None else total + part
            if base < local:
                attended_grad[rows, base : base + TILE] = total.astype(BF16)
            else:
                cols = slice(base - local, base - local + TILE)
                slope_in[: rows.size, :] = total

                @pl.loop(0, rows.size // 32)
                def _(part):
                    inner = pl.ds(pl.multiple_of(part * 32, 32), 32)
                    there = pl.ds(pl.multiple_of(rows.start + part * 32, 32), 32)
                    slope = gelu_slope(hidden[there, cols])
                    hidden_grad[there, cols] = (slope_in[inner, :] * slope).astype(BF16)

        row_loop(0, tokens, run, 256)
        if at + 1 == low_tiles:
            hidden_copy().start()

    def head_grad(head):
        cols = slice(head * HEAD_DIM, (head + 1) * HEAD_DIM)
        key_cols = slice(local + head * HEAD_DIM, local + (head + 1) * HEAD_DIM)
        value_cols = slice(2 * local + head * HEAD_DIM, 2 * local + (head + 1) * HEAD_DIM)
        scale = HEAD_DIM ** (-0.5)
        value_sum[...] = jnp.zeros_like(value_sum)
        key_sum[...] = jnp.zeros_like(key_sum)

        def run(rows):
            query, key, value = heads[rows, cols], heads[:, key_cols], heads[:, value_cols]
            upstream = attended_grad[rows, cols]
            probs = attention_probs(query, key, two[...], rows.start)
            probs_grad = dot(upstream, value, ((1,), (1,)))
            value_sum[...] += dot(probs.astype(BF16), upstream, ((0,), (0,)))
            row = jnp.sum(probs * probs_grad, axis=1, keepdims=True)
            scores_grad = (probs * (probs_grad - row)).astype(BF16)
            query_grad = dot(scores_grad, key, ((1,), (0,))) * scale
            turns = [turn[which, rows, :] for which in range(3)]
            qkv_low[rows, cols] = unrotate(query_grad, turns).astype(BF16)
            key_sum[...] += dot(scores_grad, query, ((0,), (0,)))

        row_loop(0, tokens, run)
        turns = [turn[which] for which in range(3)]
        qkv_low[:, value_cols] = value_sum[...].astype(BF16)
        qkv_low[:, key_cols] = unrotate(key_sum[...] * scale, turns).astype(BF16)
        if (head + 1) * HEAD_DIM == local:
            qkv_copy().start()

    def part_store(stream, at):
        return pltpu.make_async_copy(
            stage.at[stream], parts.at[stream, :, pl.ds(at * TILE, TILE)], stage_sem.at[stream]
        )

    def up_part(at):
        index = low_tiles + at
        load(index + 1).start()
        load(index).wait()
        if at:
            part_store(3, at - 1).wait()

        def run(rows):
            stage[3, rows, :] = dot(hidden_grad[rows, :], up_tile[at % 2], ((1,), (1,))).astype(BF16)

        row_loop(0, tokens, run, 256)
        part_store(3, at).start()

    def qkv_part(at):
        index = low_tiles + width_tiles + at
        if index + 1 < len(order):
            load(index + 1).start()
        load(index).wait()
        for stream in range(3):
            if at:
                part_store(stream, at - 1).wait()

        def run(rows):
            for stream in range(3):
                cols = slice(stream * local, (stream + 1) * local)
                stage[stream, rows, :] = dot(
                    qkv_low[rows, cols], qkv_tile[at % 2, :, cols], ((1,), (1,))
                ).astype(BF16)

        row_loop(0, tokens, run, 256)
        for stream in range(3):
            part_store(stream, at).start()

    def gen_copies(step):
        return [
            pltpu.make_async_remote_copy(
                src_ref=sent.at[step],
                dst_ref=got.at[step],
                send_sem=gen_send.at[step, which],
                recv_sem=gen_recv.at[step, which],
                device_id=(partners[step], lane),
                device_id_type=MESH,
            )
            for which, (sent, got) in enumerate(((gen_sent, gen_got), (mid_sent, mid_got)))
        ]

    quarter = gen_sent.shape[2]

    def share(which):
        if which == 0:
            cols = pl.ds(pl.multiple_of(lane * quarter, quarter), quarter)
            there = (me, twin)
        else:
            cols = pl.ds(pl.multiple_of(chip * 2 * quarter, 2 * quarter), 2 * quarter)
            there = (me, across)
        return pltpu.make_async_remote_copy(
            src_ref=gen_all.at[:, cols],
            dst_ref=gen_all.at[:, cols],
            send_sem=share_sem.at[0, which],
            recv_sem=share_sem.at[1, which],
            device_id=there,
            device_id_type=MESH,
        )

    def gen_step(step):
        cols = pl.ds(pl.multiple_of(lane * quarter, quarter), quarter)
        if step == 0:
            units = gen_grad.shape[0]
            gen_sent[0, :units, :] = gen_grad[:, cols].astype(BF16)
            gen_sent[0, units:, :] = jnp.broadcast_to(
                gen_gain[:, cols].astype(BF16), (gen_sent.shape[1] - units, quarter)
            )
            mid_sent[0] = gen_mid[...]
        elif step <= steps:
            for copy in gen_copies(step - 1):
                copy.wait_recv()
            total = gen_sent[step - 1].astype(F32) + gen_got[step - 1].astype(F32)
            mid_total = mid_sent[step - 1] + mid_got[step - 1]
            if step == steps:
                gen_all[:, cols] = total
                mid_sum[...] = mid_total
                share(0).start()
            else:
                gen_sent[step] = total.astype(BF16)
                mid_sent[step] = mid_total
        elif step == steps + 1:
            share(0).wait_recv()
            share(1).start()
        else:
            share(1).wait_recv()
            gen_sum[...] = gen_all[...]
        if step < steps:
            for copy in gen_copies(step):
                copy.start()

    tasks = [(low_grad, at) for at in range(low_tiles)]
    tasks += [(head_grad, head) for head in range(local // HEAD_DIM)]
    tasks += [(up_part, at) for at in range(width_tiles)]
    tasks += [(qkv_part, at) for at in range(width_tiles)]
    for step in range(steps + 3):
        tasks.insert(2 + 3 * step, (gen_step, step))
    count = len(tasks)
    slots = half * pieces
    slot = 0
    for hop in range(1, half + 1):
        for piece in range(pieces):

            @pl.loop(0, 2)
            def _(way):
                send(hop - 1, way, piece).wait_recv()
                owner = index_at(place + (half - hop) * (1 - 2 * way), size)

                def with_got(rows):
                    got = ring[hop - 1, way, rows, :].astype(F32)
                    ring[hop - 1, way, rows, :] = (term(owner, rows) + got).astype(BF16)

                def alone(rows):
                    ring[hop - 1, way, rows, :] = term(owner, rows).astype(BF16)

                if hop == 1:
                    row_loop(piece * TILE + way * cut, cut, with_got)
                    row_loop(piece * TILE + (1 - way) * cut, cut, alone)
                elif hop < half:
                    row_loop(piece * TILE, TILE, with_got)
                if hop < half:
                    send(hop, way, piece).start()

            if hop == half:

                def finish(rows):
                    low_sum[rows, :] = (
                        term(me, rows)
                        + ring[hop - 1, 0, rows, :].astype(F32)
                        + ring[hop - 1, 1, rows, :].astype(F32)
                    ).astype(BF16)

                row_loop(piece * TILE, TILE, finish)
                grad_copy(piece).start()
            if hop == 1 and piece == early - 1:
                for late in range(early, pieces):
                    for way in range(2):
                        send(0, way, late).start()
            slot += 1
            while tasks and (slot == slots or len(tasks) * (slots - 2) > count * max(slots - 2 - slot, 0)):
                run, value = tasks.pop(0)
                run(value)
    for stream in range(4):
        part_store(stream, width_tiles - 1).wait()
    hidden_copy().wait()
    qkv_copy().wait()
    for piece in range(pieces):
        grad_copy(piece).wait()
    for step in range(steps):
        for copy in gen_copies(step):
            copy.wait_send()
    for which in range(2):
        share(which).wait_send()
    for hop in range(half):
        for piece in range(pieces):
            for way in range(2):
                send(hop, way, piece).wait_send()


def mid_stage(
    size,
    low_t,
    grad_blocks,
    hidden,
    heads,
    turn,
    two,
    gen_grad,
    gen_gain,
    gen_mid,
    low_all,
    up_full,
    qkv_full,
):
    half = size // 2
    rows_all, tokens = low_t.shape
    shard = grad_blocks.shape[2]
    hidden_cols = hidden.shape[1]
    local = heads.shape[1] // 3
    width = up_full.shape[0]
    pieces = rows_all // TILE
    steps = size.bit_length() - 1
    units = gen_grad.shape[0]
    vmem = pl.BlockSpec(memory_space=pltpu.VMEM)
    hbm = pl.BlockSpec(memory_space=pl.ANY)
    dma = pltpu.SemaphoreType.DMA
    return pl.pallas_call(
        lambda *refs: mid_kernel(size, *refs),
        in_specs=[vmem] * 5 + [hbm] * 7,
        out_specs=[vmem] * 2 + [hbm] * 5,
        out_shape=[
            jax.ShapeDtypeStruct((units + 8, width), F32),
            jax.ShapeDtypeStruct(gen_mid.shape, F32),
            jax.ShapeDtypeStruct((local, shard), BF16),
            jax.ShapeDtypeStruct((hidden_cols, shard), BF16),
            jax.ShapeDtypeStruct((tokens, hidden_cols), BF16),
            jax.ShapeDtypeStruct((tokens, 3 * local), BF16),
            jax.ShapeDtypeStruct((4, tokens, width), BF16),
        ],
        scratch_shapes=[
            pltpu.VMEM((rows_all, tokens), BF16),
            pltpu.VMEM((size, tokens, shard), BF16),
            pltpu.VMEM((tokens, hidden_cols), F32),
            pltpu.VMEM((tokens, 3 * local), BF16),
            pltpu.VMEM((rows_all, shard), BF16),
            pltpu.VMEM((tokens, hidden_cols), BF16),
            pltpu.VMEM((tokens, 3 * local), BF16),
            pltpu.VMEM((tokens, local), BF16),
            pltpu.VMEM((rows_all, shard), BF16),
            pltpu.VMEM((half, 2, rows_all, shard), BF16),
            pltpu.VMEM((2, size, TILE, shard), BF16),
            pltpu.VMEM((2, TILE, hidden_cols), BF16),
            pltpu.VMEM((2, TILE, 3 * local), BF16),
            pltpu.VMEM((4, tokens, TILE), BF16),
            pltpu.VMEM((steps, units + 8, width // 4), BF16),
            pltpu.VMEM((steps, units + 8, width // 4), BF16),
            pltpu.VMEM((steps,) + gen_mid.shape, F32),
            pltpu.VMEM((steps,) + gen_mid.shape, F32),
            pltpu.VMEM((tokens, HEAD_DIM), F32),
            pltpu.VMEM((tokens, HEAD_DIM), F32),
            pltpu.VMEM((units + 8, width), F32),
            pltpu.VMEM((256, TILE), F32),
            dma((2, 2)),
            dma((4,)),
            dma((2 + pieces,)),
            dma((half, 2, pieces)),
            dma((half, 2, pieces)),
            dma((3, 2)),
            dma((4,)),
            dma((steps, 2)),
            dma((steps, 2)),
        ],
        cost_estimate=pl.CostEstimate(
            flops=tokens * width * 4000, bytes_accessed=tokens * width * 40, transcendentals=0
        ),
        compiler_params=pltpu.CompilerParams(
            collective_id=2, has_side_effects=True, vmem_limit_bytes=62 * MIB
        ),
        name="mid_stage",
    )(
        turn,
        two,
        gen_grad,
        gen_gain,
        gen_mid,
        low_t,
        grad_blocks,
        hidden,
        heads,
        low_all,
        up_full,
        qkv_full,
    )


def front_kernel(
    size,
    mix_in,
    gains,
    segments,
    frequency,
    history,
    w_query,
    w_key,
    w_value,
    w_up,
    w_out,
    w_down,
    stats,
    branch,
    mix,
    turn,
    two,
    heads_out,
    hidden_out,
    low_t_out,
    normed_out,
    streams,
    qkv_all,
    up_all,
    low_all,
    heads,
    hidden,
    low_t,
    normed,
    low,
    weight_tile,
    low_tile,
    state_in,
    stream_out,
    from_core,
    from_link,
    qkv_send,
    qkv_recv,
    up_send,
    up_recv,
    low_send,
    low_recv,
    own_sem,
    state_sem,
    stream_sem,
    normed_sem,
    out_sem,
    weight_sem,
    tile_sem,
    core_send,
    core_recv,
    link_send,
    link_recv,
    twin_send,
    twin_recv,
    freed,
):
    half = size // 2
    states, tokens, width = history.shape
    shard = width // size
    local = w_query.shape[1]
    hidden_cols = w_up.shape[1]
    inverse = 1.0 / width
    me = lax.axis_index("dp")
    lane = lax.axis_index("tensor")
    place = place_of(me, size)
    right = index_at(place + 1, size)
    left = index_at(place - 1, size)
    core = lax.rem(lane, 2)
    chip = lax.div(lane, 2)
    twin = chip * 2 + 1 - core
    across = (1 - chip) * 2 + core
    rows_half = tokens // 2

    barrier = pltpu.get_barrier_semaphore()
    for there in ((right, lane), (left, lane), (me, twin), (me, across)):
        pl.semaphore_signal(barrier, inc=1, device_id=there, device_id_type=MESH)
    pl.semaphore_wait(barrier, 4)

    wide = TILE
    groups = [
        [(w_query, 0, 0), (w_key, 0, local), (w_value, 0, 2 * local)],
        [(w_up, at, at) for at in range(0, hidden_cols, wide)],
        [(w_out, at, at) for at in range(0, local, wide)]
        + [(w_down, at, local + at) for at in range(0, hidden_cols, wide)],
    ]
    sems = [(qkv_send, qkv_recv), (up_send, up_recv), (low_send, low_recv)]
    cut = (shard // 2, shard // 2, wide // 2)

    def own(group, piece, lo, count):
        source, at, _ = groups[group][piece]
        if group == 2:
            return source.at[pl.ds(at + lo, count), :]
        cols = local if group == 0 else wide
        return source.at[pl.ds(lo, count), pl.ds(at, cols)]

    def held(group, piece, owner, lo, count):
        _, _, at = groups[group][piece]
        if group == 2:
            return low_all.at[owner, pl.ds(at + lo, count), :]
        rows = pl.ds(pl.multiple_of(owner * shard + lo, cut[0]), count)
        if group == 0:
            return qkv_all.at[rows, pl.ds(at, local)]
        return up_all.at[rows, pl.ds(at, wide)]

    def send(group, hop, way, piece):
        owner = index_at(place + (hop - 1) * (2 * way - 1), size)
        whole = shard if group < 2 else wide
        lo, count = (0, whole) if hop < half else (way * cut[group], cut[group])
        target = held(group, piece, owner, lo, count)
        source = own(group, piece, lo, count) if hop == 1 else target
        send_sem, recv_sem = sems[group]
        return pltpu.make_async_remote_copy(
            src_ref=source,
            dst_ref=target,
            send_sem=send_sem.at[hop - 1, way, piece],
            recv_sem=recv_sem.at[hop - 1, way, piece],
            device_id=((right, left)[way], lane),
            device_id_type=MESH,
        )

    def own_copies(group):
        whole = shard if group < 2 else wide
        return [
            pltpu.make_async_copy(
                own(group, piece, 0, whole), held(group, piece, me, 0, whole), own_sem.at[group, piece]
            )
            for piece in range(len(groups[group]))
        ]

    units = tokens // UNIT

    def state_load(unit):
        rows = pl.ds(pl.multiple_of(unit * UNIT, UNIT), UNIT)
        slot = lax.rem(unit, 2)
        return pltpu.make_async_copy(history.at[:, rows, :], state_in.at[slot], state_sem.at[slot])

    def stream_store(unit):
        rows = pl.ds(pl.multiple_of(unit * UNIT, UNIT), UNIT)
        slot = lax.rem(unit, 2)
        return pltpu.make_async_copy(stream_out.at[slot], streams.at[:, rows, :], stream_sem.at[slot])

    per_task = 4

    def tables():
        count = mix_in.shape[0]
        padded = -(-count // 8) * 8
        mix[...] = jnp.concatenate(
            [mix_in[...], jnp.zeros((padded - count, tokens), F32)], axis=0
        ).T
        two[...] = jnp.broadcast_to(segments[0:1, tokens - 1 : tokens], (1, tokens))
        row = lax.broadcasted_iota(jnp.int32, (tokens, HEAD_DIM), 0)
        lanes = lax.broadcasted_iota(jnp.int32, (tokens, HEAD_DIM), 1)
        flag = jnp.broadcast_to(segments[0:1, tokens - 1 : tokens], (tokens, HEAD_DIM))
        place_in = row - jnp.where(row >= tokens // 2, jnp.where(flag != 0, tokens // 2, 0), 0)
        angles = place_in.astype(F32) * frequency[...]
        sine = jnp.sin(angles)
        turn[0] = jnp.cos(angles)
        turn[1] = jnp.where(lanes < ROT // 2, sine, 0.0)
        turn[2] = jnp.where(lanes < ROT // 2, 0.0, -sine)

    def out_copies():
        return [
            pltpu.make_async_copy(source, target, out_sem.at[at])
            for at, (source, target) in enumerate(
                ((heads, heads_out), (hidden, hidden_out), (low_t, low_t_out))
            )
        ]

    def mix_task(task):
        @pl.loop(0, per_task)
        def _(which):
            mix_unit(task * per_task + which, task)

        if (task + 1) * per_task == units:
            normed_store().start()

    def mix_unit(unit, task):
        slot = lax.rem(unit, 2)

        @pl.when(unit + 1 < units)
        def _():
            state_load(unit + 1).start()

        state_load(unit).wait()
        if task > 0:
            stream_store(unit - 2).wait()
        else:

            @pl.when(unit >= 2)
            def _():
                stream_store(unit - 2).wait()

        @pl.loop(0, UNIT // GROUP)
        def _(step):
            rows = pl.ds(pl.multiple_of(unit * UNIT + step * GROUP, GROUP), GROUP)
            inner = pl.ds(pl.multiple_of(step * GROUP, GROUP), GROUP)
            weights = mix[rows, :]

            sums = [jnp.zeros((GROUP, 128), F32) for _ in range(4)]
            for at in range(0, width, CHUNK):
                cols = pl.ds(at, CHUNK)
                total = [None] * 4
                for source in range(states):
                    state = state_in[slot, source, inner, cols].astype(F32)
                    for stream in range(4):
                        k = stream * states + source
                        term = weights[:, k : k + 1] * state
                        total[stream] = term if source == 0 else total[stream] + term
                for stream in range(4):
                    stream_out[slot, stream, inner, cols] = total[stream]
                    for at_lane in range(0, CHUNK, 128):
                        sums[stream] = sums[stream] + total[stream][:, at_lane : at_lane + 128]
            for stream in range(4):
                mean = jnp.sum(sums[stream], axis=1, keepdims=True) * inverse
                square = jnp.zeros((GROUP, 128), F32)
                for at in range(0, width, CHUNK):
                    center = stream_out[slot, stream, inner, pl.ds(at, CHUNK)] - mean
                    center = center * center
                    for at_lane in range(0, CHUNK, 128):
                        square = square + center[:, at_lane : at_lane + 128]
                scale = lax.rsqrt(jnp.sum(square, axis=1, keepdims=True) * inverse + EPSILON)
                stats[rows, stream : stream + 1] = mean
                stats[rows, 4 + stream : 5 + stream] = scale
                for at in range(0, width, CHUNK):
                    cols = pl.ds(at, CHUNK)
                    center = stream_out[slot, stream, inner, cols] - mean
                    value = (center * scale * gains[stream : stream + 1, cols]).astype(BF16)
                    for owner in range(at // shard, (at + CHUNK) // shard):
                        base = owner * shard - at
                        normed[stream, owner, rows, :] = value[:, base : base + shard]

        stream_store(unit).start()

    def normed_store():
        return pltpu.make_async_copy(normed, normed_out, normed_sem)

    tiles = 3 + hidden_cols // wide

    def weight_load(tile):
        if tile < 3:
            source = qkv_all.at[:, pl.ds(tile * local, local)]
        else:
            source = up_all.at[:, pl.ds((tile - 3) * wide, wide)]
        return pltpu.make_async_copy(source, weight_tile.at[tile % 2], weight_sem.at[tile % 2])

    def arrived(group):
        for copy in own_copies(group):
            copy.wait()
        for piece in range(len(groups[group])):
            for way in range(2):
                send(group, half, way, piece).wait_recv()

    def tile_product(tile, stream, rows):
        total = None
        for owner in range(size):
            part = jnp.dot(
                normed[stream, owner, rows, :],
                weight_tile[tile % 2, owner * shard : (owner + 1) * shard, :],
                preferred_element_type=F32,
            )
            total = part if total is None else total + part
        return total

    def qkv_task(which):
        if which == 0:
            arrived(0)
            weight_load(0).start()
        if which < 2:
            weight_load(which + 1).start()
        weight_load(which).wait()

        def run(rows):
            product = tile_product(which, which, rows)
            for head in range(local // HEAD_DIM):
                at = head * HEAD_DIM
                part = product[:, at : at + HEAD_DIM]
                if which < 2:
                    part = (
                        part * turn[0, rows, :]
                        - pltpu.roll(part, HEAD_DIM - ROT // 2, 1) * turn[1, rows, :]
                        - pltpu.roll(part, ROT // 2, 1) * turn[2, rows, :]
                    )
                heads[rows, which * local + at : which * local + at + HEAD_DIM] = part.astype(BF16)

        row_loop(0, tokens, run, 64)

    def head_task(pair):
        @pl.loop(0, 2)
        def _(which):
            at = pl.multiple_of((2 * pair + which) * HEAD_DIM, HEAD_DIM)
            query_cols, key_cols, value_cols = (
                pl.ds(pl.multiple_of(part * local + at, HEAD_DIM), HEAD_DIM) for part in range(3)
            )

            def run(rows):
                probs = attention_probs(
                    heads[rows, query_cols], heads[:, key_cols], two[...], rows.start
                ).astype(BF16)
                attended = jnp.dot(probs, heads[:, value_cols], preferred_element_type=F32)
                low[rows, query_cols] = attended.astype(BF16)
                low_t[query_cols, rows] = attended.T.astype(BF16)

            row_loop(0, tokens, run, 128)

    def up_task(at):
        if at == 0:
            arrived(1)
            weight_load(3).start()
        if at + 1 < tiles - 3:
            weight_load(4 + at).start()
        weight_load(3 + at).wait()
        cols = slice(at * wide, (at + 1) * wide)
        low_cols = slice(local + at * wide, local + (at + 1) * wide)

        def run(rows):
            product = tile_product(3 + at, 3, rows)
            hidden[rows, cols] = product

            @pl.loop(0, rows.size // 32)
            def _(part):
                there = pl.ds(pl.multiple_of(rows.start + part * 32, 32), 32)
                low[there, low_cols] = gelu(hidden[there, cols]).astype(BF16)

            low_t[low_cols, rows] = low[rows, low_cols].T

        row_loop(0, tokens, run)
        if at + 1 == tiles - 3:
            for copy in out_copies():
                copy.start()

    distances = [0]
    for hop in range(1, half):
        distances += [-hop, hop]
    distances += [half]

    def tile_load(index):
        owner = index_at(place + distances[index], size)
        return pltpu.make_async_copy(low_all.at[owner], low_tile.at[index % 2], tile_sem.at[index % 2])

    def mine(index):
        return pl.ds(pl.multiple_of(core * rows_half, rows_half), rows_half)

    def core_copy(index):
        owner = index_at(place + distances[index], size)
        rows = pl.ds(pl.multiple_of((1 - core) * rows_half, rows_half), rows_half)
        return pltpu.make_async_remote_copy(
            src_ref=branch.at[owner, rows, :],
            dst_ref=from_core.at[index],
            send_sem=core_send.at[index],
            recv_sem=core_recv.at[index],
            device_id=(me, twin),
            device_id_type=MESH,
        )

    def link_copy(index):
        owner = index_at(place + distances[index], size)
        return pltpu.make_async_remote_copy(
            src_ref=branch.at[owner, mine(index), :],
            dst_ref=from_link.at[index],
            send_sem=link_send.at[index],
            recv_sem=link_recv.at[index],
            device_id=(me, across),
            device_id_type=MESH,
        )

    def twin_copy(index):
        owner = index_at(place + distances[index], size)
        return pltpu.make_async_remote_copy(
            src_ref=branch.at[owner, mine(index), :],
            dst_ref=branch.at[owner, mine(index), :],
            send_sem=twin_send.at[index],
            recv_sem=twin_recv.at[index],
            device_id=(me, twin),
            device_id_type=MESH,
        )

    def low_task(index):
        if index == 0:
            for copy in own_copies(2):
                copy.wait()
        owner = index_at(place + distances[index], size)
        load = tile_load(index)
        load.start()
        load.wait()

        def run(rows):
            branch[owner, rows, :] = jnp.dot(
                low[rows, :], low_tile[index % 2], preferred_element_type=F32
            ).astype(BF16)

        row_loop(0, tokens, run)
        core_copy(index).start()

    def add_into(index, other):
        owner = index_at(place + distances[index], size)
        rows = mine(index)
        branch[owner, rows, :] = (
            branch[owner, rows, :].astype(F32) + other[index].astype(F32)
        ).astype(BF16)

    def link_task(index):
        copy = core_copy(index)
        copy.wait_send()
        pl.semaphore_signal(freed.at[index], inc=1, device_id=(me, twin), device_id_type=MESH)
        copy.wait_recv()
        add_into(index, from_core)
        link_copy(index).start()

    def twin_task(index):
        copy = link_copy(index)
        copy.wait_send()
        copy.wait_recv()
        add_into(index, from_link)
        pl.semaphore_wait(freed.at[index], 1)
        twin_copy(index).start()

    state_load(0).start()
    slots = [(group, hop) for group in range(3) for hop in range(1, half + 1)]
    counts = [len(pieces) for pieces in groups]
    first = [0, counts[0] * half, (counts[0] + counts[1]) * half]
    total_slots = sum(counts) * half
    tasks = []
    mixes = units // per_task
    for task in range(mixes):
        tasks.append((counts[0] - 1 + task * (first[1] - counts[0]) / mixes, mix_task, task))
    early = first[1] + counts[1]
    for which in range(3):
        tasks.append((early + which, qkv_task, which))
    for pair in range(local // HEAD_DIM // 2):
        tasks.append((early + 3 + 2 * pair, head_task, pair))
    middle = first[2] + counts[2]
    for at in range(tiles - 3):
        tasks.append((middle + at, up_task, at))
    for index in range(len(distances) - 1):
        due = max(first[2] + counts[2] * (abs(distances[index]) + 1) - 1, middle + tiles - 3) + 0.5 * (index % 2)
        tasks.append((due, low_task, index))
        tasks.append((due + 1, link_task, index))
        tasks.append((due + 3, twin_task, index))
    tasks.sort(key=lambda item: item[0])

    at_slot = 0
    for group, hop in slots:
        if hop == 1:
            for copy in own_copies(group):
                copy.start()
        for piece in range(counts[group]):
            for way in range(2):
                if hop > 1:
                    send(group, hop - 1, way, piece).wait_recv()
                send(group, hop, way, piece).start()
            if at_slot == 0:
                tables()
            while tasks and tasks[0][0] <= at_slot and at_slot < total_slots - 1:
                _, run, value = tasks.pop(0)
                run(value)
            at_slot += 1
    for _, run, value in tasks:
        run(value)
    for piece in range(counts[2]):
        for way in range(2):
            send(2, half, way, piece).wait_recv()
    last = len(distances) - 1
    low_task(last)
    link_task(last)
    twin_task(last)
    for index in range(len(distances)):
        copy = twin_copy(index)
        copy.wait_send()
        copy.wait_recv()
    for unit in range(units - 2, units):
        stream_store(unit).wait()
    normed_store().wait()
    for copy in out_copies():
        copy.wait()
    for group, hop in slots:
        for piece in range(counts[group]):
            for way in range(2):
                send(group, hop, way, piece).wait_send()


def front_stage(size, mix, gains, segments, frequency, history, w_query, w_key, w_value, w_up, w_out, w_down):
    half = size // 2
    states, tokens, width = history.shape
    shard = width // size
    local = w_query.shape[1]
    hidden_cols = w_up.shape[1]
    rows_all = local + hidden_cols
    vmem = pl.BlockSpec(memory_space=pltpu.VMEM)
    hbm = pl.BlockSpec(memory_space=pl.ANY)
    dma = pltpu.SemaphoreType.DMA
    up_pieces = hidden_cols // TILE
    low_pieces = rows_all // TILE
    return pl.pallas_call(
        lambda *refs: front_kernel(size, *refs),
        in_specs=[vmem] * 4 + [hbm] * 7,
        out_specs=[vmem] * 5 + [hbm] * 8,
        out_shape=[
            jax.ShapeDtypeStruct((tokens, 8), F32),
            jax.ShapeDtypeStruct((size, tokens, shard), BF16),
            jax.ShapeDtypeStruct((tokens, -(-mix.shape[0] // 8) * 8), F32),
            jax.ShapeDtypeStruct((3, tokens, HEAD_DIM), F32),
            jax.ShapeDtypeStruct((1, tokens), jnp.int32),
            jax.ShapeDtypeStruct((tokens, 3 * local), BF16),
            jax.ShapeDtypeStruct((tokens, hidden_cols), F32),
            jax.ShapeDtypeStruct((rows_all, tokens), BF16),
            jax.ShapeDtypeStruct((4, size, tokens, shard), BF16),
            jax.ShapeDtypeStruct((4, tokens, width), F32),
            jax.ShapeDtypeStruct((width, 3 * local), BF16),
            jax.ShapeDtypeStruct((width, hidden_cols), BF16),
            jax.ShapeDtypeStruct((size, rows_all, shard), BF16),
        ],
        scratch_shapes=[
            pltpu.VMEM((tokens, 3 * local), BF16),
            pltpu.VMEM((tokens, hidden_cols), F32),
            pltpu.VMEM((rows_all, tokens), BF16),
            pltpu.VMEM((4, size, tokens, shard), BF16),
            pltpu.VMEM((tokens, rows_all), BF16),
            pltpu.VMEM((2, width, TILE), BF16),
            pltpu.VMEM((2, rows_all, shard), BF16),
            pltpu.VMEM((2, states, UNIT, width), BF16),
            pltpu.VMEM((2, 4, UNIT, width), F32),
            pltpu.VMEM((size, tokens // 2, shard), BF16),
            pltpu.VMEM((size, tokens // 2, shard), BF16),
            dma((half, 2, 3)),
            dma((half, 2, 3)),
            dma((half, 2, up_pieces)),
            dma((half, 2, up_pieces)),
            dma((half, 2, low_pieces)),
            dma((half, 2, low_pieces)),
            dma((3, low_pieces)),
            dma((2,)),
            dma((2,)),
            dma(()),
            dma((3,)),
            dma((2,)),
            dma((2,)),
            dma((size,)),
            dma((size,)),
            dma((size,)),
            dma((size,)),
            dma((size,)),
            dma((size,)),
            pltpu.SemaphoreType.REGULAR((size,)),
        ],
        cost_estimate=pl.CostEstimate(
            flops=tokens * width * 8000, bytes_accessed=tokens * width * 80, transcendentals=0
        ),
        compiler_params=pltpu.CompilerParams(
            collective_id=3, has_side_effects=True, vmem_limit_bytes=62 * MIB
        ),
        name="front_stage",
    )(mix, gains, segments, frequency, history, w_query, w_key, w_value, w_up, w_out, w_down)


def finish_kernel(count, mix, grads, mix_grad, gain_sum, gen_gain, *refs):
    sources = refs[:count]
    history_grad, mix_out, gain_out = refs[count : count + 3]
    targets = refs[count + 3 : 2 * count + 3]
    spread = refs[2 * count + 3]
    states, tokens, width = history_grad.shape
    step = pl.program_id(0)
    for source, target in zip(sources, targets):
        target[...] = source[...].astype(F32)

    @pl.when(step == 0)
    def _():
        gain_out[:4, :] = gain_sum[...]
        gain_out[4:5, :] = gen_gain[0:1, :]
        mix_out[...] = mix_grad[...].T[: mix_out.shape[0], :]

    own = lax.broadcasted_iota(jnp.int32, (tokens, tokens), 0) == lax.broadcasted_iota(
        jnp.int32, (tokens, tokens), 1
    )
    weights = mix[...]
    for source in range(states):
        parts = [
            jnp.where(own, weights[:, stream * states + source : stream * states + source + 1], 0.0)
            for stream in range(4)
        ]
        spread[source * tokens : (source + 1) * tokens, :] = jnp.concatenate(parts, axis=1).astype(BF16)

    @pl.loop(0, width // 512)
    def _(at):
        cols = pl.ds(pl.multiple_of(at * 512, 512), 512)
        grad = jnp.concatenate([grads[stream, :, cols] for stream in range(4)], axis=0)
        mixed = jnp.dot(spread[...], grad, preferred_element_type=F32)
        for source in range(states):
            history_grad[source, :, cols] = mixed[source * tokens : (source + 1) * tokens].astype(BF16)


def finish_stage(states, mixes, mix, grads, mix_grad, gain_sum, gen_sum, sources, block=64):
    _, tokens, width = grads.shape
    steps = tokens // block
    row = lambda i: (i, 0)
    passed = [pl.BlockSpec((source.shape[0] // steps, source.shape[1]), row) for source in sources]
    fixed = lambda i: (0, 0)
    units = gen_sum.shape[0] - 8
    return pl.pallas_call(
        lambda *refs: finish_kernel(len(sources), *refs),
        grid=(steps,),
        in_specs=[
            pl.BlockSpec((block, mix.shape[1]), lambda i: (i, 0)),
            pl.BlockSpec((4, block, width), lambda i: (0, i, 0)),
            pl.BlockSpec(mix_grad.shape, fixed),
            pl.BlockSpec(gain_sum.shape, fixed),
            pl.BlockSpec((8, width), lambda i: (units // 8, 0)),
        ]
        + passed,
        out_specs=[
            pl.BlockSpec((states, block, width), lambda i: (0, i, 0)),
            pl.BlockSpec((mixes, tokens), fixed),
            pl.BlockSpec((5, width), fixed),
        ]
        + passed,
        out_shape=[
            jax.ShapeDtypeStruct((states, tokens, width), BF16),
            jax.ShapeDtypeStruct((mixes, tokens), F32),
            jax.ShapeDtypeStruct((5, width), F32),
        ]
        + [jax.ShapeDtypeStruct(source.shape, F32) for source in sources],
        scratch_shapes=[
            pltpu.VMEM((states * block, 4 * block), BF16),
        ],
        cost_estimate=pl.CostEstimate(
            flops=tokens * width * 72, bytes_accessed=tokens * width * 26, transcendentals=0
        ),
        compiler_params=pltpu.CompilerParams(vmem_limit_bytes=62 * MIB),
        name="finish_stage",
    )(mix, grads, mix_grad, gain_sum, gen_sum, *sources)


def body(
    sizes,
    history,
    mix_weights,
    segments,
    norm_gains,
    w_query,
    w_key,
    w_value,
    w_out,
    w_up,
    w_down,
    gen_in,
    gen_out,
    out_grad,
    next_grad,
):
    dp_size, tensor_size = sizes
    places = np.arange(HEAD_DIM)
    frequency = np.where(
        places < ROT, np.float32(ROPE_BASE) ** (-2.0 * (places % (ROT // 2)).astype(np.float32) / ROT), 0.0
    ).astype(np.float32)
    stats, branch, mix_rows, turn, two, heads, hidden, low_t, normed, streams, full_qkv, full_up, low_all = front_stage(
        dp_size,
        mix_weights,
        norm_gains,
        segments[None, :],
        jnp.asarray(frequency)[None, :],
        history,
        w_query,
        w_key,
        w_value,
        w_up,
        w_out,
        w_down,
    )
    layer_out, next_mix, out_total, branch_grad, gain_gen_grad, grad_gen_in, grad_gen_out = gen_stage(
        dp_size, streams, branch, norm_gains, gen_in.T, gen_out, out_grad, next_grad
    )

    gen_units, gen_next = gen_out.shape
    gen_sum, mid_sum, grad_out, grad_down, hidden_grad, qkv_low, parts = mid_stage(
        dp_size,
        low_t,
        branch_grad,
        hidden,
        heads,
        turn,
        two,
        grad_gen_in,
        gain_gen_grad,
        grad_gen_out,
        low_all,
        full_up,
        full_qkv,
    )
    mix_grad, gain_sums, grad_up, grad_query, grad_key, grad_value, stream_grad = back_stage(
        dp_size,
        normed,
        hidden_grad,
        qkv_low,
        stats,
        mix_rows,
        norm_gains,
        parts,
        history,
        streams,
        out_total,
    )
    history_grad, mix_grad, grad_gains, grad_up, grad_query, grad_key, grad_value, grad_out, grad_down = finish_stage(
        history.shape[0],
        mix_weights.shape[0],
        mix_rows,
        stream_grad,
        mix_grad,
        gain_sums,
        gen_sum,
        (grad_up, grad_query, grad_key, grad_value, grad_out, grad_down),
    )
    return (
        layer_out,
        next_mix,
        history_grad,
        mix_grad,
        grad_gains,
        grad_query,
        grad_key,
        grad_value,
        grad_out,
        grad_up,
        grad_down,
        gen_sum[:gen_units].T,
        mid_sum[:, :gen_next],
    )


def solution(mesh):
    sizes = (mesh.shape["dp"], mesh.shape["tensor"])
    in_specs = (
        P(None, "dp", None),
        P(None, "dp"),
        P("dp"),
        P(),
        P("dp", "tensor"),
        P("dp", "tensor"),
        P("dp", "tensor"),
        P("tensor", "dp"),
        P("dp", "tensor"),
        P("tensor", "dp"),
        P(),
        P(),
        P("dp", None),
        P(None, "dp"),
    )
    out_specs = (
        P("dp", None),
        P(None, "dp"),
        P(None, "dp", None),
        P(None, "dp"),
        P(),
        P("dp", "tensor"),
        P("dp", "tensor"),
        P("dp", "tensor"),
        P("tensor", "dp"),
        P("dp", "tensor"),
        P("tensor", "dp"),
        P(),
        P(),
    )

    def step(*arrays):
        return body(sizes, *arrays)

    return jax.shard_map(step, mesh=mesh, in_specs=in_specs, out_specs=out_specs, check_vma=False)
```

```python
import jax
import jax.numpy as jnp
import numpy as np
from jax import lax
from jax.experimental import pallas as pl
from jax.experimental.pallas import tpu as pltpu
from jax.sharding import PartitionSpec as P

HEAD_DIM = 128
ROT = 32


EPSILON = 1e-05
ROPE_BASE = 10000.0

F32 = jnp.float32
BF16 = jnp.bfloat16


MIB = 1 << 20
GROUP = 16
CHUNK = 512


def gelu(x):
    return 0.5 * x * (1.0 + lax.erf(x * (0.5**0.5)))


def gelu_slope(x):
    return 0.5 * (1.0 + lax.erf(x * (0.5**0.5))) + x * jnp.exp(-0.5 * x * x) * 0.3989422804014327


def dot(a, b, dims):
    return lax.dot_general(a, b, (dims, ((), ())), preferred_element_type=F32)


def gen_kernel(stream, branch, gain, gen_in, gen_out, out_grad, next_grad, layer_out, next_mix, branch_grad, gain_grad, in_grad, mid_grad):
    first = pl.program_id(0) == 0
    x = stream[0] + jnp.concatenate([branch[owner] for owner in range(branch.shape[0])], axis=1).astype(F32)
    layer_out[...] = x.astype(BF16)
    center = x - jnp.mean(x, axis=1, keepdims=True)
    scale = lax.rsqrt(jnp.mean(center * center, axis=1, keepdims=True) + EPSILON)
    unit = center * scale
    gains = gain[4:5, :]
    low = (unit * gains).astype(BF16)
    hidden = dot(low, gen_in[...], ((1,), (1,)))
    active = gelu(hidden).astype(BF16)
    next_mix[...] = dot(active, gen_out[...], ((1,), (0,))).T
    upstream = next_grad[...].T.astype(BF16)
    active_grad = dot(upstream, gen_out[...], ((1,), (1,)))
    hidden_grad = (active_grad * gelu_slope(hidden)).astype(BF16)
    y = dot(hidden_grad, gen_in[...], ((1,), (0,)))
    e = y * gains
    grad = scale * (
        e - jnp.mean(e, axis=1, keepdims=True) - unit * jnp.mean(e * unit, axis=1, keepdims=True)
    )
    total = out_grad[...].astype(F32) + grad
    low_total = total.astype(BF16)
    shard = branch_grad.shape[2]
    for owner in range(branch_grad.shape[0]):
        branch_grad[owner] = low_total[:, owner * shard : (owner + 1) * shard]
    gain_part = jnp.sum(y * unit, axis=0, keepdims=True)
    in_part = dot(hidden_grad, low, ((0,), (0,)))
    mid_part = dot(active, upstream, ((0,), (0,)))

    @pl.when(first)
    def _():
        gain_grad[...] = gain_part
        in_grad[...] = in_part
        mid_grad[...] = jnp.zeros_like(mid_grad)
        mid_grad[:, : mid_part.shape[1]] = mid_part

    @pl.when(jnp.logical_not(first))
    def _():
        gain_grad[...] += gain_part
        in_grad[...] += in_part
        mid_grad[:, : mid_part.shape[1]] += mid_part


def gen_stage(size, streams, branch, gains, gen_in, gen_out, out_grad, next_grad, block=128):
    _, tokens, width = streams.shape
    units = gen_in.shape[0]
    nxt = gen_out.shape[1]
    row = lambda i: (i, 0)
    fixed = lambda i: (0, 0)
    return pl.pallas_call(
        gen_kernel,
        grid=(tokens // block,),
        in_specs=[
            pl.BlockSpec((1, block, width), lambda i: (3, i, 0)),
            pl.BlockSpec((size, block, width // size), lambda i: (0, i, 0)),
            pl.BlockSpec(gains.shape, fixed),
            pl.BlockSpec(gen_in.shape, fixed),
            pl.BlockSpec(gen_out.shape, fixed),
            pl.BlockSpec((block, width), row),
            pl.BlockSpec((nxt, block), lambda i: (0, i)),
        ],
        out_specs=[
            pl.BlockSpec((block, width), row),
            pl.BlockSpec((nxt, block), lambda i: (0, i)),
            pl.BlockSpec((size, block, width // size), lambda i: (0, i, 0)),
            pl.BlockSpec((1, width), fixed),
            pl.BlockSpec((units, width), fixed),
            pl.BlockSpec((units, 128), fixed),
        ],
        out_shape=[
            jax.ShapeDtypeStruct((tokens, width), BF16),
            jax.ShapeDtypeStruct((nxt, tokens), F32),
            jax.ShapeDtypeStruct((size, tokens, width // size), BF16),
            jax.ShapeDtypeStruct((1, width), F32),
            jax.ShapeDtypeStruct((units, width), F32),
            jax.ShapeDtypeStruct((units, 128), F32),
        ],
        cost_estimate=pl.CostEstimate(
            flops=tokens * width * 300, bytes_accessed=tokens * width * 16, transcendentals=0
        ),
        compiler_params=pltpu.CompilerParams(vmem_limit_bytes=62 * MIB),
        name="gen_stage",
    )(streams, branch, gains, gen_in, gen_out, out_grad, next_grad)


MESH = pl.DeviceIdType.MESH


def place_of(me, size):
    odd = lax.rem(me, 2)
    at = lax.div(me, 2)
    return (1 - odd) * at + odd * (size - 1 - at)


def index_at(place, size):
    at = lax.rem(place + 2 * size, size)
    back = lax.div(at, size // 2)
    return (1 - back) * 2 * at + back * (2 * (size - 1 - at) + 1)


UNIT = 32


def back_kernel(
    size,
    stats,
    mix,
    gains,
    normed_in,
    hidden_grad_in,
    qkv_low_in,
    parts_in,
    history,
    streams,
    out_total,
    mix_grad,
    gain_sum,
    grad_up_out,
    grad_query_out,
    grad_key_out,
    grad_value_out,
    stream_grad,
    normed,
    hidden_grad,
    qkv_low,
    grad_up,
    grad_qkv,
    gain_grad,
    gain_sent,
    gain_got,
    parts,
    from_core,
    from_link,
    far,
    ring,
    state_in,
    stream_in,
    total_in,
    grad_out,
    held,
    flipped,
    in_sem,
    out_sem,
    ring_send,
    ring_recv,
    core_send,
    core_recv,
    link_send,
    link_recv,
    twin_send,
    twin_recv,
    load_sem,
    unit_sem,
    store_sem,
    gain_send,
    gain_recv,
    freed,
):
    half = size // 2
    shard = normed.shape[3]
    cut = shard // 2
    tokens, hidden_cols = hidden_grad.shape
    width = history.shape[2]
    inverse = 1.0 / width
    states = history.shape[0]
    me = lax.axis_index("dp")
    lane = lax.axis_index("tensor")
    place = place_of(me, size)
    right = index_at(place + 1, size)
    left = index_at(place - 1, size)
    core = lax.rem(lane, 2)
    chip = lax.div(lane, 2)
    twin = chip * 2 + 1 - core
    across = (1 - chip) * 2 + core

    loads = [
        pltpu.make_async_copy(hidden_grad_in, hidden_grad, in_sem.at[4]),
        pltpu.make_async_copy(normed_in.at[3], normed.at[3], in_sem.at[3]),
        pltpu.make_async_copy(qkv_low_in, qkv_low, in_sem.at[5]),
    ] + [
        pltpu.make_async_copy(normed_in.at[stream], normed.at[stream], in_sem.at[stream])
        for stream in range(3)
    ]
    for copy in loads:
        copy.start()

    barrier = pltpu.get_barrier_semaphore()
    steps = size.bit_length() - 1
    partners = [me + (1 << step) * (1 - 2 * lax.rem(lax.div(me, 1 << step), 2)) for step in range(steps)]
    for there in [(right, lane), (left, lane), (me, twin), (me, across)] + [(it, lane) for it in partners]:
        pl.semaphore_signal(barrier, inc=1, device_id=there, device_id_type=MESH)
    pl.semaphore_wait(barrier, 4 + steps)

    block = 64
    rows_half = tokens // 2
    blocks = rows_half // block
    load = pltpu.make_async_copy(parts_in, parts, load_sem)
    load.start()

    wide = 512 if half <= 4 else hidden_cols
    pieces = [(0, at, wide) for at in range(0, hidden_cols, wide)]
    local = qkv_low.shape[1] // 3
    pieces += [(1 + which, which * local, local) for which in range(3)]
    starts = []
    offset = 0
    for _, _, cols in pieces:
        starts.append(offset)
        offset += cols

    def flip(way, distance, some=(0, 1, 2, 3)):
        owner = index_at(place + distance, size)
        for stream in some:
            flipped[way, stream] = normed[stream, owner].T

    def term(way, piece, rows):
        which, at, cols = pieces[piece]
        stream = 3 if which == 0 else which - 1
        other = hidden_grad if which == 0 else qkv_low
        return jnp.dot(
            flipped[way, stream, rows, :], other[:, at : at + cols], preferred_element_type=F32
        )

    def send(hop, way, piece):
        cols = pl.ds(starts[piece], pieces[piece][2])
        if hop == 0:
            rows = pl.ds(pl.multiple_of(way * cut, cut), cut)
            source = far.at[rows, cols]
            target = ring.at[0, way, rows, cols]
        else:
            source = ring.at[hop - 1, way, :, cols]
            target = ring.at[hop, way, :, cols]
        return pltpu.make_async_remote_copy(
            src_ref=source,
            dst_ref=target,
            send_sem=ring_send.at[hop, way, piece],
            recv_sem=ring_recv.at[hop, way, piece],
            device_id=(right + way * (left - right), lane),
            device_id_type=MESH,
        )

    def open_ring(some):
        for piece in some:
            far_term(piece)
            for way in range(2):
                send(0, way, piece).start()

    def far_term(piece):
        cols = pl.ds(starts[piece], pieces[piece][2])

        def far_rows(rows):
            far[rows, cols] = term(0, piece, rows).astype(BF16)

        row_loop(0, shard, far_rows)

    early = len(pieces) // 2
    for copy in loads[:2]:
        copy.wait()
    flip(0, half, (3,))
    open_ring(range(early))
    load.wait()
    for at in range(blocks):
        rows = pl.ds(pl.multiple_of((1 - core) * rows_half + at * block, block), block)
        pltpu.make_async_remote_copy(
            src_ref=parts.at[:, rows, :],
            dst_ref=from_core.at[at],
            send_sem=core_send.at[at],
            recv_sem=core_recv.at[at],
            device_id=(me, twin),
            device_id_type=MESH,
        ).start()
    for copy in loads[2:]:
        copy.wait()
    flip(0, half, (0, 1, 2))
    for piece in range(early, len(pieces)):
        far_term(piece)

    def mine(at):
        return pl.ds(pl.multiple_of(core * rows_half + at * block, block), block)

    def core_copy(at):
        rows = pl.ds(pl.multiple_of((1 - core) * rows_half + at * block, block), block)
        return pltpu.make_async_remote_copy(
            src_ref=parts.at[:, rows, :],
            dst_ref=from_core.at[at],
            send_sem=core_send.at[at],
            recv_sem=core_recv.at[at],
            device_id=(me, twin),
            device_id_type=MESH,
        )

    def link_copy(at):
        return pltpu.make_async_remote_copy(
            src_ref=parts.at[:, mine(at), :],
            dst_ref=from_link.at[at],
            send_sem=link_send.at[at],
            recv_sem=link_recv.at[at],
            device_id=(me, across),
            device_id_type=MESH,
        )

    def twin_copy(at):
        return pltpu.make_async_remote_copy(
            src_ref=parts.at[:, mine(at), :],
            dst_ref=parts.at[:, mine(at), :],
            send_sem=twin_send.at[at],
            recv_sem=twin_recv.at[at],
            device_id=(me, twin),
            device_id_type=MESH,
        )

    def add_into(at, other):
        base = core * rows_half + at * block

        @pl.loop(0, block // 16)
        def _(step):
            rows = pl.ds(pl.multiple_of(base + step * 16, 16), 16)
            theirs = pl.ds(pl.multiple_of(step * 16, 16), 16)
            for stream in range(4):
                total = parts[stream, rows, :].astype(F32) + other[at, stream, theirs, :].astype(F32)
                parts[stream, rows, :] = total.astype(BF16)

    def to_link(at):
        copy = core_copy(at)
        copy.wait_send()
        pl.semaphore_signal(freed.at[at], inc=1, device_id=(me, twin), device_id_type=MESH)
        copy.wait_recv()
        add_into(at, from_core)
        link_copy(at).start()

    def to_twin(at):
        copy = link_copy(at)
        copy.wait_send()
        copy.wait_recv()
        add_into(at, from_link)
        pl.semaphore_wait(freed.at[at], 1)
        twin_copy(at).start()

    def ready(at):
        copy = twin_copy(at)
        copy.wait_send()
        copy.wait_recv()

    def grad_copy(piece):
        which, at, count = pieces[piece]
        if which == 0:
            source = grad_up.at[:, pl.ds(at, count)]
            target = grad_up_out.at[:, pl.ds(at, count)]
        else:
            source = grad_qkv.at[which - 1]
            target = (grad_query_out, grad_key_out, grad_value_out)[which - 1]
        return pltpu.make_async_copy(source, target, out_sem.at[piece])

    def unit_loads(base, slot):
        rows = pl.ds(pl.multiple_of(base, UNIT), UNIT)
        return (
            pltpu.make_async_copy(history.at[:, rows, :], state_in.at[slot], unit_sem.at[slot, 0]),
            pltpu.make_async_copy(streams.at[:, rows, :], stream_in.at[slot], unit_sem.at[slot, 1]),
            pltpu.make_async_copy(out_total.at[:, rows, :], total_in.at[slot], unit_sem.at[slot, 2]),
        )

    def unit_store(base, slot):
        rows = pl.ds(pl.multiple_of(base, UNIT), UNIT)
        return pltpu.make_async_copy(grad_out.at[slot], stream_grad.at[:, rows, :], store_sem.at[slot])

    def unit_base(at, unit):
        return lax.div(unit, 2) * rows_half + at * block + lax.rem(unit, 2) * UNIT

    gain_grad[...] = jnp.zeros_like(gain_grad)
    mix_grad[...] = jnp.zeros_like(mix_grad)
    for copy in unit_loads(0, 0):
        copy.start()

    def mix_task(at):
        @pl.loop(0, 4)
        def _(unit):
            slot = lax.rem(unit, 2)
            base = unit_base(at, unit)

            @pl.when(unit < 3)
            def _():
                for copy in unit_loads(unit_base(at, unit + 1), 1 - slot):
                    copy.start()

            if at + 1 < blocks:

                @pl.when(unit == 3)
                def _():
                    for copy in unit_loads((at + 1) * block, 0):
                        copy.start()

            for copy in unit_loads(base, slot):
                copy.wait()
            if at > 0:
                unit_store(base, slot).wait()
            else:

                @pl.when(unit >= 2)
                def _():
                    unit_store(base, slot).wait()

            @pl.loop(0, UNIT // GROUP)
            def _(step):
                mix_group(base + step * GROUP, slot, step * GROUP)

            unit_store(base, slot).start()

    def mix_group(base, slot, inner_base):
        rows = pl.ds(pl.multiple_of(base, GROUP), GROUP)
        inner = pl.ds(pl.multiple_of(inner_base, GROUP), GROUP)
        zero = jnp.zeros((GROUP, 128), F32)
        chunks = width // CHUNK

        def window(at):
            return pl.ds(at * CHUNK, CHUNK)

        def lanes(total, value):
            for at_lane in range(0, CHUNK, 128):
                total = total + value[:, at_lane : at_lane + 128]
            return total

        for stream in range(4):
            mean = stats[rows, stream : stream + 1]
            scale = stats[rows, 4 + stream : 5 + stream]
            sum_e, sum_ex = zero, zero
            for at in range(chunks):
                cols = window(at)
                unit_x = (stream_in[slot, stream, inner, cols] - mean) * scale
                upstream = parts[stream, rows, cols].astype(F32)
                e = upstream * gains[stream : stream + 1, cols]
                gain = upstream * unit_x
                gain_grad[stream, :, cols] += gain[:8] + gain[8:]
                sum_e = lanes(sum_e, e)
                sum_ex = lanes(sum_ex, e * unit_x)
            mean_e = jnp.sum(sum_e, axis=1, keepdims=True) * inverse
            mean_ex = jnp.sum(sum_ex, axis=1, keepdims=True) * inverse
            for at in range(chunks):
                cols = window(at)
                unit_x = (stream_in[slot, stream, inner, cols] - mean) * scale
                e = parts[stream, rows, cols].astype(F32) * gains[stream : stream + 1, cols]
                grad = scale * (e - mean_e - unit_x * mean_ex)
                if stream == 3:
                    first = at * CHUNK // shard
                    totals = [total_in[slot, owner, inner, :] for owner in range(first, first + CHUNK // shard)]
                    grad = grad + jnp.concatenate(totals, axis=1).astype(F32)
                held[stream, :, cols] = grad
                grad_out[slot, stream, inner, cols] = grad.astype(BF16)
        for source in range(states):
            sums = [zero] * 4
            for at in range(chunks):
                cols = window(at)
                state = state_in[slot, source, inner, cols].astype(F32)
                for stream in range(4):
                    sums[stream] = lanes(sums[stream], state * held[stream, :, cols])
            for stream in range(4):
                k = stream * states + source
                mix_grad[rows, k : k + 1] = jnp.sum(sums[stream], axis=1, keepdims=True)

    def gain_copy(step):
        return pltpu.make_async_remote_copy(
            src_ref=gain_sent.at[step],
            dst_ref=gain_got.at[step],
            send_sem=gain_send.at[step],
            recv_sem=gain_recv.at[step],
            device_id=(partners[step], lane),
            device_id_type=MESH,
        )

    def gain_step(step):
        if step == 0:
            for stream in range(4):
                gain_sent[0, stream : stream + 1, :] = jnp.sum(
                    gain_grad[stream], axis=0, keepdims=True
                )
        else:
            gain_copy(step - 1).wait_recv()
            total = gain_sent[step - 1] + gain_got[step - 1]
            if step == steps:
                gain_sum[...] = total
            else:
                gain_sent[step] = total
        if step < steps:
            gain_copy(step).start()

    tasks = []
    for at in range(blocks):
        tasks.append((0.02 + 0.03 * at, to_link, at))
        tasks.append((0.19 + 0.16 * at, to_twin, at))
        tasks.append((0.23 + 0.16 * at, ready, at))
        tasks.append((0.24 + 0.16 * at, mix_task, at))
    for step in range(steps + 1):
        tasks.append((0.87 + 0.12 * step / steps, gain_step, step))
    tasks.sort(key=lambda item: item[0])
    for hop in range(1, half + 1):
        if hop == half:
            flip(0, 0)
        else:

            @pl.loop(0, 2)
            def _(way):
                flip(way, (half - hop) * (1 - 2 * way))

        for piece in range(len(pieces)):
            passed = ((hop - 1.5 if hop > 1 else 0.0) + (piece + 1) / len(pieces) * (1 if hop > 1 else 0.5)) / (half - 0.5)
            cols = pl.ds(starts[piece], pieces[piece][2])

            @pl.loop(0, 2)
            def _(way):
                send(hop - 1, way, piece).wait_recv()

                def with_got(rows):
                    got = ring[hop - 1, way, rows, cols].astype(F32)
                    ring[hop - 1, way, rows, cols] = (term(way, piece, rows) + got).astype(BF16)

                def alone(rows):
                    ring[hop - 1, way, rows, cols] = term(way, piece, rows).astype(BF16)

                if hop == 1:
                    row_loop(way * cut, cut, with_got)
                    row_loop((1 - way) * cut, cut, alone)
                elif hop < half:
                    row_loop(0, shard, with_got)
                if hop < half:
                    send(hop, way, piece).start()

            if hop == half:

                def finish(rows):
                    total = (
                        term(0, piece, rows)
                        + ring[hop - 1, 0, rows, cols].astype(F32)
                        + ring[hop - 1, 1, rows, cols].astype(F32)
                    )
                    which, at, count = pieces[piece]
                    if which == 0:
                        grad_up[rows, at : at + count] = total.astype(BF16)
                    else:
                        grad_qkv[which - 1, rows, :] = total.astype(BF16)

                row_loop(0, shard, finish)
                grad_copy(piece).start()
            if hop == 1 and piece == early - 1:
                for late in range(early, len(pieces)):
                    for way in range(2):
                        send(0, way, late).start()
            while tasks and tasks[0][0] <= passed:
                _, run, value = tasks.pop(0)
                run(value)
    for _, run, value in tasks:
        run(value)
    for piece in range(len(pieces)):
        grad_copy(piece).wait()
    for slot in range(2):
        unit_store((blocks - 1) * block, slot).wait()
    for step in range(steps):
        gain_copy(step).wait_send()
    for hop in range(half):
        for piece in range(len(pieces)):
            for way in range(2):
                send(hop, way, piece).wait_send()


def back_stage(size, normed, hidden_grad, qkv_low, stats, mix, gains, parts, history, streams, out_total):
    half = size // 2
    tokens, hidden = hidden_grad.shape
    states, _, width = history.shape
    shard = normed.shape[3]
    local = qkv_low.shape[1] // 3
    cols = hidden + 3 * local
    count = (hidden // 512 if half <= 4 else 1) + 3
    blocks = tokens // 128
    steps = size.bit_length() - 1
    vmem = pl.BlockSpec(memory_space=pltpu.VMEM)
    hbm = pl.BlockSpec(memory_space=pl.ANY)
    dma = pltpu.SemaphoreType.DMA
    small = jax.ShapeDtypeStruct((shard, local), BF16)
    return pl.pallas_call(
        lambda *refs: back_kernel(size, *refs),
        in_specs=[vmem] * 3 + [hbm] * 7,
        out_specs=[vmem] * 2 + [hbm] * 5,
        out_shape=[
            jax.ShapeDtypeStruct((tokens, mix.shape[1]), F32),
            jax.ShapeDtypeStruct((4, width), F32),
            jax.ShapeDtypeStruct((shard, hidden), BF16),
            small,
            small,
            small,
            jax.ShapeDtypeStruct((4, tokens, width), BF16),
        ],
        scratch_shapes=[
            pltpu.VMEM(normed.shape, BF16),
            pltpu.VMEM((tokens, hidden), BF16),
            pltpu.VMEM((tokens, 3 * local), BF16),
            pltpu.VMEM((shard, hidden), BF16),
            pltpu.VMEM((3, shard, local), BF16),
            pltpu.VMEM((4, 8, width), F32),
            pltpu.VMEM((steps, 4, width), F32),
            pltpu.VMEM((steps, 4, width), F32),
            pltpu.VMEM((4, tokens, width), BF16),
            pltpu.VMEM((blocks, 4, 64, width), BF16),
            pltpu.VMEM((blocks, 4, 64, width), BF16),
            pltpu.VMEM((shard, cols), BF16),
            pltpu.VMEM((half, 2, shard, cols), BF16),
            pltpu.VMEM((2, states, UNIT, width), BF16),
            pltpu.VMEM((2, 4, UNIT, width), F32),
            pltpu.VMEM((2, size, UNIT, shard), BF16),
            pltpu.VMEM((2, 4, UNIT, width), BF16),
            pltpu.VMEM((4, GROUP, width), F32),
            pltpu.VMEM((2, 4, shard, tokens), BF16),
            dma((6,)),
            dma((count,)),
            dma((half, 2, count)),
            dma((half, 2, count)),
            dma((blocks,)),
            dma((blocks,)),
            dma((blocks,)),
            dma((blocks,)),
            dma((blocks,)),
            dma((blocks,)),
            dma(()),
            dma((2, 3)),
            dma((2,)),
            dma((steps,)),
            dma((steps,)),
            pltpu.SemaphoreType.REGULAR((blocks,)),
        ],
        cost_estimate=pl.CostEstimate(
            flops=tokens * width * 2000, bytes_accessed=tokens * width * 64, transcendentals=0
        ),
        compiler_params=pltpu.CompilerParams(
            collective_id=1, has_side_effects=True, vmem_limit_bytes=62 * MIB
        ),
        name="back_stage",
    )(stats, mix, gains, normed, hidden_grad, qkv_low, parts, history, streams, out_total)


TILE = 512


def unrotate(values, turn):
    return (
        values * turn[0]
        + pltpu.roll(values, HEAD_DIM - ROT // 2, 1) * turn[1]
        + pltpu.roll(values, ROT // 2, 1) * turn[2]
    )


def row_loop(base, count, run, step=128):
    step = min(step, count)

    @pl.loop(0, count // step)
    def _(at):
        run(pl.ds(pl.multiple_of(base + at * step, step), step))


def attention_probs(query, key, two, first):
    shape = (query.shape[0], key.shape[0])
    middle = key.shape[0] // 2
    scores = dot(query, key, ((1,), (1,))) * (HEAD_DIM ** (-0.5))
    row = first + lax.broadcasted_iota(jnp.int32, shape, 0)
    col = lax.broadcasted_iota(jnp.int32, shape, 1)
    apart = jnp.where(row >= middle, jnp.where(col < middle, two, 0), 0)
    scores = jnp.where(jnp.logical_or(apart != 0, col > row), -1e30, scores)
    weights = jnp.exp(scores - jnp.max(scores, axis=1, keepdims=True))
    return weights / jnp.sum(weights, axis=1, keepdims=True)


def mid_kernel(
    size,
    turn,
    two,
    gen_grad,
    gen_gain,
    gen_mid,
    low_t_in,
    grad_blocks_in,
    hidden_in,
    heads_in,
    low_all,
    up_full,
    qkv_full,
    gen_sum,
    mid_sum,
    grad_out,
    grad_down,
    hidden_grad_out,
    qkv_low_out,
    parts,
    low_t,
    grad_blocks,
    hidden,
    heads,
    low_sum,
    hidden_grad,
    qkv_low,
    attended_grad,
    far,
    ring,
    low_tile,
    up_tile,
    qkv_tile,
    stage,
    gen_sent,
    gen_got,
    mid_sent,
    mid_got,
    value_sum,
    key_sum,
    gen_all,
    slope_in,
    share_sem,
    in_sem,
    out_sem,
    ring_send,
    ring_recv,
    tile_sem,
    stage_sem,
    gen_send,
    gen_recv,
):
    half = size // 2
    rows_all, tokens = low_t.shape
    shard = grad_blocks.shape[2]
    local = heads.shape[1] // 3
    me = lax.axis_index("dp")
    lane = lax.axis_index("tensor")
    place = place_of(me, size)
    right = index_at(place + 1, size)
    left = index_at(place - 1, size)
    steps = size.bit_length() - 1
    partners = [me + (1 << step) * (1 - 2 * lax.rem(lax.div(me, 1 << step), 2)) for step in range(steps)]
    loads = [
        pltpu.make_async_copy(source, target, in_sem.at[at])
        for at, (source, target) in enumerate(
            ((low_t_in, low_t), (grad_blocks_in, grad_blocks), (hidden_in, hidden), (heads_in, heads))
        )
    ]
    for copy in loads:
        copy.start()
    core = lax.rem(lane, 2)
    chip = lax.div(lane, 2)
    twin = chip * 2 + 1 - core
    across = (1 - chip) * 2 + core
    barrier = pltpu.get_barrier_semaphore()
    for there in [(it, lane) for it in [right, left] + partners] + [(me, twin), (me, across)]:
        pl.semaphore_signal(barrier, inc=1, device_id=there, device_id_type=MESH)
    pl.semaphore_wait(barrier, 4 + steps)

    low_tiles = rows_all // TILE
    width_tiles = up_full.shape[0] // TILE
    order = (
        [("low", at) for at in range(low_tiles)]
        + [("up", at) for at in range(width_tiles)]
        + [("qkv", at) for at in range(width_tiles)]
    )

    def load(index):
        kind, at = order[index]
        slot = at % 2
        rows = pl.ds(at * TILE, TILE)
        if kind == "low":
            return pltpu.make_async_copy(low_all.at[:, rows, :], low_tile.at[slot], tile_sem.at[0, slot])
        if kind == "up":
            return pltpu.make_async_copy(up_full.at[rows, :], up_tile.at[slot], tile_sem.at[1, slot])
        return pltpu.make_async_copy(qkv_full.at[rows, :], qkv_tile.at[slot], tile_sem.at[2, slot])

    load(0).start()

    pieces = rows_all // TILE
    cut = TILE // 2

    def term(owner, rows):
        return jnp.dot(low_t[rows, :], grad_blocks[owner], preferred_element_type=F32)

    def send(hop, way, piece):
        if hop == 0:
            rows = pl.ds(pl.multiple_of(piece * TILE + way * cut, cut), cut)
            source = far.at[rows, :]
        else:
            rows = pl.ds(piece * TILE, TILE)
            source = ring.at[hop - 1, way, rows, :]
        return pltpu.make_async_remote_copy(
            src_ref=source,
            dst_ref=ring.at[hop, way, rows, :],
            send_sem=ring_send.at[hop, way, piece],
            recv_sem=ring_recv.at[hop, way, piece],
            device_id=(right + way * (left - right), lane),
            device_id_type=MESH,
        )

    for copy in loads[:2]:
        copy.wait()
    def far_term(piece):
        def far_rows(rows):
            far[rows, :] = term(index_at(place + half, size), rows).astype(BF16)

        row_loop(piece * TILE, TILE, far_rows)

    early = pieces // 2
    for piece in range(early):
        far_term(piece)
        for way in range(2):
            send(0, way, piece).start()
    for piece in range(early, pieces):
        far_term(piece)
    for copy in loads[2:]:
        copy.wait()

    def grad_copy(piece):
        base = piece * TILE
        source = low_sum.at[pl.ds(base, TILE), :]
        if base < local:
            target = grad_out.at[pl.ds(base, TILE), :]
        else:
            target = grad_down.at[pl.ds(base - local, TILE), :]
        return pltpu.make_async_copy(source, target, out_sem.at[2 + piece])

    def hidden_copy():
        return pltpu.make_async_copy(hidden_grad, hidden_grad_out, out_sem.at[0])

    def qkv_copy():
        return pltpu.make_async_copy(qkv_low, qkv_low_out, out_sem.at[1])

    def low_grad(at):
        index = at
        load(index + 1).start()
        load(index).wait()
        base = at * TILE

        def run(rows):
            total = None
            for owner in range(size):
                part = dot(grad_blocks[owner, rows, :], low_tile[at % 2, owner], ((1,), (1,)))
                total = part if total is None else total + part
            if base < local:
                attended_grad[rows, base : base + TILE] = total.astype(BF16)
            else:
                cols = slice(base - local, base - local + TILE)
                slope_in[: rows.size, :] = total

                @pl.loop(0, rows.size // 32)
                def _(part):
                    inner = pl.ds(pl.multiple_of(part * 32, 32), 32)
                    there = pl.ds(pl.multiple_of(rows.start + part * 32, 32), 32)
                    slope = gelu_slope(hidden[there, cols])
                    hidden_grad[there, cols] = (slope_in[inner, :] * slope).astype(BF16)

        row_loop(0, tokens, run, 256)
        if at + 1 == low_tiles:
            hidden_copy().start()

    def head_grad(head):
        cols = slice(head * HEAD_DIM, (head + 1) * HEAD_DIM)
        key_cols = slice(local + head * HEAD_DIM, local + (head + 1) * HEAD_DIM)
        value_cols = slice(2 * local + head * HEAD_DIM, 2 * local + (head + 1) * HEAD_DIM)
        scale = HEAD_DIM ** (-0.5)
        value_sum[...] = jnp.zeros_like(value_sum)
        key_sum[...] = jnp.zeros_like(key_sum)

        def run(rows):
            query, key, value = heads[rows, cols], heads[:, key_cols], heads[:, value_cols]
            upstream = attended_grad[rows, cols]
            probs = attention_probs(query, key, two[...], rows.start)
            probs_grad = dot(upstream, value, ((1,), (1,)))
            value_sum[...] += dot(probs.astype(BF16), upstream, ((0,), (0,)))
            row = jnp.sum(probs * probs_grad, axis=1, keepdims=True)
            scores_grad = (probs * (probs_grad - row)).astype(BF16)
            query_grad = dot(scores_grad, key, ((1,), (0,))) * scale
            turns = [turn[which, rows, :] for which in range(3)]
            qkv_low[rows, cols] = unrotate(query_grad, turns).astype(BF16)
            key_sum[...] += dot(scores_grad, query, ((0,), (0,)))

        row_loop(0, tokens, run)
        turns = [turn[which] for which in range(3)]
        qkv_low[:, value_cols] = value_sum[...].astype(BF16)
        qkv_low[:, key_cols] = unrotate(key_sum[...] * scale, turns).astype(BF16)
        if (head + 1) * HEAD_DIM == local:
            qkv_copy().start()

    def part_store(stream, at):
        return pltpu.make_async_copy(
            stage.at[stream], parts.at[stream, :, pl.ds(at * TILE, TILE)], stage_sem.at[stream]
        )

    def up_part(at):
        index = low_tiles + at
        load(index + 1).start()
        load(index).wait()
        if at:
            part_store(3, at - 1).wait()

        def run(rows):
            stage[3, rows, :] = dot(hidden_grad[rows, :], up_tile[at % 2], ((1,), (1,))).astype(BF16)

        row_loop(0, tokens, run, 256)
        part_store(3, at).start()

    def qkv_part(at):
        index = low_tiles + width_tiles + at
        if index + 1 < len(order):
            load(index + 1).start()
        load(index).wait()
        for stream in range(3):
            if at:
                part_store(stream, at - 1).wait()

        def run(rows):
            for stream in range(3):
                cols = slice(stream * local, (stream + 1) * local)
                stage[stream, rows, :] = dot(
                    qkv_low[rows, cols], qkv_tile[at % 2, :, cols], ((1,), (1,))
                ).astype(BF16)

        row_loop(0, tokens, run, 256)
        for stream in range(3):
            part_store(stream, at).start()

    def gen_copies(step):
        return [
            pltpu.make_async_remote_copy(
                src_ref=sent.at[step],
                dst_ref=got.at[step],
                send_sem=gen_send.at[step, which],
                recv_sem=gen_recv.at[step, which],
                device_id=(partners[step], lane),
                device_id_type=MESH,
            )
            for which, (sent, got) in enumerate(((gen_sent, gen_got), (mid_sent, mid_got)))
        ]

    quarter = gen_sent.shape[2]

    def share(which):
        if which == 0:
            cols = pl.ds(pl.multiple_of(lane * quarter, quarter), quarter)
            there = (me, twin)
        else:
            cols = pl.ds(pl.multiple_of(chip * 2 * quarter, 2 * quarter), 2 * quarter)
            there = (me, across)
        return pltpu.make_async_remote_copy(
            src_ref=gen_all.at[:, cols],
            dst_ref=gen_all.at[:, cols],
            send_sem=share_sem.at[0, which],
            recv_sem=share_sem.at[1, which],
            device_id=there,
            device_id_type=MESH,
        )

    def gen_step(step):
        cols = pl.ds(pl.multiple_of(lane * quarter, quarter), quarter)
        if step == 0:
            units = gen_grad.shape[0]
            gen_sent[0, :units, :] = gen_grad[:, cols].astype(BF16)
            gen_sent[0, units:, :] = jnp.broadcast_to(
                gen_gain[:, cols].astype(BF16), (gen_sent.shape[1] - units, quarter)
            )
            mid_sent[0] = gen_mid[...]
        elif step <= steps:
            for copy in gen_copies(step - 1):
                copy.wait_recv()
            total = gen_sent[step - 1].astype(F32) + gen_got[step - 1].astype(F32)
            mid_total = mid_sent[step - 1] + mid_got[step - 1]
            if step == steps:
                gen_all[:, cols] = total
                mid_sum[...] = mid_total
                share(0).start()
            else:
                gen_sent[step] = total.astype(BF16)
                mid_sent[step] = mid_total
        elif step == steps + 1:
            share(0).wait_recv()
            share(1).start()
        else:
            share(1).wait_recv()
            gen_sum[...] = gen_all[...]
        if step < steps:
            for copy in gen_copies(step):
                copy.start()

    tasks = [(low_grad, at) for at in range(low_tiles)]
    tasks += [(head_grad, head) for head in range(local // HEAD_DIM)]
    tasks += [(up_part, at) for at in range(width_tiles)]
    tasks += [(qkv_part, at) for at in range(width_tiles)]
    for step in range(steps + 3):
        tasks.insert(2 + 3 * step, (gen_step, step))
    count = len(tasks)
    slots = half * pieces
    slot = 0
    for hop in range(1, half + 1):
        for piece in range(pieces):

            @pl.loop(0, 2)
            def _(way):
                send(hop - 1, way, piece).wait_recv()
                owner = index_at(place + (half - hop) * (1 - 2 * way), size)

                def with_got(rows):
                    got = ring[hop - 1, way, rows, :].astype(F32)
                    ring[hop - 1, way, rows, :] = (term(owner, rows) + got).astype(BF16)

                def alone(rows):
                    ring[hop - 1, way, rows, :] = term(owner, rows).astype(BF16)

                if hop == 1:
                    row_loop(piece * TILE + way * cut, cut, with_got)
                    row_loop(piece * TILE + (1 - way) * cut, cut, alone)
                elif hop < half:
                    row_loop(piece * TILE, TILE, with_got)
                if hop < half:
                    send(hop, way, piece).start()

            if hop == half:

                def finish(rows):
                    low_sum[rows, :] = (
                        term(me, rows)
                        + ring[hop - 1, 0, rows, :].astype(F32)
                        + ring[hop - 1, 1, rows, :].astype(F32)
                    ).astype(BF16)

                row_loop(piece * TILE, TILE, finish)
                grad_copy(piece).start()
            if hop == 1 and piece == early - 1:
                for late in range(early, pieces):
                    for way in range(2):
                        send(0, way, late).start()
            slot += 1
            while tasks and (slot == slots or len(tasks) * (slots - 2) > count * max(slots - 2 - slot, 0)):
                run, value = tasks.pop(0)
                run(value)
    for stream in range(4):
        part_store(stream, width_tiles - 1).wait()
    hidden_copy().wait()
    qkv_copy().wait()
    for piece in range(pieces):
        grad_copy(piece).wait()
    for step in range(steps):
        for copy in gen_copies(step):
            copy.wait_send()
    for which in range(2):
        share(which).wait_send()
    for hop in range(half):
        for piece in range(pieces):
            for way in range(2):
                send(hop, way, piece).wait_send()


def mid_stage(
    size,
    low_t,
    grad_blocks,
    hidden,
    heads,
    turn,
    two,
    gen_grad,
    gen_gain,
    gen_mid,
    low_all,
    up_full,
    qkv_full,
):
    half = size // 2
    rows_all, tokens = low_t.shape
    shard = grad_blocks.shape[2]
    hidden_cols = hidden.shape[1]
    local = heads.shape[1] // 3
    width = up_full.shape[0]
    pieces = rows_all // TILE
    steps = size.bit_length() - 1
    units = gen_grad.shape[0]
    vmem = pl.BlockSpec(memory_space=pltpu.VMEM)
    hbm = pl.BlockSpec(memory_space=pl.ANY)
    dma = pltpu.SemaphoreType.DMA
    return pl.pallas_call(
        lambda *refs: mid_kernel(size, *refs),
        in_specs=[vmem] * 5 + [hbm] * 7,
        out_specs=[vmem] * 2 + [hbm] * 5,
        out_shape=[
            jax.ShapeDtypeStruct((units + 8, width), F32),
            jax.ShapeDtypeStruct(gen_mid.shape, F32),
            jax.ShapeDtypeStruct((local, shard), BF16),
            jax.ShapeDtypeStruct((hidden_cols, shard), BF16),
            jax.ShapeDtypeStruct((tokens, hidden_cols), BF16),
            jax.ShapeDtypeStruct((tokens, 3 * local), BF16),
            jax.ShapeDtypeStruct((4, tokens, width), BF16),
        ],
        scratch_shapes=[
            pltpu.VMEM((rows_all, tokens), BF16),
            pltpu.VMEM((size, tokens, shard), BF16),
            pltpu.VMEM((tokens, hidden_cols), F32),
            pltpu.VMEM((tokens, 3 * local), BF16),
            pltpu.VMEM((rows_all, shard), BF16),
            pltpu.VMEM((tokens, hidden_cols), BF16),
            pltpu.VMEM((tokens, 3 * local), BF16),
            pltpu.VMEM((tokens, local), BF16),
            pltpu.VMEM((rows_all, shard), BF16),
            pltpu.VMEM((half, 2, rows_all, shard), BF16),
            pltpu.VMEM((2, size, TILE, shard), BF16),
            pltpu.VMEM((2, TILE, hidden_cols), BF16),
            pltpu.VMEM((2, TILE, 3 * local), BF16),
            pltpu.VMEM((4, tokens, TILE), BF16),
            pltpu.VMEM((steps, units + 8, width // 4), BF16),
            pltpu.VMEM((steps, units + 8, width // 4), BF16),
            pltpu.VMEM((steps,) + gen_mid.shape, F32),
            pltpu.VMEM((steps,) + gen_mid.shape, F32),
            pltpu.VMEM((tokens, HEAD_DIM), F32),
            pltpu.VMEM((tokens, HEAD_DIM), F32),
            pltpu.VMEM((units + 8, width), F32),
            pltpu.VMEM((256, TILE), F32),
            dma((2, 2)),
            dma((4,)),
            dma((2 + pieces,)),
            dma((half, 2, pieces)),
            dma((half, 2, pieces)),
            dma((3, 2)),
            dma((4,)),
            dma((steps, 2)),
            dma((steps, 2)),
        ],
        cost_estimate=pl.CostEstimate(
            flops=tokens * width * 4000, bytes_accessed=tokens * width * 40, transcendentals=0
        ),
        compiler_params=pltpu.CompilerParams(
            collective_id=2, has_side_effects=True, vmem_limit_bytes=62 * MIB
        ),
        name="mid_stage",
    )(
        turn,
        two,
        gen_grad,
        gen_gain,
        gen_mid,
        low_t,
        grad_blocks,
        hidden,
        heads,
        low_all,
        up_full,
        qkv_full,
    )


def front_kernel(
    size,
    mix_in,
    gains,
    segments,
    frequency,
    history,
    w_query,
    w_key,
    w_value,
    w_up,
    w_out,
    w_down,
    stats,
    branch,
    mix,
    turn,
    two,
    heads_out,
    hidden_out,
    low_t_out,
    normed_out,
    streams,
    qkv_all,
    up_all,
    low_all,
    heads,
    hidden,
    low_t,
    normed,
    low,
    weight_tile,
    low_tile,
    state_in,
    stream_out,
    from_core,
    from_link,
    qkv_send,
    qkv_recv,
    up_send,
    up_recv,
    low_send,
    low_recv,
    own_sem,
    state_sem,
    stream_sem,
    normed_sem,
    out_sem,
    weight_sem,
    tile_sem,
    core_send,
    core_recv,
    link_send,
    link_recv,
    twin_send,
    twin_recv,
    freed,
):
    half = size // 2
    states, tokens, width = history.shape
    shard = width // size
    local = w_query.shape[1]
    hidden_cols = w_up.shape[1]
    inverse = 1.0 / width
    me = lax.axis_index("dp")
    lane = lax.axis_index("tensor")
    place = place_of(me, size)
    right = index_at(place + 1, size)
    left = index_at(place - 1, size)
    core = lax.rem(lane, 2)
    chip = lax.div(lane, 2)
    twin = chip * 2 + 1 - core
    across = (1 - chip) * 2 + core
    rows_half = tokens // 2

    barrier = pltpu.get_barrier_semaphore()
    for there in ((right, lane), (left, lane), (me, twin), (me, across)):
        pl.semaphore_signal(barrier, inc=1, device_id=there, device_id_type=MESH)
    pl.semaphore_wait(barrier, 4)

    wide = TILE
    groups = [
        [(w_query, 0, 0), (w_key, 0, local), (w_value, 0, 2 * local)],
        [(w_up, at, at) for at in range(0, hidden_cols, wide)],
        [(w_out, at, at) for at in range(0, local, wide)]
        + [(w_down, at, local + at) for at in range(0, hidden_cols, wide)],
    ]
    sems = [(qkv_send, qkv_recv), (up_send, up_recv), (low_send, low_recv)]
    cut = (shard // 2, shard // 2, wide // 2)

    def own(group, piece, lo, count):
        source, at, _ = groups[group][piece]
        if group == 2:
            return source.at[pl.ds(at + lo, count), :]
        cols = local if group == 0 else wide
        return source.at[pl.ds(lo, count), pl.ds(at, cols)]

    def held(group, piece, owner, lo, count):
        _, _, at = groups[group][piece]
        if group == 2:
            return low_all.at[owner, pl.ds(at + lo, count), :]
        rows = pl.ds(pl.multiple_of(owner * shard + lo, cut[0]), count)
        if group == 0:
            return qkv_all.at[rows, pl.ds(at, local)]
        return up_all.at[rows, pl.ds(at, wide)]

    def send(group, hop, way, piece):
        owner = index_at(place + (hop - 1) * (2 * way - 1), size)
        whole = shard if group < 2 else wide
        lo, count = (0, whole) if hop < half else (way * cut[group], cut[group])
        target = held(group, piece, owner, lo, count)
        source = own(group, piece, lo, count) if hop == 1 else target
        send_sem, recv_sem = sems[group]
        return pltpu.make_async_remote_copy(
            src_ref=source,
            dst_ref=target,
            send_sem=send_sem.at[hop - 1, way, piece],
            recv_sem=recv_sem.at[hop - 1, way, piece],
            device_id=((right, left)[way], lane),
            device_id_type=MESH,
        )

    def own_copies(group):
        whole = shard if group < 2 else wide
        return [
            pltpu.make_async_copy(
                own(group, piece, 0, whole), held(group, piece, me, 0, whole), own_sem.at[group, piece]
            )
            for piece in range(len(groups[group]))
        ]

    units = tokens // UNIT

    def state_load(unit):
        rows = pl.ds(pl.multiple_of(unit * UNIT, UNIT), UNIT)
        slot = lax.rem(unit, 2)
        return pltpu.make_async_copy(history.at[:, rows, :], state_in.at[slot], state_sem.at[slot])

    def stream_store(unit):
        rows = pl.ds(pl.multiple_of(unit * UNIT, UNIT), UNIT)
        slot = lax.rem(unit, 2)
        return pltpu.make_async_copy(stream_out.at[slot], streams.at[:, rows, :], stream_sem.at[slot])

    per_task = 4

    def tables():
        count = mix_in.shape[0]
        padded = -(-count // 8) * 8
        mix[...] = jnp.concatenate(
            [mix_in[...], jnp.zeros((padded - count, tokens), F32)], axis=0
        ).T
        two[...] = jnp.broadcast_to(segments[0:1, tokens - 1 : tokens], (1, tokens))
        row = lax.broadcasted_iota(jnp.int32, (tokens, HEAD_DIM), 0)
        lanes = lax.broadcasted_iota(jnp.int32, (tokens, HEAD_DIM), 1)
        flag = jnp.broadcast_to(segments[0:1, tokens - 1 : tokens], (tokens, HEAD_DIM))
        place_in = row - jnp.where(row >= tokens // 2, jnp.where(flag != 0, tokens // 2, 0), 0)
        angles = place_in.astype(F32) * frequency[...]
        sine = jnp.sin(angles)
        turn[0] = jnp.cos(angles)
        turn[1] = jnp.where(lanes < ROT // 2, sine, 0.0)
        turn[2] = jnp.where(lanes < ROT // 2, 0.0, -sine)

    def out_copies():
        return [
            pltpu.make_async_copy(source, target, out_sem.at[at])
            for at, (source, target) in enumerate(
                ((heads, heads_out), (hidden, hidden_out), (low_t, low_t_out))
            )
        ]

    def mix_task(task):
        @pl.loop(0, per_task)
        def _(which):
            mix_unit(task * per_task + which, task)

        if (task + 1) * per_task == units:
            normed_store().start()

    def mix_unit(unit, task):
        slot = lax.rem(unit, 2)

        @pl.when(unit + 1 < units)
        def _():
            state_load(unit + 1).start()

        state_load(unit).wait()
        if task > 0:
            stream_store(unit - 2).wait()
        else:

            @pl.when(unit >= 2)
            def _():
                stream_store(unit - 2).wait()

        @pl.loop(0, UNIT // GROUP)
        def _(step):
            rows = pl.ds(pl.multiple_of(unit * UNIT + step * GROUP, GROUP), GROUP)
            inner = pl.ds(pl.multiple_of(step * GROUP, GROUP), GROUP)
            weights = mix[rows, :]

            sums = [jnp.zeros((GROUP, 128), F32) for _ in range(4)]
            for at in range(0, width, CHUNK):
                cols = pl.ds(at, CHUNK)
                total = [None] * 4
                for source in range(states):
                    state = state_in[slot, source, inner, cols].astype(F32)
                    for stream in range(4):
                        k = stream * states + source
                        term = weights[:, k : k + 1] * state
                        total[stream] = term if source == 0 else total[stream] + term
                for stream in range(4):
                    stream_out[slot, stream, inner, cols] = total[stream]
                    for at_lane in range(0, CHUNK, 128):
                        sums[stream] = sums[stream] + total[stream][:, at_lane : at_lane + 128]
            for stream in range(4):
                mean = jnp.sum(sums[stream], axis=1, keepdims=True) * inverse
                square = jnp.zeros((GROUP, 128), F32)
                for at in range(0, width, CHUNK):
                    center = stream_out[slot, stream, inner, pl.ds(at, CHUNK)] - mean
                    center = center * center
                    for at_lane in range(0, CHUNK, 128):
                        square = square + center[:, at_lane : at_lane + 128]
                scale = lax.rsqrt(jnp.sum(square, axis=1, keepdims=True) * inverse + EPSILON)
                stats[rows, stream : stream + 1] = mean
                stats[rows, 4 + stream : 5 + stream] = scale
                for at in range(0, width, CHUNK):
                    cols = pl.ds(at, CHUNK)
                    center = stream_out[slot, stream, inner, cols] - mean
                    value = (center * scale * gains[stream : stream + 1, cols]).astype(BF16)
                    for owner in range(at // shard, (at + CHUNK) // shard):
                        base = owner * shard - at
                        normed[stream, owner, rows, :] = value[:, base : base + shard]

        stream_store(unit).start()

    def normed_store():
        return pltpu.make_async_copy(normed, normed_out, normed_sem)

    tiles = 3 + hidden_cols // wide

    def weight_load(tile):
        if tile < 3:
            source = qkv_all.at[:, pl.ds(tile * local, local)]
        else:
            source = up_all.at[:, pl.ds((tile - 3) * wide, wide)]
        return pltpu.make_async_copy(source, weight_tile.at[tile % 2], weight_sem.at[tile % 2])

    def arrived(group):
        for copy in own_copies(group):
            copy.wait()
        for piece in range(len(groups[group])):
            for way in range(2):
                send(group, half, way, piece).wait_recv()

    def tile_product(tile, stream, rows):
        total = None
        for owner in range(size):
            part = jnp.dot(
                normed[stream, owner, rows, :],
                weight_tile[tile % 2, owner * shard : (owner + 1) * shard, :],
                preferred_element_type=F32,
            )
            total = part if total is None else total + part
        return total

    def qkv_task(which):
        if which == 0:
            arrived(0)
            weight_load(0).start()
        if which < 2:
            weight_load(which + 1).start()
        weight_load(which).wait()

        def run(rows):
            product = tile_product(which, which, rows)
            for head in range(local // HEAD_DIM):
                at = head * HEAD_DIM
                part = product[:, at : at + HEAD_DIM]
                if which < 2:
                    part = (
                        part * turn[0, rows, :]
                        - pltpu.roll(part, HEAD_DIM - ROT // 2, 1) * turn[1, rows, :]
                        - pltpu.roll(part, ROT // 2, 1) * turn[2, rows, :]
                    )
                heads[rows, which * local + at : which * local + at + HEAD_DIM] = part.astype(BF16)

        row_loop(0, tokens, run, 64)

    def head_task(pair):
        @pl.loop(0, 2)
        def _(which):
            at = pl.multiple_of((2 * pair + which) * HEAD_DIM, HEAD_DIM)
            query_cols, key_cols, value_cols = (
                pl.ds(pl.multiple_of(part * local + at, HEAD_DIM), HEAD_DIM) for part in range(3)
            )

            def run(rows):
                probs = attention_probs(
                    heads[rows, query_cols], heads[:, key_cols], two[...], rows.start
                ).astype(BF16)
                attended = jnp.dot(probs, heads[:, value_cols], preferred_element_type=F32)
                low[rows, query_cols] = attended.astype(BF16)
                low_t[query_cols, rows] = attended.T.astype(BF16)

            row_loop(0, tokens, run, 128)

    def up_task(at):
        if at == 0:
            arrived(1)
            weight_load(3).start()
        if at + 1 < tiles - 3:
            weight_load(4 + at).start()
        weight_load(3 + at).wait()
        cols = slice(at * wide, (at + 1) * wide)
        low_cols = slice(local + at * wide, local + (at + 1) * wide)

        def run(rows):
            product = tile_product(3 + at, 3, rows)
            hidden[rows, cols] = product

            @pl.loop(0, rows.size // 32)
            def _(part):
                there = pl.ds(pl.multiple_of(rows.start + part * 32, 32), 32)
                low[there, low_cols] = gelu(hidden[there, cols]).astype(BF16)

            low_t[low_cols, rows] = low[rows, low_cols].T

        row_loop(0, tokens, run)
        if at + 1 == tiles - 3:
            for copy in out_copies():
                copy.start()

    distances = [0]
    for hop in range(1, half):
        distances += [-hop, hop]
    distances += [half]

    def tile_load(index):
        owner = index_at(place + distances[index], size)
        return pltpu.make_async_copy(low_all.at[owner], low_tile.at[index % 2], tile_sem.at[index % 2])

    def mine(index):
        return pl.ds(pl.multiple_of(core * rows_half, rows_half), rows_half)

    def core_copy(index):
        owner = index_at(place + distances[index], size)
        rows = pl.ds(pl.multiple_of((1 - core) * rows_half, rows_half), rows_half)
        return pltpu.make_async_remote_copy(
            src_ref=branch.at[owner, rows, :],
            dst_ref=from_core.at[index],
            send_sem=core_send.at[index],
            recv_sem=core_recv.at[index],
            device_id=(me, twin),
            device_id_type=MESH,
        )

    def link_copy(index):
        owner = index_at(place + distances[index], size)
        return pltpu.make_async_remote_copy(
            src_ref=branch.at[owner, mine(index), :],
            dst_ref=from_link.at[index],
            send_sem=link_send.at[index],
            recv_sem=link_recv.at[index],
            device_id=(me, across),
            device_id_type=MESH,
        )

    def twin_copy(index):
        owner = index_at(place + distances[index], size)
        return pltpu.make_async_remote_copy(
            src_ref=branch.at[owner, mine(index), :],
            dst_ref=branch.at[owner, mine(index), :],
            send_sem=twin_send.at[index],
            recv_sem=twin_recv.at[index],
            device_id=(me, twin),
            device_id_type=MESH,
        )

    def low_task(index):
        if index == 0:
            for copy in own_copies(2):
                copy.wait()
        owner = index_at(place + distances[index], size)
        load = tile_load(index)
        load.start()
        load.wait()

        def run(rows):
            branch[owner, rows, :] = jnp.dot(
                low[rows, :], low_tile[index % 2], preferred_element_type=F32
            ).astype(BF16)

        row_loop(0, tokens, run)
        core_copy(index).start()

    def add_into(index, other):
        owner = index_at(place + distances[index], size)
        rows = mine(index)
        branch[owner, rows, :] = (
            branch[owner, rows, :].astype(F32) + other[index].astype(F32)
        ).astype(BF16)

    def link_task(index):
        copy = core_copy(index)
        copy.wait_send()
        pl.semaphore_signal(freed.at[index], inc=1, device_id=(me, twin), device_id_type=MESH)
        copy.wait_recv()
        add_into(index, from_core)
        link_copy(index).start()

    def twin_task(index):
        copy = link_copy(index)
        copy.wait_send()
        copy.wait_recv()
        add_into(index, from_link)
        pl.semaphore_wait(freed.at[index], 1)
        twin_copy(index).start()

    state_load(0).start()
    slots = [(group, hop) for group in range(3) for hop in range(1, half + 1)]
    counts = [len(pieces) for pieces in groups]
    first = [0, counts[0] * half, (counts[0] + counts[1]) * half]
    total_slots = sum(counts) * half
    tasks = []
    mixes = units // per_task
    for task in range(mixes):
        tasks.append((counts[0] - 1 + task * (first[1] - counts[0]) / mixes, mix_task, task))
    early = first[1] + counts[1]
    for which in range(3):
        tasks.append((early + which, qkv_task, which))
    for pair in range(local // HEAD_DIM // 2):
        tasks.append((early + 3 + 2 * pair, head_task, pair))
    middle = first[2] + counts[2]
    for at in range(tiles - 3):
        tasks.append((middle + at, up_task, at))
    for index in range(len(distances) - 1):
        due = max(first[2] + counts[2] * (abs(distances[index]) + 1) - 1, middle + tiles - 3) + 0.5 * (index % 2)
        tasks.append((due, low_task, index))
        tasks.append((due + 1, link_task, index))
        tasks.append((due + 3, twin_task, index))
    tasks.sort(key=lambda item: item[0])

    at_slot = 0
    for group, hop in slots:
        if hop == 1:
            for copy in own_copies(group):
                copy.start()
        for piece in range(counts[group]):
            for way in range(2):
                if hop > 1:
                    send(group, hop - 1, way, piece).wait_recv()
                send(group, hop, way, piece).start()
            if at_slot == 0:
                tables()
            while tasks and tasks[0][0] <= at_slot and at_slot < total_slots - 1:
                _, run, value = tasks.pop(0)
                run(value)
            at_slot += 1
    for _, run, value in tasks:
        run(value)
    for piece in range(counts[2]):
        for way in range(2):
            send(2, half, way, piece).wait_recv()
    last = len(distances) - 1
    low_task(last)
    link_task(last)
    twin_task(last)
    for index in range(len(distances)):
        copy = twin_copy(index)
        copy.wait_send()
        copy.wait_recv()
    for unit in range(units - 2, units):
        stream_store(unit).wait()
    normed_store().wait()
    for copy in out_copies():
        copy.wait()
    for group, hop in slots:
        for piece in range(counts[group]):
            for way in range(2):
                send(group, hop, way, piece).wait_send()


def front_stage(size, mix, gains, segments, frequency, history, w_query, w_key, w_value, w_up, w_out, w_down):
    half = size // 2
    states, tokens, width = history.shape
    shard = width // size
    local = w_query.shape[1]
    hidden_cols = w_up.shape[1]
    rows_all = local + hidden_cols
    vmem = pl.BlockSpec(memory_space=pltpu.VMEM)
    hbm = pl.BlockSpec(memory_space=pl.ANY)
    dma = pltpu.SemaphoreType.DMA
    up_pieces = hidden_cols // TILE
    low_pieces = rows_all // TILE
    return pl.pallas_call(
        lambda *refs: front_kernel(size, *refs),
        in_specs=[vmem] * 4 + [hbm] * 7,
        out_specs=[vmem] * 5 + [hbm] * 8,
        out_shape=[
            jax.ShapeDtypeStruct((tokens, 8), F32),
            jax.ShapeDtypeStruct((size, tokens, shard), BF16),
            jax.ShapeDtypeStruct((tokens, -(-mix.shape[0] // 8) * 8), F32),
            jax.ShapeDtypeStruct((3, tokens, HEAD_DIM), F32),
            jax.ShapeDtypeStruct((1, tokens), jnp.int32),
            jax.ShapeDtypeStruct((tokens, 3 * local), BF16),
            jax.ShapeDtypeStruct((tokens, hidden_cols), F32),
            jax.ShapeDtypeStruct((rows_all, tokens), BF16),
            jax.ShapeDtypeStruct((4, size, tokens, shard), BF16),
            jax.ShapeDtypeStruct((4, tokens, width), F32),
            jax.ShapeDtypeStruct((width, 3 * local), BF16),
            jax.ShapeDtypeStruct((width, hidden_cols), BF16),
            jax.ShapeDtypeStruct((size, rows_all, shard), BF16),
        ],
        scratch_shapes=[
            pltpu.VMEM((tokens, 3 * local), BF16),
            pltpu.VMEM((tokens, hidden_cols), F32),
            pltpu.VMEM((rows_all, tokens), BF16),
            pltpu.VMEM((4, size, tokens, shard), BF16),
            pltpu.VMEM((tokens, rows_all), BF16),
            pltpu.VMEM((2, width, TILE), BF16),
            pltpu.VMEM((2, rows_all, shard), BF16),
            pltpu.VMEM((2, states, UNIT, width), BF16),
            pltpu.VMEM((2, 4, UNIT, width), F32),
            pltpu.VMEM((size, tokens // 2, shard), BF16),
            pltpu.VMEM((size, tokens // 2, shard), BF16),
            dma((half, 2, 3)),
            dma((half, 2, 3)),
            dma((half, 2, up_pieces)),
            dma((half, 2, up_pieces)),
            dma((half, 2, low_pieces)),
            dma((half, 2, low_pieces)),
            dma((3, low_pieces)),
            dma((2,)),
            dma((2,)),
            dma(()),
            dma((3,)),
            dma((2,)),
            dma((2,)),
            dma((size,)),
            dma((size,)),
            dma((size,)),
            dma((size,)),
            dma((size,)),
            dma((size,)),
            pltpu.SemaphoreType.REGULAR((size,)),
        ],
        cost_estimate=pl.CostEstimate(
            flops=tokens * width * 8000, bytes_accessed=tokens * width * 80, transcendentals=0
        ),
        compiler_params=pltpu.CompilerParams(
            collective_id=3, has_side_effects=True, vmem_limit_bytes=62 * MIB
        ),
        name="front_stage",
    )(mix, gains, segments, frequency, history, w_query, w_key, w_value, w_up, w_out, w_down)


def finish_kernel(count, mix, grads, mix_grad, gain_sum, gen_sum, mid_sum, *refs):
    sources = refs[:count]
    history_grad, mix_out, gain_out, gen_out, mid_out = refs[count : count + 5]
    targets = refs[count + 5 : 2 * count + 5]
    spread = refs[2 * count + 5]
    units = gen_out.shape[0]
    states, tokens, width = history_grad.shape
    step = pl.program_id(0)
    for source, target in zip(sources, targets):
        target[...] = source[...].astype(F32)

    @pl.when(step == 0)
    def _():
        gain_out[:4, :] = gain_sum[...]
        gain_out[4:5, :] = gen_sum[units : units + 1, :]
        gen_out[...] = gen_sum[:units, :]
        mid_out[...] = mid_sum[:, : mid_out.shape[1]]
        mix_out[...] = mix_grad[...].T[: mix_out.shape[0], :]

    own = lax.broadcasted_iota(jnp.int32, (tokens, tokens), 0) == lax.broadcasted_iota(
        jnp.int32, (tokens, tokens), 1
    )
    weights = mix[...]
    for source in range(states):
        parts = [
            jnp.where(own, weights[:, stream * states + source : stream * states + source + 1], 0.0)
            for stream in range(4)
        ]
        spread[source * tokens : (source + 1) * tokens, :] = jnp.concatenate(parts, axis=1).astype(BF16)

    @pl.loop(0, width // 512)
    def _(at):
        cols = pl.ds(pl.multiple_of(at * 512, 512), 512)
        grad = jnp.concatenate([grads[stream, :, cols] for stream in range(4)], axis=0)
        mixed = jnp.dot(spread[...], grad, preferred_element_type=F32)
        for source in range(states):
            history_grad[source, :, cols] = mixed[source * tokens : (source + 1) * tokens].astype(BF16)


def finish_stage(states, mixes, following, mix, grads, mix_grad, gain_sum, gen_sum, mid_sum, sources, block=64):
    _, tokens, width = grads.shape
    steps = tokens // block
    row = lambda i: (i, 0)
    passed = [pl.BlockSpec((source.shape[0] // steps, source.shape[1]), row) for source in sources]
    fixed = lambda i: (0, 0)
    units = gen_sum.shape[0] - 8
    return pl.pallas_call(
        lambda *refs: finish_kernel(len(sources), *refs),
        grid=(steps,),
        in_specs=[
            pl.BlockSpec((block, mix.shape[1]), lambda i: (i, 0)),
            pl.BlockSpec((4, block, width), lambda i: (0, i, 0)),
            pl.BlockSpec(mix_grad.shape, fixed),
            pl.BlockSpec(gain_sum.shape, fixed),
            pl.BlockSpec(gen_sum.shape, fixed),
            pl.BlockSpec(mid_sum.shape, fixed),
        ]
        + passed,
        out_specs=[
            pl.BlockSpec((states, block, width), lambda i: (0, i, 0)),
            pl.BlockSpec((mixes, tokens), fixed),
            pl.BlockSpec((5, width), fixed),
            pl.BlockSpec((units, width), fixed),
            pl.BlockSpec((units, following), fixed),
        ]
        + passed,
        out_shape=[
            jax.ShapeDtypeStruct((states, tokens, width), BF16),
            jax.ShapeDtypeStruct((mixes, tokens), F32),
            jax.ShapeDtypeStruct((5, width), F32),
            jax.ShapeDtypeStruct((units, width), F32),
            jax.ShapeDtypeStruct((units, following), F32),
        ]
        + [jax.ShapeDtypeStruct(source.shape, F32) for source in sources],
        scratch_shapes=[
            pltpu.VMEM((states * block, 4 * block), BF16),
        ],
        cost_estimate=pl.CostEstimate(
            flops=tokens * width * 72, bytes_accessed=tokens * width * 26, transcendentals=0
        ),
        compiler_params=pltpu.CompilerParams(vmem_limit_bytes=62 * MIB),
        name="finish_stage",
    )(mix, grads, mix_grad, gain_sum, gen_sum, mid_sum, *sources)


def body(
    sizes,
    history,
    mix_weights,
    segments,
    norm_gains,
    w_query,
    w_key,
    w_value,
    w_out,
    w_up,
    w_down,
    gen_in,
    gen_out,
    out_grad,
    next_grad,
):
    dp_size, tensor_size = sizes
    places = np.arange(HEAD_DIM)
    frequency = np.where(
        places < ROT, np.float32(ROPE_BASE) ** (-2.0 * (places % (ROT // 2)).astype(np.float32) / ROT), 0.0
    ).astype(np.float32)
    stats, branch, mix_rows, turn, two, heads, hidden, low_t, normed, streams, full_qkv, full_up, low_all = front_stage(
        dp_size,
        mix_weights,
        norm_gains,
        segments[None, :],
        jnp.asarray(frequency)[None, :],
        history,
        w_query,
        w_key,
        w_value,
        w_up,
        w_out,
        w_down,
    )
    layer_out, next_mix, branch_grad, gain_gen_grad, grad_gen_in, grad_gen_out = gen_stage(
        dp_size, streams, branch, norm_gains, gen_in.T, gen_out, out_grad, next_grad
    )

    gen_sum, mid_sum, grad_out, grad_down, hidden_grad, qkv_low, parts = mid_stage(
        dp_size,
        low_t,
        branch_grad,
        hidden,
        heads,
        turn,
        two,
        grad_gen_in,
        gain_gen_grad,
        grad_gen_out,
        low_all,
        full_up,
        full_qkv,
    )
    mix_grad, gain_sums, grad_up, grad_query, grad_key, grad_value, stream_grad = back_stage(
        dp_size,
        normed,
        hidden_grad,
        qkv_low,
        stats,
        mix_rows,
        norm_gains,
        parts,
        history,
        streams,
        branch_grad,
    )
    history_grad, mix_grad, grad_gains, grad_gen_in, grad_gen_out, grad_up, grad_query, grad_key, grad_value, grad_out, grad_down = finish_stage(
        history.shape[0],
        mix_weights.shape[0],
        gen_out.shape[1],
        mix_rows,
        stream_grad,
        mix_grad,
        gain_sums,
        gen_sum,
        mid_sum,
        (grad_up, grad_query, grad_key, grad_value, grad_out, grad_down),
    )
    return (
        layer_out,
        next_mix,
        history_grad,
        mix_grad,
        grad_gains,
        grad_query,
        grad_key,
        grad_value,
        grad_out,
        grad_up,
        grad_down,
        grad_gen_in.T,
        grad_gen_out,
    )


def solution(mesh):
    sizes = (mesh.shape["dp"], mesh.shape["tensor"])
    in_specs = (
        P(None, "dp", None),
        P(None, "dp"),
        P("dp"),
        P(),
        P("dp", "tensor"),
        P("dp", "tensor"),
        P("dp", "tensor"),
        P("tensor", "dp"),
        P("dp", "tensor"),
        P("tensor", "dp"),
        P(),
        P(),
        P("dp", None),
        P(None, "dp"),
    )
    out_specs = (
        P("dp", None),
        P(None, "dp"),
        P(None, "dp", None),
        P(None, "dp"),
        P(),
        P("dp", "tensor"),
        P("dp", "tensor"),
        P("dp", "tensor"),
        P("tensor", "dp"),
        P("dp", "tensor"),
        P("tensor", "dp"),
        P(),
        P(),
    )

    def step(*arrays):
        return body(sizes, *arrays)

    return jax.shard_map(step, mesh=mesh, in_specs=in_specs, out_specs=out_specs, check_vma=False)
```
